256 devices in a mesh: space: 64 (over z_hi, y, x, core), dp: 4 (over z_lo).
Axes of the slice: x: 4, y: 4, z: 8 (z_hi: 2, z_lo: 4; z = z_hi * 4 + z_lo), core: 2. Of those that a mesh axis runs over, the one named last changes fastest.
Arguments:
- activations: bfloat16 [4, 256, 16, 16, 128], P('dp', 'space'), may hold values from -100 to 100
- upstream: bfloat16 [4, 256, 16, 16, 128], P('dp', 'space'), may hold values from -100 to 100
- kernel_weight: bfloat16 [27, 128, 128], replicated, may hold values from -0.109375 to 0.109375
- patch_inverse: float32 [27, 128, 3456], P(None, 'space'), may hold values from -0.1 to 1.6, as said below
- output_inverse: float32 [128, 128], replicated, may hold values from -0.1 to 1.6, as said below
Outputs:
- activated: bfloat16 [4, 256, 16, 16, 128], P('dp', 'space')
- input_grad: bfloat16 [4, 256, 16, 16, 128], P('dp', 'space')
- patch_factor: float32 [128, 63, 128], P('space', None, 'dp')
- output_factor: float32 [128, 128], replicated
- precond_grad: float32 [27, 128, 128], P(None, 'space')
The draws below stay inside these ranges and needn't reach their ends.
Inputs may be any that keep to these rules, and one draw needn't show every extreme that they name: Symmetric as a 3456 x 3456 matrix whose row o * 128 + c is patch_inverse[o, c, :]. `output_inverse`: symmetric.
All inputs are finite; a program needn't handle non-finite values.
Results may differ from the reference program's by a relative error of at most 0.0015.
The reference program's roundings to bfloat16 on the way (of `slope`) count: a program that leaves them out, or rounds other values in their place, can miss the bound.
Values may be sent and summed in bfloat16 or wider, within the bound.
A program may use at most 128 MiB of HBM per device.

```python
import math
import jax
import jax.numpy as jnp
from jax import lax

C = 128
TAPS = 27
LAGS = 63
CZ = 4
NY = 16
NX = 16
PATCH = 3456
VOLS = 4
NZ = 256
CELLS_ALL = 262144


def shared_field(key):
    field_shape = (VOLS, NZ, NY, NX, C)
    noise_field = jax.random.normal(jax.random.fold_in(key, 101), field_shape, jnp.float32)
    smooth = (noise_field + 0.6 * jnp.roll(noise_field, 1, 1) + 0.4 * jnp.roll(noise_field, 1, 2) + 0.4 * jnp.roll(noise_field, 1, 3)) / math.sqrt(1.68)
    mixing = jnp.eye(C, dtype=jnp.float32) + 0.4 * jax.random.normal(jax.random.fold_in(key, 102), (C, C), jnp.float32) / math.sqrt(C)
    mixed_field = jnp.dot(smooth.reshape(-1, C), mixing).reshape(field_shape)
    chan_scale = jnp.exp(jax.random.uniform(jax.random.fold_in(key, 103), (C,), jnp.float32, math.log(0.3), math.log(3.0)))
    depth_ramp = jnp.exp(0.55 * jnp.arange(NZ, dtype=jnp.float32) / NZ)
    slab_count = NZ // CZ
    slab_owner = jax.random.permutation(jax.random.fold_in(key, 104), slab_count)
    slab_of = jnp.arange(NZ) // CZ
    block_of = jnp.arange(C) // (C // slab_count)
    spike_gain = jnp.where(slab_owner[slab_of][:, None] == block_of[None, :], 3.0, 1.0)
    return mixed_field * chan_scale * depth_ramp[None, :, None, None, None] * spike_gain[None, :, None, None, :]


def draw_activations(key, part):
    return jnp.clip(shared_field(key), -100.0, 100.0).astype(jnp.bfloat16)


def draw_upstream(key, part):
    extra = jax.random.normal(jax.random.fold_in(key, 105), (VOLS, NZ, NY, NX, C), jnp.float32)
    return jnp.clip(0.3 * shared_field(key) + extra, -100.0, 100.0).astype(jnp.bfloat16)


def symmetric_inverse(key, order):
    reach = min(0.05, 0.6 / math.sqrt(order))
    entries = jax.random.uniform(jax.random.fold_in(key, 1), (order, order), jnp.float32, -reach, reach)
    diagonal = jax.random.uniform(jax.random.fold_in(key, 2), (order,), jnp.float32, 0.5, 1.45)
    return entries + entries.T + jnp.diag(diagonal)


def draw_patch_inverse(key, part):
    return symmetric_inverse(jax.random.fold_in(key, 201), PATCH).reshape(TAPS, C, PATCH)


def draw_output_inverse(key, part):
    return symmetric_inverse(jax.random.fold_in(key, 202), C)


def scatter_about(own_key, shape, width, most, held_as=jnp.bfloat16):
    return jnp.clip(width * jax.random.normal(own_key, shape, jnp.float32), -most, most).astype(held_as)


def setup_inputs(seed: int = 0) -> dict:
    arg_keys = jax.random.split(jax.random.key(seed), 6)
    return {
        "activations": draw_activations(jax.random.fold_in(arg_keys[5], 71), 0),
        "upstream": draw_upstream(jax.random.fold_in(arg_keys[5], 71), 0),
        "kernel_weight": scatter_about(arg_keys[2], (TAPS, C, C), PATCH ** -0.5, 0.109375),
        "patch_inverse": draw_patch_inverse(jax.random.fold_in(arg_keys[5], 71), 0),
        "output_inverse": draw_output_inverse(jax.random.fold_in(arg_keys[5], 71), 0),
    }


def tap_shift(offset):
    return (offset // 9 - 1, (offset // 3) % 3 - 1, offset % 3 - 1)


def lag_shift(lag):
    number = lag + 62
    return (number // 25 - 2, (number // 5) % 5 - 2, number % 5 - 2)


def rolled(field, displacement):
    return jnp.roll(field, (-displacement[0], -displacement[1], -displacement[2]), axis=(1, 2, 3))


def reference(activations, upstream, kernel_weight, patch_inverse, output_inverse):
    pre = jnp.zeros((CELLS_ALL, C), jnp.float32)
    for offset in range(TAPS):
        moved = rolled(activations, tap_shift(offset)).reshape(-1, C)
        pre = pre + jnp.dot(moved, kernel_weight[offset], preferred_element_type=jnp.float32)
    logistic = jax.nn.sigmoid(pre)
    activated = (pre * logistic).astype(jnp.bfloat16).reshape(activations.shape)
    slope = (upstream.reshape(-1, C).astype(jnp.float32) * logistic * (1.0 + pre * (1.0 - logistic))).astype(jnp.bfloat16)
    slope_field = slope.reshape(activations.shape)
    back = jnp.zeros((CELLS_ALL, C), jnp.float32)
    grads = []
    for offset in range(TAPS):
        displacement = tap_shift(offset)
        negated = (-displacement[0], -displacement[1], -displacement[2])
        slope_moved = rolled(slope_field, negated).reshape(-1, C)
        back = back + jnp.dot(slope_moved, kernel_weight[offset].T, preferred_element_type=jnp.float32)
        moved = rolled(activations, displacement).reshape(-1, C)
        grads.append(jnp.dot(moved.T, slope, preferred_element_type=jnp.float32))
    input_grad = back.astype(jnp.bfloat16).reshape(activations.shape)
    weight_grad = jnp.stack(grads, axis=0) / CELLS_ALL
    output_factor = jnp.dot(slope.T, slope, preferred_element_type=jnp.float32) / CELLS_ALL
    flat = activations.reshape(-1, C)
    blocks = []
    for lag in range(LAGS):
        moved = rolled(activations, lag_shift(lag)).reshape(-1, C)
        blocks.append(jnp.dot(flat.T, moved, preferred_element_type=jnp.float32))
    patch_factor = jnp.stack(blocks, axis=1) / CELLS_ALL
    left = jnp.dot(patch_inverse.reshape(PATCH, PATCH), weight_grad.reshape(PATCH, C), precision=lax.Precision.HIGHEST)
    precond_grad = jnp.dot(left, output_inverse, precision=lax.Precision.HIGHEST).reshape(TAPS, C, C)
    return activated, input_grad, patch_factor, output_factor, precond_grad
```

```python
import functools

import jax
import jax.numpy as jnp
from jax import lax
from jax.experimental import pallas as pl
from jax.experimental.pallas import tpu as pltpu
from jax.sharding import PartitionSpec as P

F32 = jnp.float32
BF16 = jnp.bfloat16
TOTAL = 262144.0
NT = (((1,), (1,)), ((), ()))
HIGHEST = lax.Precision.HIGHEST


def dot(a, b):
    return jnp.dot(a, b, preferred_element_type=F32)


def tap_shift(offset):
    return (offset // 9 - 1, offset // 3 % 3 - 1, offset % 3 - 1)


def step_kernel(
    act,
    up,
    kw,
    pinv,
    oinv,
    activated,
    input_grad,
    patch_factor,
    output_factor,
    precond,
    halo_a,
    halo_s,
    slope,
    ext_a,
    ext_s,
    left,
    left12,
    slope_t,
    prod_l,
    got_lc,
    out_l1,
    got_l1,
    sum_l1,
    out_l2,
    got_l2,
    out_l3,
    got_l3,
    prod_w,
    got_wc,
    out_w1,
    got_w1,
    out_w2,
    got_w2,
    out_w3,
    got_w3,
    weights,
    inverse,
    part_p,
    got_p,
    send_sem,
    recv_sem,
):
    space = lax.axis_index("space")
    quarter = lax.axis_index("dp")
    core = lax.rem(space, 2)
    col = lax.rem(space // 2, 4)
    row = lax.rem(space // 8, 4)
    half = space // 32
    depth = half * 4 + quarter
    other = 1 - core

    def device(half, row, col, core, quarter):
        return {"space": ((half * 4 + row) * 4 + col) * 2 + core, "dp": quarter}

    sibling = device(half, row, col, other, quarter)
    following = {"space": lax.rem(space + 1, 64), "dp": quarter}
    preceding = {"space": lax.rem(space + 63, 64), "dp": quarter}
    far = {"space": lax.rem(space + 2 * core + 63, 64), "dp": quarter}

    def along_x(t):
        at = lax.rem(col + t, 4)
        return at, device(half, row, at, core, quarter)

    def along_y(t):
        at = lax.rem(row + t, 4)
        return at, device(half, at, col, core, quarter)

    def along_z(t):
        at = lax.rem(depth + t, 8)
        return at, device(at // 4, row, col, core, lax.rem(at, 4))

    def along_dp(t):
        at = lax.rem(quarter + t, 4)
        return at, device(half, row, col, core, at)

    count = [0]

    def send(src, dst, to):
        n = count[0]
        count[0] += 1
        copy = pltpu.make_async_remote_copy(
            src_ref=src,
            dst_ref=dst,
            send_sem=send_sem.at[n],
            recv_sem=recv_sem.at[n],
            device_id=to,
            device_id_type=pl.DeviceIdType.MESH,
        )
        copy.start()
        sent.append(copy)
        return copy

    sent = []

    partners = [sibling, far]
    partners += [along_x(t)[1] for t in (1, 2, 3)]
    partners += [along_y(t)[1] for t in (1, 2, 3)]
    partners += [along_z(t)[1] for t in range(1, 8)]
    barrier = pltpu.get_barrier_semaphore()
    for partner in partners:
        pl.semaphore_signal(
            barrier, inc=1, device_id=partner, device_id_type=pl.DeviceIdType.MESH
        )
    pl.semaphore_wait(barrier, len(partners))

    before = send(act.at[3], halo_a.at[0], following)
    after = send(act.at[0], halo_a.at[1], preceding)

    r = lax.broadcasted_iota(jnp.int32, (128, 128), 0)
    c = lax.broadcasted_iota(jnp.int32, (128, 128), 1)

    def picked(first, second):
        chan = (
            (r & 1)
            + 2 * ((r >> 6) & 1)
            + first * ((r >> 4) & 3)
            + second * ((r >> 2) & 3)
            + 64 * ((r >> 1) & 1)
        )
        return jnp.where(c == chan, 1.0, 0.0).astype(BF16)

    orders = (picked(4, 16), picked(16, 4))
    unit = jnp.where(c == r, 1.0, 0.0).astype(BF16)

    def turned(order, plane):
        return lax.dot_general(order, plane, NT, preferred_element_type=F32).astype(BF16)

    def place_a(plane, at):
        wide = plane.astype(F32).reshape(16, 16, 128)
        for dx in range(-2, 3):
            moved = plane
            if dx:
                moved = pltpu.roll(wide, (-dx) % 16, 1).reshape(256, 128).astype(BF16)
            ext_a[dx + 2, at, 32:288, :] = moved
            ext_a[dx + 2, at, 0:32, :] = moved[224:256]
            ext_a[dx + 2, at, 288:320, :] = moved[0:32]
        for part in range(2):
            left[part, :, at * 256 : (at + 1) * 256] = turned(orders[part], plane)

    def place_s(plane, at):
        wide = plane.astype(F32).reshape(16, 16, 128)
        for dx in range(-1, 2):
            moved = plane
            if dx:
                moved = pltpu.roll(wide, (-dx) % 16, 1).reshape(256, 128).astype(BF16)
            ext_s[dx + 1, at, 16:272, :] = moved
            ext_s[dx + 1, at, 0:16, :] = moved[240:256]
            ext_s[dx + 1, at, 272:288, :] = moved[0:16]

    def rows_a(first, dy, dx):
        return ext_a[dx + 2, first : first + 4, (2 + dy) * 16 : (2 + dy) * 16 + 256, :].reshape(
            1024, 128
        )

    for z in range(4):
        place_a(act[z], z + 1)

    prod_l[1, 31] = jnp.zeros((128, 128), F32)
    prod_w[3, 6] = jnp.zeros((128, 128), F32)
    inverse[:, 3456:3584] = jnp.zeros((56, 128), F32)
    inverse[48:56, :] = jnp.zeros((8, 3584), F32)
    for o in range(27):
        inverse[2 * o : 2 * o + 2, 0:3456] = pinv[o]

    for k in range(13):
        m = k + 62
        part, slot = (0, 25 + k) if k < 7 else (1, 18 + k)
        prod_l[part, slot] = dot(
            left[part, :, 256:1280], rows_a(1, m // 5 % 5 - 2, m % 5 - 2)
        )

    before.wait_recv()
    after.wait_recv()
    place_a(halo_a[0], 0)
    place_a(halo_a[1], 5)
    left12[0:128, :] = left[0, :, 256:1280]
    left12[128:256, :] = left[1, :, 0:1024]

    kernel_rows = kw[...].reshape(27 * 128, 128)
    for z in (0, 3, 1, 2):
        taps = []
        for o in range(27):
            dz, dy, dx = tap_shift(o)
            taps.append(ext_a[dx + 2, z + 1 + dz, (2 + dy) * 16 : (2 + dy) * 16 + 256, :])
        pre = dot(jnp.concatenate(taps, axis=1), kernel_rows)
        logistic = jax.nn.sigmoid(pre)
        activated[z] = (pre * logistic).astype(BF16)
        sloped = (up[z].astype(F32) * logistic * (1.0 + pre * (1.0 - logistic))).astype(BF16)
        slope[z] = sloped
        slope_t[:, z * 256 : (z + 1) * 256] = turned(unit, sloped)
        if z == 3:
            before_s = send(slope.at[3], halo_s.at[0], following)
            after_s = send(slope.at[0], halo_s.at[1], preceding)

    for o in range(27):
        dz, dy, dx = tap_shift(o)
        prod_w[o // 7, o % 7] = dot(slope_t[...], rows_a(1 + dz, dy, dx))
    own = dot(slope_t[...], slope[...].reshape(1024, 128))
    for d in range(4):
        prod_w[d, 7] = own

    theirs = pl.ds(pl.multiple_of(other * 64, 64), 64)
    mine = pl.ds(pl.multiple_of(core * 64, 64), 64)
    wc = send(prod_w.at[:, :, theirs, :], got_wc, sibling)

    pairs = [(dy, dx) for dy in range(-2, 3) for dx in range(-2, 3)]

    def lag_block(first, last):
        for s in range(first, last):
            both = dot(left12[...], rows_a(2, *pairs[s]))
            prod_l[0, s] = both[0:128]
            prod_l[1, s] = both[128:256]

    lag_block(0, 12)

    wc.wait_recv()
    out_w1[...] = (prod_w[:, :, mine, :] + got_wc[...]).astype(out_w1.dtype)
    firsts = (col, row)
    first_axis = (along_x, along_y)
    second_axis = (along_y, along_x)
    seconds = (row, col)

    w1 = []
    for part in range(2):
        for t in range(1, 4):
            at, to = first_axis[part](t)
            w1.append(
                send(
                    out_w1.at[:, 4 * part : 4 * part + 4, pl.ds(pl.multiple_of(at * 16, 16), 16), :],
                    got_w1.at[part, t - 1],
                    to,
                )
            )

    lag_block(12, 25)
    lc = send(prod_l.at[:, :, theirs, :], got_lc, sibling)

    before_s.wait_recv()
    after_s.wait_recv()
    for z in range(4):
        place_s(slope[z], z + 1)
    place_s(halo_s[0], 0)
    place_s(halo_s[1], 5)

    for copy in w1:
        copy.wait_recv()
    w2 = []
    for part in range(2):
        kept = pl.ds(pl.multiple_of(firsts[part] * 16, 16), 16)
        tall = pl.ds(pl.multiple_of(core * 64 + firsts[part] * 16, 16), 16)
        for b in range(4):
            out_w2[part, b] = (
                prod_w[:, 4 * part + b, tall, :]
                + got_wc[:, 4 * part + b, kept, :]
                + got_w1[part, 0, :, b].astype(F32)
                + got_w1[part, 1, :, b].astype(F32)
                + got_w1[part, 2, :, b].astype(F32)
            )
        for t in range(1, 4):
            at, to = second_axis[part](t)
            w2.append(send(out_w2.at[part, at], got_w2.at[part, t - 1], to))

    kernel_cols = jnp.concatenate([kw[o] for o in range(27)], axis=1)

    def back(z):
        taps = []
        for o in range(27):
            dz, dy, dx = tap_shift(o)
            taps.append(ext_s[1 - dx, z + 1 - dz, (1 - dy) * 16 : (1 - dy) * 16 + 256, :])
        grad = lax.dot_general(
            jnp.concatenate(taps, axis=1), kernel_cols, NT, preferred_element_type=F32
        )
        input_grad[z] = grad.astype(BF16)

    back(0)

    lc.wait_recv()
    for part in range(2):
        out_l1[part] = (prod_l[part, :, mine, :] + got_lc[part]).astype(BF16)
    l1 = []
    for part in range(2):
        for t in range(1, 4):
            at, to = first_axis[part](t)
            l1.append(
                send(
                    out_l1.at[part, :, pl.ds(pl.multiple_of(at * 16, 16), 16), :],
                    got_l1.at[part, t - 1],
                    to,
                )
            )

    for copy in w2:
        copy.wait_recv()
    for part in range(2):
        total = out_w2[part, seconds[part]]
        for t in range(3):
            total = total + got_w2[part, t]
        for d in range(4):
            out_w3[d, part] = total[d]
    got_w3[depth] = out_w3[quarter]
    w3 = []
    for t in range(1, 8):
        at, to = along_z(t)
        w3.append(send(out_w3.at[lax.rem(at, 4)], got_w3.at[depth], to))

    back(1)

    for copy in w3:
        copy.wait_recv()
    reduced = got_w3[0]
    for z in range(1, 8):
        reduced = reduced + got_w3[z]
    rows0 = pl.ds(pl.multiple_of(core * 64 + col * 16, 16), 16)
    rows1 = pl.ds(pl.multiple_of(core * 64 + row * 16, 16), 16)
    weights[row, rows0, :] = reduced[0]
    weights[4 + col, rows1, :] = reduced[1]
    g1 = []
    for t in range(1, 4):
        g1.append(send(weights.at[row, rows0, :], weights.at[row, rows0, :], along_y(t)[1]))
        g1.append(send(weights.at[4 + col, rows1, :], weights.at[4 + col, rows1, :], along_x(t)[1]))

    back(2)

    for copy in g1:
        copy.wait_recv()
    g2 = []
    for t in range(1, 4):
        g2.append(send(weights.at[0:4, rows0, :], weights.at[0:4, rows0, :], along_x(t)[1]))
        g2.append(send(weights.at[4:8, rows1, :], weights.at[4:8, rows1, :], along_y(t)[1]))

    back(3)

    for copy in l1:
        copy.wait_recv()
    l2 = []
    for part in range(2):
        kept = pl.ds(pl.multiple_of(firsts[part] * 16, 16), 16)
        tall = pl.ds(pl.multiple_of(core * 64 + firsts[part] * 16, 16), 16)
        total = prod_l[part, :, tall, :] + got_lc[part, :, kept, :]
        for t in range(3):
            total = total + got_l1[part, t].astype(F32)
        sum_l1[part] = total.reshape(512, 128)
        for b in range(4):
            for n in range(4):
                for g in range(4):
                    out_l2[part, b, n, 8 * g : 8 * g + 8, :] = sum_l1[
                        part, pl.ds(4 * b + n + 128 * g, 8, stride=16), :
                    ]
        for t in range(1, 4):
            at, to = second_axis[part](t)
            l2.append(send(out_l2.at[part, at], got_l2.at[part, t - 1], to))

    for copy in g2:
        copy.wait_recv()
    g3 = send(weights.at[:, mine, :], weights.at[:, mine, :], sibling)

    for copy in l2:
        copy.wait_recv()
    lane = lax.broadcasted_iota(jnp.int32, (32, 128), 1) // 32
    totals = []
    for part in range(2):
        total = out_l2[part, seconds[part]]
        for t in range(3):
            total = total + got_l2[part, t]
        totals.append(total)
    for h in range(2):
        groups = [totals[part][2 * h + i] for part in range(2) for i in range(2)]
        for q in range(4):
            packed = jnp.zeros((32, 128), F32)
            for j in range(4):
                shift = (32 * (j - q)) % 128
                piece = pltpu.roll(groups[j], shift, 1) if shift else groups[j]
                packed = jnp.where(lane == j, piece, packed)
            out_l3[4 * h + q] = packed
    l3 = []
    for t in range(1, 8):
        at, to = along_z(t)
        l3.append(send(out_l3.at[at], got_l3.at[t - 1], to))

    g3.wait_recv()
    cut = pl.ds(pl.multiple_of(quarter * 896, 128), 896)
    gathered = jnp.concatenate([weights[b] for b in range(7)], axis=1)
    part_p[...] = lax.dot_general(
        inverse[:, cut], gathered, NT, preferred_element_type=F32, precision=HIGHEST
    )
    got_p[quarter] = part_p[...]
    pp = []
    for t in range(1, 4):
        pp.append(send(part_p, got_p.at[quarter], along_dp(t)[1]))
    output_factor[...] = weights[7] * (1.0 / TOTAL)

    for copy in l3:
        copy.wait_recv()
    final = out_l3[depth]
    for t in range(7):
        final = final + got_l3[t]
    final = final * (1.0 / TOTAL)
    for i in range(2):
        for part in range(2):
            j = 2 * part + i
            piece = (pltpu.roll(final, (-32 * j) % 128, 1) if j else final)[:, 0:32]
            if part == 0:
                patch_factor[i, 13:38, :] = piece[0:25]
                patch_factor[i, 0:7, :] = piece[25:32]
            else:
                patch_factor[i, 38:63, :] = piece[0:25]
                patch_factor[i, 7:13, :] = piece[25:31]

    for copy in pp:
        copy.wait_recv()
    product = got_p[0] + got_p[1] + got_p[2] + got_p[3]
    product = jnp.dot(
        product, oinv[...], preferred_element_type=F32, precision=HIGHEST
    ) * (1.0 / TOTAL)
    for o in range(27):
        precond[o] = product[2 * o : 2 * o + 2]

    for copy in sent:
        copy.wait_send()


def per_device(activations, upstream, kernel_weight, patch_inverse, output_inverse):
    vmem = pl.BlockSpec(memory_space=pltpu.VMEM)
    scratch = [
        ((2, 256, 128), BF16),
        ((2, 256, 128), BF16),
        ((4, 256, 128), BF16),
        ((5, 6, 320, 128), BF16),
        ((3, 6, 288, 128), BF16),
        ((2, 128, 1536), BF16),
        ((256, 1024), BF16),
        ((128, 1024), BF16),
        ((2, 32, 128, 128), F32),
        ((2, 32, 64, 128), F32),
        ((2, 32, 64, 128), BF16),
        ((2, 3, 32, 16, 128), BF16),
        ((2, 512, 128), F32),
        ((2, 4, 4, 32, 128), F32),
        ((2, 3, 4, 32, 128), F32),
        ((8, 32, 128), F32),
        ((7, 32, 128), F32),
        ((4, 8, 128, 128), F32),
        ((4, 8, 64, 128), F32),
        ((4, 8, 64, 128), F32),
        ((2, 3, 4, 4, 16, 128), F32),
        ((2, 4, 4, 16, 128), F32),
        ((2, 3, 4, 16, 128), F32),
        ((4, 2, 16, 128), F32),
        ((8, 2, 16, 128), F32),
        ((8, 128, 128), F32),
        ((56, 3584), F32),
        ((56, 128), F32),
        ((4, 56, 128), F32),
    ]
    outs = pl.pallas_call(
        step_kernel,
        out_shape=(
            jax.ShapeDtypeStruct((4, 256, 128), BF16),
            jax.ShapeDtypeStruct((4, 256, 128), BF16),
            jax.ShapeDtypeStruct((2, 63, 32), F32),
            jax.ShapeDtypeStruct((128, 128), F32),
            jax.ShapeDtypeStruct((27, 2, 128), F32),
        ),
        in_specs=[vmem] * 5,
        out_specs=[vmem] * 5,
        scratch_shapes=[pltpu.VMEM(shape, dtype) for shape, dtype in scratch]
        + [pltpu.SemaphoreType.DMA((72,)), pltpu.SemaphoreType.DMA((72,))],
        compiler_params=pltpu.CompilerParams(
            collective_id=0, has_side_effects=True, vmem_limit_bytes=56 * 1024 * 1024
        ),
        name="step_kernel",
    )(
        activations.reshape(4, 256, 128),
        upstream.reshape(4, 256, 128),
        kernel_weight,
        patch_inverse,
        output_inverse,
    )
    activated, input_grad, patch_factor, output_factor, precond = outs
    return (
        activated.reshape(activations.shape),
        input_grad.reshape(activations.shape),
        patch_factor,
        output_factor,
        precond,
    )


def solution(mesh):
    return jax.shard_map(
        per_device,
        mesh=mesh,
        in_specs=(
            P("dp", "space", None, None, None),
            P("dp", "space", None, None, None),
            P(),
            P(None, "space", None),
            P(),
        ),
        out_specs=(
            P("dp", "space", None, None, None),
            P("dp", "space", None, None, None),
            P("space", None, "dp"),
            P(),
            P(None, "space", None),
        ),
        check_vma=False,
    )
```

```python
import functools

import jax
import jax.numpy as jnp
from jax import lax
from jax.experimental import pallas as pl
from jax.experimental.pallas import tpu as pltpu
from jax.sharding import PartitionSpec as P

F32 = jnp.float32
BF16 = jnp.bfloat16
TOTAL = 262144.0
NT = (((1,), (1,)), ((), ()))
HIGHEST = lax.Precision.HIGHEST


def dot(a, b):
    return jnp.dot(a, b, preferred_element_type=F32)


def tap_shift(offset):
    return (offset // 9 - 1, offset // 3 % 3 - 1, offset % 3 - 1)


def step_kernel(
    act_hbm,
    up_hbm,
    kw_hbm,
    pinv_hbm,
    oinv_hbm,
    activated_hbm,
    input_grad_hbm,
    patch_factor,
    output_factor,
    precond,
    act,
    up,
    kw,
    pinv,
    oinv,
    activated,
    input_grad,
    halo_a,
    halo_s,
    slope,
    ext_a,
    ext_s,
    left,
    left12,
    slope_t,
    prod_l,
    got_lc,
    out_l1,
    got_l1,
    sum_l1,
    out_l2,
    got_l2,
    out_l3,
    got_l3,
    prod_w,
    got_wc,
    out_w1,
    got_w1,
    out_w3,
    got_w3,
    weights,
    inverse,
    part_p,
    got_p,
    local_sem,
    send_sem,
    recv_sem,
):
    space = lax.axis_index("space")
    quarter = lax.axis_index("dp")
    core = lax.rem(space, 2)
    col = lax.rem(space // 2, 4)
    row = lax.rem(space // 8, 4)
    half = space // 32
    depth = half * 4 + quarter
    other = 1 - core

    def device(half, row, col, core, quarter):
        return {"space": ((half * 4 + row) * 4 + col) * 2 + core, "dp": quarter}

    sibling = device(half, row, col, other, quarter)
    following = {"space": lax.rem(space + 1, 64), "dp": quarter}
    preceding = {"space": lax.rem(space + 63, 64), "dp": quarter}
    far = {"space": lax.rem(space + 2 * core + 63, 64), "dp": quarter}

    def along_x(t):
        at = lax.rem(col + t, 4)
        return at, device(half, row, at, core, quarter)

    def along_y(t):
        at = lax.rem(row + t, 4)
        return at, device(half, at, col, core, quarter)

    def in_plane(t):
        at_y = lax.rem(row + t // 4, 4)
        at_x = lax.rem(col + t % 4, 4)
        return at_y, at_x, device(half, at_y, at_x, core, quarter)

    def along_z(t):
        at = lax.rem(depth + t, 8)
        return at, device(at // 4, row, col, core, lax.rem(at, 4))

    def along_dp(t):
        at = lax.rem(quarter + t, 4)
        return at, device(half, row, col, core, at)

    def sixteen(at):
        return pl.ds(pl.multiple_of(at * 16, 16), 16)

    count = [0, 0]
    sent = []
    moved_out = []

    def send(src, dst, to):
        n = count[0]
        count[0] += 1
        copy = pltpu.make_async_remote_copy(
            src_ref=src,
            dst_ref=dst,
            send_sem=send_sem.at[n],
            recv_sem=recv_sem.at[n],
            device_id=to,
            device_id_type=pl.DeviceIdType.MESH,
        )
        copy.start()
        sent.append(copy)
        return copy

    def move(src, dst):
        n = count[1]
        count[1] += 1
        copy = pltpu.make_async_copy(src, dst, local_sem.at[n])
        copy.start()
        return copy

    partners = [sibling, far]
    partners += [in_plane(t)[2] for t in range(1, 16)]
    partners += [along_z(t)[1] for t in range(1, 8)]
    barrier = pltpu.get_barrier_semaphore()
    for partner in partners:
        pl.semaphore_signal(
            barrier, inc=1, device_id=partner, device_id_type=pl.DeviceIdType.MESH
        )

    act_in = move(act_hbm, act)
    kw_in = move(kw_hbm, kw)
    up_in = move(up_hbm, up)
    pinv_in = move(pinv_hbm, pinv)
    oinv_in = move(oinv_hbm, oinv)

    r = lax.broadcasted_iota(jnp.int32, (128, 128), 0)
    c = lax.broadcasted_iota(jnp.int32, (128, 128), 1)

    def picked(first, second):
        chan = (
            (r & 1)
            + 2 * ((r >> 6) & 1)
            + first * ((r >> 4) & 3)
            + second * ((r >> 2) & 3)
            + 64 * ((r >> 1) & 1)
        )
        return jnp.where(c == chan, 1.0, 0.0).astype(BF16)

    orders = (picked(4, 16), picked(16, 4))
    unit = jnp.where(c == r, 1.0, 0.0).astype(BF16)

    def turned(order, plane):
        return lax.dot_general(order, plane, NT, preferred_element_type=F32).astype(BF16)

    def place_a(plane, at):
        wide = plane.astype(F32).reshape(16, 16, 128)
        for dx in range(-2, 3):
            moved = plane
            if dx:
                moved = pltpu.roll(wide, (-dx) % 16, 1).reshape(256, 128).astype(BF16)
            ext_a[dx + 2, at, 32:288, :] = moved
            ext_a[dx + 2, at, 0:32, :] = moved[224:256]
            ext_a[dx + 2, at, 288:320, :] = moved[0:32]
        for part in range(2):
            left[part, :, at * 256 : (at + 1) * 256] = turned(orders[part], plane)

    def place_s(plane, at):
        wide = plane.astype(F32).reshape(16, 16, 128)
        for dx in range(-1, 2):
            moved = plane
            if dx:
                moved = pltpu.roll(wide, (-dx) % 16, 1).reshape(256, 128).astype(BF16)
            ext_s[dx + 1, at, 16:272, :] = moved
            ext_s[dx + 1, at, 0:16, :] = moved[240:256]
            ext_s[dx + 1, at, 272:288, :] = moved[0:16]

    def rows_a(first, dy, dx, planes=4):
        return ext_a[
            dx + 2, first : first + planes, (2 + dy) * 16 : (2 + dy) * 16 + 256, :
        ].reshape(planes * 256, 128)

    def ends_a(dz, dy, dx):
        return jnp.concatenate([rows_a(1 + dz, dy, dx, 1), rows_a(4 + dz, dy, dx, 1)], axis=0)

    prod_l[1, 31] = jnp.zeros((128, 128), F32)
    prod_w[3, 1, 2] = jnp.zeros((128, 128), F32)
    inverse[:, 3456:3584] = jnp.zeros((56, 128), F32)
    inverse[48:56, :] = jnp.zeros((8, 3584), F32)

    act_in.wait()
    for z in range(4):
        place_a(act[z], z + 1)
    for k in range(13):
        m = k + 62
        part, slot = (0, 25 + k) if k < 7 else (1, 18 + k)
        prod_l[part, slot] = dot(
            left[part, :, 256:1280], rows_a(1, m // 5 % 5 - 2, m % 5 - 2)
        )

    kw_in.wait()
    up_in.wait()

    def forward(z):
        taps = []
        for o in range(27):
            dz, dy, dx = tap_shift(o)
            taps.append(ext_a[dx + 2, z + 1 + dz, (2 + dy) * 16 : (2 + dy) * 16 + 256, :])
        pre = dot(jnp.concatenate(taps, axis=1), kw[...].reshape(27 * 128, 128))
        logistic = jax.nn.sigmoid(pre)
        activated[z] = (pre * logistic).astype(BF16)
        sloped = (up[z].astype(F32) * logistic * (1.0 + pre * (1.0 - logistic))).astype(BF16)
        slope[z] = sloped
        slope_t[:, z * 256 : (z + 1) * 256] = turned(unit, sloped)

    forward(1)
    forward(2)

    pl.semaphore_wait(barrier, len(partners))
    before = send(act.at[3], halo_a.at[0], following)
    after = send(act.at[0], halo_a.at[1], preceding)

    theirs = pl.ds(pl.multiple_of(other * 64, 64), 64)
    mine = pl.ds(pl.multiple_of(core * 64, 64), 64)
    firsts = (col, row)
    seconds = (row, col)
    first_axis = (along_x, along_y)
    second_axis = (along_y, along_x)

    def swap_l(first, last):
        return send(
            prod_l.at[:, first:last, theirs, :], got_lc.at[:, first:last], sibling
        )

    def spread_l(first, last):
        copies = []
        for part in range(2):
            out_l1[part, first:last] = (
                prod_l[part, first:last, mine, :] + got_lc[part, first:last]
            ).astype(BF16)
            for t in range(1, 4):
                at, to = first_axis[part](t)
                copies.append(
                    send(
                        out_l1.at[part, first:last, sixteen(at), :],
                        got_l1.at[part, t - 1, first:last],
                        to,
                    )
                )
        return copies

    early_c = swap_l(25, 32)

    def blocks(d):
        for b in range(7):
            if 7 * d + b < 27:
                yield b, tap_shift(7 * d + b)

    inner_t = slope_t[:, 256:768]
    for d in range(4):
        for b, (dz, dy, dx) in blocks(d):
            prod_w[d, b // 4, b % 4] = dot(inner_t, rows_a(2 + dz, dy, dx, 2))
    inner_own = dot(inner_t, slope[1:3].reshape(512, 128))

    early_c.wait_recv()
    l1 = spread_l(25, 32)

    pinv_in.wait()
    for o in range(27):
        inverse[2 * o : 2 * o + 2, 0:3456] = pinv[o]

    before.wait_recv()
    place_a(halo_a[0], 0)
    after.wait_recv()
    place_a(halo_a[1], 5)
    forward(3)
    forward(0)
    before_s = send(slope.at[3], halo_s.at[0], following)
    after_s = send(slope.at[0], halo_s.at[1], preceding)
    activated_out = move(activated, activated_hbm)

    outer_t = jnp.concatenate([slope_t[:, 0:256], slope_t[:, 768:1024]], axis=1)
    own = inner_own + dot(outer_t, jnp.concatenate([slope[0], slope[3]], axis=0))
    wc = []
    for d in range(4):
        prod_w[d, 1, 3] = own
        for b, (dz, dy, dx) in blocks(d):
            prod_w[d, b // 4, b % 4] += dot(outer_t, ends_a(dz, dy, dx))
        wc.append(send(prod_w.at[d, :, :, theirs, :], got_wc.at[d], sibling))

    left12[0:128, :] = left[0, :, 256:1280]
    left12[128:256, :] = left[1, :, 0:1024]
    pairs = [(dy, dx) for dy in range(-2, 3) for dx in range(-2, 3)]

    def lag_block(first, last):
        for s in range(first, last):
            both = dot(left12[...], rows_a(2, *pairs[s]))
            prod_l[0, s] = both[0:128]
            prod_l[1, s] = both[128:256]
        return swap_l(first, last)

    lc = [lag_block(0, 12)]

    for copy in wc:
        copy.wait_recv()
    out_w1[...] = (prod_w[:, :, :, mine, :] + got_wc[...]).astype(BF16)
    w1 = []
    for t in range(1, 16):
        at_y, at_x, to = in_plane(t)
        w1.append(send(out_w1.at[:, :, at_y, sixteen(at_x), :], got_w1.at[t - 1], to))

    lc.append(lag_block(12, 25))
    for copy in lc:
        copy.wait_recv()
    l1 += spread_l(0, 25)

    for z in range(4):
        place_s(slope[z], z + 1)
    before_s.wait_recv()
    after_s.wait_recv()
    place_s(halo_s[0], 0)
    place_s(halo_s[1], 5)

    kernel_cols = jnp.concatenate([kw[o] for o in range(27)], axis=1)

    def back(z):
        taps = []
        for o in range(27):
            dz, dy, dx = tap_shift(o)
            taps.append(ext_s[1 - dx, z + 1 - dz, (1 - dy) * 16 : (1 - dy) * 16 + 256, :])
        grad = lax.dot_general(
            jnp.concatenate(taps, axis=1), kernel_cols, NT, preferred_element_type=F32
        )
        input_grad[z] = grad.astype(BF16)

    back(0)

    for copy in w1:
        copy.wait_recv()
    tall = sixteen(core * 4 + col)
    total_w = prod_w[:, :, row, tall, :] + got_wc[:, :, row, sixteen(col), :]
    for t in range(15):
        total_w = total_w + got_w1[t].astype(F32)
    out_w3[...] = total_w
    got_w3[depth] = out_w3[quarter]
    w3 = []
    for t in range(1, 8):
        at, to = along_z(t)
        w3.append(send(out_w3.at[lax.rem(at, 4)], got_w3.at[depth], to))

    back(1)

    for copy in l1:
        copy.wait_recv()
    l2 = []
    for part in range(2):
        kept = sixteen(firsts[part])
        high = sixteen(core * 4 + firsts[part])
        total = prod_l[part, :, high, :] + got_lc[part, :, kept, :]
        for t in range(3):
            total = total + got_l1[part, t].astype(F32)
        sum_l1[part] = total.reshape(512, 128)
        for b in range(4):
            for n in range(4):
                for g in range(4):
                    out_l2[part, b, n, 8 * g : 8 * g + 8, :] = sum_l1[
                        part, pl.ds(4 * b + n + 128 * g, 8, stride=16), :
                    ]
        for t in range(1, 4):
            at, to = second_axis[part](t)
            l2.append(send(out_l2.at[part, at], got_l2.at[part, t - 1], to))

    back(2)

    for copy in w3:
        copy.wait_recv()
    reduced = got_w3[0]
    for z in range(1, 8):
        reduced = reduced + got_w3[z]
    weights[:, row, tall, :] = reduced
    g1 = []
    for t in range(1, 16):
        piece = weights.at[:, row, tall, :]
        g1.append(send(piece, piece, in_plane(t)[2]))

    back(3)
    input_grad_out = move(input_grad, input_grad_hbm)

    for copy in l2:
        copy.wait_recv()
    group = c[0:32] // 32
    totals = []
    for part in range(2):
        total = out_l2[part, seconds[part]]
        for t in range(3):
            total = total + got_l2[part, t]
        totals.append(total)
    for h in range(2):
        groups = [totals[part][2 * h + i] for part in range(2) for i in range(2)]
        for q in range(4):
            packed = jnp.zeros((32, 128), F32)
            for j in range(4):
                shift = (32 * (j - q)) % 128
                piece = pltpu.roll(groups[j], shift, 1) if shift else groups[j]
                packed = jnp.where(group == j, piece, packed)
            out_l3[4 * h + q] = packed
    l3 = []
    for t in range(1, 8):
        at, to = along_z(t)
        l3.append(send(out_l3.at[at], got_l3.at[t - 1], to))

    for copy in g1:
        copy.wait_recv()
    g3 = send(weights.at[:, :, mine, :], weights.at[:, :, mine, :], sibling)
    g3.wait_recv()
    cut = pl.ds(pl.multiple_of(quarter * 896, 128), 896)
    gathered = jnp.concatenate([weights[b // 4, b % 4] for b in range(7)], axis=1)
    part_p[...] = lax.dot_general(
        inverse[:, cut], gathered, NT, preferred_element_type=F32, precision=HIGHEST
    )
    got_p[quarter] = part_p[...]
    pp = []
    for t in range(1, 4):
        pp.append(send(part_p, got_p.at[quarter], along_dp(t)[1]))
    output_factor[...] = weights[1, 3] * (1.0 / TOTAL)

    for copy in l3:
        copy.wait_recv()
    final = out_l3[depth]
    for t in range(7):
        final = final + got_l3[t]
    final = final * (1.0 / TOTAL)
    flipped = jnp.concatenate([final, jnp.zeros((96, 128), F32)], axis=0).T
    lane = c[0:32]
    for i in range(2):
        one = flipped[32 * i : 32 * i + 32]
        two = flipped[64 + 32 * i : 96 + 32 * i]
        piece = jnp.where(lane < 7, pltpu.roll(one, 103, 1), pltpu.roll(two, 110, 1))
        piece = jnp.where(lane < 13, piece, pltpu.roll(one, 13, 1))
        piece = jnp.where(lane < 38, piece, pltpu.roll(two, 38, 1))
        patch_factor[i] = piece[:, 0:63]

    oinv_in.wait()
    for copy in pp:
        copy.wait_recv()
    product = got_p[0] + got_p[1] + got_p[2] + got_p[3]
    product = jnp.dot(
        product, oinv[...], preferred_element_type=F32, precision=HIGHEST
    ) * (1.0 / TOTAL)
    for o in range(27):
        precond[o] = product[2 * o : 2 * o + 2]

    activated_out.wait()
    input_grad_out.wait()
    for copy in sent:
        copy.wait_send()


def hand_on(*refs):
    sources, results, stops, sems = refs[:5], refs[5:10], refs[10:15], refs[15]
    arrivals = []
    for n in range(5):
        copy = pltpu.make_async_copy(sources[n], stops[n], sems.at[n])
        copy.start()
        arrivals.append(copy)
    departures = []
    for n in range(5):
        arrivals[n].wait()
        copy = pltpu.make_async_copy(stops[n], results[n], sems.at[5 + n])
        copy.start()
        departures.append(copy)
    for copy in departures:
        copy.wait()


def per_device(activations, upstream, kernel_weight, patch_inverse, output_inverse):
    vmem = pl.BlockSpec(memory_space=pltpu.VMEM)
    hbm = pl.BlockSpec(memory_space=pl.ANY)
    scratch = [
        ((4, 256, 128), BF16),
        ((4, 256, 128), BF16),
        ((27, 128, 128), BF16),
        ((27, 2, 3456), F32),
        ((128, 128), F32),
        ((4, 256, 128), BF16),
        ((4, 256, 128), BF16),
        ((2, 256, 128), BF16),
        ((2, 256, 128), BF16),
        ((4, 256, 128), BF16),
        ((5, 6, 320, 128), BF16),
        ((3, 6, 288, 128), BF16),
        ((2, 128, 1536), BF16),
        ((256, 1024), BF16),
        ((128, 1024), BF16),
        ((2, 32, 128, 128), F32),
        ((2, 32, 64, 128), F32),
        ((2, 32, 64, 128), BF16),
        ((2, 3, 32, 16, 128), BF16),
        ((2, 512, 128), F32),
        ((2, 4, 4, 32, 128), F32),
        ((2, 3, 4, 32, 128), F32),
        ((8, 32, 128), F32),
        ((7, 32, 128), F32),
        ((4, 2, 4, 128, 128), F32),
        ((4, 2, 4, 64, 128), F32),
        ((4, 2, 4, 64, 128), BF16),
        ((15, 4, 2, 16, 128), BF16),
        ((4, 2, 16, 128), F32),
        ((8, 2, 16, 128), F32),
        ((2, 4, 128, 128), F32),
        ((56, 3584), F32),
        ((56, 128), F32),
        ((4, 56, 128), F32),
    ]
    shapes = (
        jax.ShapeDtypeStruct((4, 256, 128), BF16),
        jax.ShapeDtypeStruct((4, 256, 128), BF16),
        jax.ShapeDtypeStruct((2, 32, 63), F32),
        jax.ShapeDtypeStruct((128, 128), F32),
        jax.ShapeDtypeStruct((27, 2, 128), F32),
    )
    outs = pl.pallas_call(
        step_kernel,
        out_shape=shapes,
        in_specs=[hbm] * 5,
        out_specs=[hbm, hbm, vmem, vmem, vmem],
        scratch_shapes=[pltpu.VMEM(shape, dtype) for shape, dtype in scratch]
        + [
            pltpu.SemaphoreType.DMA((8,)),
            pltpu.SemaphoreType.DMA((96,)),
            pltpu.SemaphoreType.DMA((96,)),
        ],
        compiler_params=pltpu.CompilerParams(
            collective_id=0, has_side_effects=True, vmem_limit_bytes=60 * 1024 * 1024
        ),
        name="step_kernel",
    )(
        activations.reshape(4, 256, 128),
        upstream.reshape(4, 256, 128),
        kernel_weight,
        patch_inverse,
        output_inverse,
    )
    outs = pl.pallas_call(
        hand_on,
        out_shape=shapes,
        in_specs=[hbm] * 5,
        out_specs=[hbm] * 5,
        scratch_shapes=[pltpu.VMEM(shape.shape, shape.dtype) for shape in shapes]
        + [pltpu.SemaphoreType.DMA((10,))],
        compiler_params=pltpu.CompilerParams(vmem_limit_bytes=60 * 1024 * 1024),
        name="hand_on",
    )(*outs)
    activated, input_grad, patch_factor, output_factor, precond = outs
    return (
        activated.reshape(activations.shape),
        input_grad.reshape(activations.shape),
        jnp.transpose(patch_factor, (0, 2, 1)),
        output_factor,
        precond,
    )


def solution(mesh):
    return jax.shard_map(
        per_device,
        mesh=mesh,
        in_specs=(
            P("dp", "space", None, None, None),
            P("dp", "space", None, None, None),
            P(),
            P(None, "space", None),
            P(),
        ),
        out_specs=(
            P("dp", "space", None, None, None),
            P("dp", "space", None, None, None),
            P("space", None, "dp"),
            P(),
            P(None, "space", None),
        ),
        check_vma=False,
    )
```

```python
import functools

import jax
import jax.numpy as jnp
from jax import lax
from jax.experimental import pallas as pl
from jax.experimental.pallas import tpu as pltpu
from jax.sharding import PartitionSpec as P

F32 = jnp.float32
BF16 = jnp.bfloat16
TOTAL = 262144.0
NT = (((1,), (1,)), ((), ()))
HIGHEST = lax.Precision.HIGHEST


def dot(a, b):
    return jnp.dot(a, b, preferred_element_type=F32)


def tap_shift(offset):
    return (offset // 9 - 1, offset // 3 % 3 - 1, offset % 3 - 1)


def step_kernel(
    act_hbm,
    up_hbm,
    kw_hbm,
    pinv_hbm,
    oinv_hbm,
    activated_hbm,
    input_grad_hbm,
    patch_factor,
    output_factor,
    precond,
    act,
    up,
    kw,
    pinv,
    oinv,
    activated,
    input_grad,
    halo_a,
    halo_s,
    slope,
    ext_a,
    ext_s,
    left,
    left12,
    slope_t,
    prod_l,
    got_lc,
    out_l1,
    got_l1,
    sum_l1,
    out_l2,
    got_l2,
    out_l3,
    got_l3,
    prod_w,
    got_wc,
    out_w1,
    got_w1,
    out_w3,
    got_w3,
    weights,
    inverse,
    inverse2,
    part_p,
    got_p,
    local_sem,
    send_sem,
    recv_sem,
):
    space = lax.axis_index("space")
    quarter = lax.axis_index("dp")
    core = lax.rem(space, 2)
    col = lax.rem(space // 2, 4)
    row = lax.rem(space // 8, 4)
    half = space // 32
    depth = half * 4 + quarter
    other = 1 - core

    def device(half, row, col, core, quarter):
        return {"space": ((half * 4 + row) * 4 + col) * 2 + core, "dp": quarter}

    sibling = device(half, row, col, other, quarter)
    following = {"space": lax.rem(space + 1, 64), "dp": quarter}
    preceding = {"space": lax.rem(space + 63, 64), "dp": quarter}
    far = {"space": lax.rem(space + 2 * core + 63, 64), "dp": quarter}

    def along_x(t):
        at = lax.rem(col + t, 4)
        return at, device(half, row, at, core, quarter)

    def along_y(t):
        at = lax.rem(row + t, 4)
        return at, device(half, at, col, core, quarter)

    def in_plane(t):
        at_y = lax.rem(row + t // 4, 4)
        at_x = lax.rem(col + t % 4, 4)
        return at_y, at_x, device(half, at_y, at_x, core, quarter)

    def along_z(t):
        at = lax.rem(depth + t, 8)
        return at, device(at // 4, row, col, core, lax.rem(at, 4))

    def along_dp(t, which):
        return device(half, row, col, which, lax.rem(quarter + t, 4))

    def sixteen(at):
        return pl.ds(pl.multiple_of(at * 16, 16), 16)

    count = [0, 0]
    sent = []
    moved_out = []

    def send(src, dst, to):
        n = count[0]
        count[0] += 1
        copy = pltpu.make_async_remote_copy(
            src_ref=src,
            dst_ref=dst,
            send_sem=send_sem.at[n],
            recv_sem=recv_sem.at[n],
            device_id=to,
            device_id_type=pl.DeviceIdType.MESH,
        )
        copy.start()
        sent.append(copy)
        return copy

    def move(src, dst):
        n = count[1]
        count[1] += 1
        copy = pltpu.make_async_copy(src, dst, local_sem.at[n])
        copy.start()
        return copy

    partners = [sibling, far]
    partners += [in_plane(t)[2] for t in range(1, 16)]
    partners += [along_z(t)[1] for t in range(1, 8)]
    partners += [along_dp(t, other) for t in range(1, 4)]
    barrier = pltpu.get_barrier_semaphore()
    for partner in partners:
        pl.semaphore_signal(
            barrier, inc=1, device_id=partner, device_id_type=pl.DeviceIdType.MESH
        )

    act_in = move(act_hbm, act)
    kw_in = move(kw_hbm, kw)
    up_in = move(up_hbm, up)
    pinv_in = move(pinv_hbm, pinv)
    oinv_in = move(oinv_hbm, oinv)

    r = lax.broadcasted_iota(jnp.int32, (128, 128), 0)
    c = lax.broadcasted_iota(jnp.int32, (128, 128), 1)

    def picked(first, second):
        chan = (
            (r & 1)
            + 2 * ((r >> 6) & 1)
            + first * ((r >> 4) & 3)
            + second * ((r >> 2) & 3)
            + 64 * ((r >> 1) & 1)
        )
        return jnp.where(c == chan, 1.0, 0.0).astype(BF16)

    orders = (picked(4, 16), picked(16, 4))
    unit = jnp.where(c == r, 1.0, 0.0).astype(BF16)

    def turned(order, plane):
        return lax.dot_general(order, plane, NT, preferred_element_type=F32).astype(BF16)

    def place_a(plane, at):
        wide = plane.astype(F32).reshape(16, 16, 128)
        for dx in range(-2, 3):
            moved = plane
            if dx:
                moved = pltpu.roll(wide, (-dx) % 16, 1).reshape(256, 128).astype(BF16)
            ext_a[dx + 2, at, 32:288, :] = moved
            ext_a[dx + 2, at, 0:32, :] = moved[224:256]
            ext_a[dx + 2, at, 288:320, :] = moved[0:32]
        for part in range(2):
            left[part, :, at * 256 : (at + 1) * 256] = turned(orders[part], plane)

    def place_s(plane, at):
        wide = plane.astype(F32).reshape(16, 16, 128)
        for dx in range(-1, 2):
            moved = plane
            if dx:
                moved = pltpu.roll(wide, (-dx) % 16, 1).reshape(256, 128).astype(BF16)
            ext_s[dx + 1, at, 16:272, :] = moved
            ext_s[dx + 1, at, 0:16, :] = moved[240:256]
            ext_s[dx + 1, at, 272:288, :] = moved[0:16]

    def rows_a(first, dy, dx, planes=4):
        return ext_a[
            dx + 2, first : first + planes, (2 + dy) * 16 : (2 + dy) * 16 + 256, :
        ].reshape(planes * 256, 128)

    def ends_a(dz, dy, dx):
        return jnp.concatenate([rows_a(1 + dz, dy, dx, 1), rows_a(4 + dz, dy, dx, 1)], axis=0)

    prod_l[1, 31] = jnp.zeros((128, 128), F32)
    prod_w[3, 1, 2] = jnp.zeros((128, 128), F32)
    inverse[:, 3456:3584] = jnp.zeros((56, 128), F32)
    inverse[48:56, :] = jnp.zeros((8, 3584), F32)

    act_in.wait()
    for z in range(4):
        place_a(act[z], z + 1)
    for k in range(13):
        m = k + 62
        part, slot = (0, 25 + k) if k < 7 else (1, 18 + k)
        prod_l[part, slot] = dot(
            left[part, :, 256:1280], rows_a(1, m // 5 % 5 - 2, m % 5 - 2)
        )

    kw_in.wait()
    up_in.wait()

    def forward(z):
        taps = []
        for o in range(27):
            dz, dy, dx = tap_shift(o)
            taps.append(ext_a[dx + 2, z + 1 + dz, (2 + dy) * 16 : (2 + dy) * 16 + 256, :])
        pre = dot(jnp.concatenate(taps, axis=1), kw[...].reshape(27 * 128, 128))
        logistic = jax.nn.sigmoid(pre)
        activated[z] = (pre * logistic).astype(BF16)
        sloped = (up[z].astype(F32) * logistic * (1.0 + pre * (1.0 - logistic))).astype(BF16)
        slope[z] = sloped
        slope_t[:, z * 256 : (z + 1) * 256] = turned(unit, sloped)

    forward(1)
    forward(2)

    pl.semaphore_wait(barrier, len(partners))
    before = send(act.at[3], halo_a.at[0], following)
    after = send(act.at[0], halo_a.at[1], preceding)

    theirs = pl.ds(pl.multiple_of(other * 64, 64), 64)
    mine = pl.ds(pl.multiple_of(core * 64, 64), 64)
    firsts = (col, row)
    seconds = (row, col)
    first_axis = (along_x, along_y)
    second_axis = (along_y, along_x)

    def swap_l(first, last):
        return send(
            prod_l.at[:, first:last, theirs, :], got_lc.at[:, first:last], sibling
        )

    def spread_l(first, last):
        copies = []
        for part in range(2):
            out_l1[part, first:last] = (
                prod_l[part, first:last, mine, :] + got_lc[part, first:last]
            ).astype(BF16)
            for t in range(1, 4):
                at, to = first_axis[part](t)
                copies.append(
                    send(
                        out_l1.at[part, first:last, sixteen(at), :],
                        got_l1.at[part, t - 1, first:last],
                        to,
                    )
                )
        return copies

    early_c = swap_l(25, 32)

    def blocks(d):
        for b in range(7):
            if 7 * d + b < 27:
                yield b, tap_shift(7 * d + b)

    inner_t = slope_t[:, 256:768]
    for d in range(4):
        for b, (dz, dy, dx) in blocks(d):
            prod_w[d, b // 4, b % 4] = dot(inner_t, rows_a(2 + dz, dy, dx, 2))
    inner_own = dot(inner_t, slope[1:3].reshape(512, 128))

    early_c.wait_recv()
    l1 = spread_l(25, 32)

    pinv_in.wait()
    for o in range(27):
        inverse[2 * o : 2 * o + 2, 0:3456] = pinv[o]
    inverse2[core] = inverse[:, pl.ds(pl.multiple_of(quarter * 896, 128), 896)]
    rows_in = send(inverse2.at[core], inverse2.at[core], sibling)

    before.wait_recv()
    place_a(halo_a[0], 0)
    after.wait_recv()
    place_a(halo_a[1], 5)
    forward(3)
    forward(0)
    before_s = send(slope.at[3], halo_s.at[0], following)
    after_s = send(slope.at[0], halo_s.at[1], preceding)
    activated_out = move(activated, activated_hbm)

    outer_t = jnp.concatenate([slope_t[:, 0:256], slope_t[:, 768:1024]], axis=1)
    own = inner_own + dot(outer_t, jnp.concatenate([slope[0], slope[3]], axis=0))
    wc = []
    for d in range(4):
        prod_w[d, 1, 3] = own
        for b, (dz, dy, dx) in blocks(d):
            prod_w[d, b // 4, b % 4] += dot(outer_t, ends_a(dz, dy, dx))
        wc.append(send(prod_w.at[d, :, :, theirs, :], got_wc.at[d], sibling))

    left12[0:128, :] = left[0, :, 256:1280]
    left12[128:256, :] = left[1, :, 0:1024]
    pairs = [(dy, dx) for dy in range(-2, 3) for dx in range(-2, 3)]

    def lag_block(first, last):
        for s in range(first, last):
            both = dot(left12[...], rows_a(2, *pairs[s]))
            prod_l[0, s] = both[0:128]
            prod_l[1, s] = both[128:256]
        return swap_l(first, last)

    w1 = []

    def spread_w(first, last):
        for copy in wc[first:last]:
            copy.wait_recv()
        out_w1[first:last] = (prod_w[first:last, :, :, mine, :] + got_wc[first:last]).astype(BF16)
        for t in range(1, 16):
            at_y, at_x, to = in_plane(t)
            w1.append(
                send(
                    out_w1.at[first:last, :, at_y, sixteen(at_x), :],
                    got_w1.at[t - 1, first:last],
                    to,
                )
            )

    spread_w(0, 2)
    lc = [lag_block(0, 6)]
    spread_w(2, 4)
    lc.append(lag_block(6, 13))
    lc.append(lag_block(13, 25))
    lc[0].wait_recv()
    lc[1].wait_recv()
    l1 += spread_l(0, 13)
    lc[2].wait_recv()
    l1 += spread_l(13, 25)

    for z in range(4):
        place_s(slope[z], z + 1)
    before_s.wait_recv()
    after_s.wait_recv()
    place_s(halo_s[0], 0)
    place_s(halo_s[1], 5)

    kernel_cols = jnp.concatenate([kw[o] for o in range(27)], axis=1)

    def back(z):
        taps = []
        for o in range(27):
            dz, dy, dx = tap_shift(o)
            taps.append(ext_s[1 - dx, z + 1 - dz, (1 - dy) * 16 : (1 - dy) * 16 + 256, :])
        grad = lax.dot_general(
            jnp.concatenate(taps, axis=1), kernel_cols, NT, preferred_element_type=F32
        )
        input_grad[z] = grad.astype(BF16)

    back(0)

    for copy in w1:
        copy.wait_recv()
    tall = sixteen(core * 4 + col)
    total_w = prod_w[:, :, row, tall, :] + got_wc[:, :, row, sixteen(col), :]
    for t in range(15):
        total_w = total_w + got_w1[t].astype(F32)
    out_w3[...] = total_w
    got_w3[depth] = out_w3[quarter]
    w3 = []
    for t in range(1, 8):
        at, to = along_z(t)
        w3.append(send(out_w3.at[lax.rem(at, 4)], got_w3.at[depth], to))

    back(1)

    for copy in l1:
        copy.wait_recv()
    l2 = []
    for part in range(2):
        kept = sixteen(firsts[part])
        high = sixteen(core * 4 + firsts[part])
        total = prod_l[part, :, high, :] + got_lc[part, :, kept, :]
        for t in range(3):
            total = total + got_l1[part, t].astype(F32)
        sum_l1[part] = total.reshape(512, 128)
        for b in range(4):
            for n in range(4):
                for g in range(4):
                    out_l2[part, b, n, 8 * g : 8 * g + 8, :] = sum_l1[
                        part, pl.ds(4 * b + n + 128 * g, 8, stride=16), :
                    ]
        for t in range(1, 4):
            at, to = second_axis[part](t)
            l2.append(send(out_l2.at[part, at], got_l2.at[part, t - 1], to))

    back(2)

    for copy in w3:
        copy.wait_recv()
    reduced = got_w3[0]
    for z in range(1, 8):
        reduced = reduced + got_w3[z]
    weights[:, row, tall, :] = reduced
    g1 = []
    for t in range(1, 16):
        piece = weights.at[:, row, tall, :]
        g1.append(send(piece, piece, in_plane(t)[2]))

    back(3)
    input_grad_out = move(input_grad, input_grad_hbm)

    for copy in l2:
        copy.wait_recv()
    group = c[0:32] // 32
    totals = []
    for part in range(2):
        total = out_l2[part, seconds[part]]
        for t in range(3):
            total = total + got_l2[part, t]
        totals.append(total)
    for h in range(2):
        groups = [totals[part][2 * h + i] for part in range(2) for i in range(2)]
        for q in range(4):
            packed = jnp.zeros((32, 128), F32)
            for j in range(4):
                shift = (32 * (j - q)) % 128
                piece = pltpu.roll(groups[j], shift, 1) if shift else groups[j]
                packed = jnp.where(group == j, piece, packed)
            out_l3[4 * h + q] = packed
    l3 = []
    for t in range(1, 8):
        at, to = along_z(t)
        l3.append(send(out_l3.at[at], got_l3.at[t - 1], to))

    for copy in g1:
        copy.wait_recv()
    own_in = send(weights.at[1, 3, mine, :], weights.at[1, 3, mine, :], sibling)
    rows_in.wait_recv()
    gathered = jnp.concatenate([weights[b // 4, b % 4, mine, :] for b in range(7)], axis=1)
    both_p = lax.dot_general(
        inverse2[...].reshape(112, 896),
        gathered,
        NT,
        preferred_element_type=F32,
        precision=HIGHEST,
    )
    part_p[0] = both_p[0:56]
    part_p[1] = both_p[56:112]
    got_p[quarter, core] = part_p[core]
    pp = [send(part_p.at[other], got_p.at[quarter, core], sibling)]
    for t in (3, 1, 2):
        for which in (core, other):
            pp.append(send(part_p.at[which], got_p.at[quarter, core], along_dp(t, which)))
    own_in.wait_recv()
    output_factor[...] = weights[1, 3] * (1.0 / TOTAL)

    for copy in l3:
        copy.wait_recv()
    final = out_l3[depth]
    for t in range(7):
        final = final + got_l3[t]
    final = final * (1.0 / TOTAL)
    flipped = jnp.concatenate([final, jnp.zeros((96, 128), F32)], axis=0).T
    lane = c[0:32]
    for i in range(2):
        one = flipped[32 * i : 32 * i + 32]
        two = flipped[64 + 32 * i : 96 + 32 * i]
        piece = jnp.where(lane < 7, pltpu.roll(one, 103, 1), pltpu.roll(two, 110, 1))
        piece = jnp.where(lane < 13, piece, pltpu.roll(one, 13, 1))
        piece = jnp.where(lane < 38, piece, pltpu.roll(two, 38, 1))
        patch_factor[i] = piece[:, 0:63]

    oinv_in.wait()
    for copy in pp:
        copy.wait_recv()
    product = jnp.zeros((56, 128), F32)
    for which in range(2):
        piece = got_p[0, which] + got_p[1, which] + got_p[2, which] + got_p[3, which]
        product += jnp.dot(
            piece,
            oinv[64 * which : 64 * which + 64, :],
            preferred_element_type=F32,
            precision=HIGHEST,
        )
    product = product * (1.0 / TOTAL)
    for o in range(27):
        precond[o] = product[2 * o : 2 * o + 2]

    activated_out.wait()
    input_grad_out.wait()
    for copy in sent:
        copy.wait_send()


def hand_on(*refs):
    sources, results, stops, sems = refs[:5], refs[5:10], refs[10:15], refs[15]
    arrivals = []
    for n in range(5):
        copy = pltpu.make_async_copy(sources[n], stops[n], sems.at[n])
        copy.start()
        arrivals.append(copy)
    departures = []
    for n in range(5):
        arrivals[n].wait()
        copy = pltpu.make_async_copy(stops[n], results[n], sems.at[5 + n])
        copy.start()
        departures.append(copy)
    for copy in departures:
        copy.wait()


def per_device(activations, upstream, kernel_weight, patch_inverse, output_inverse):
    vmem = pl.BlockSpec(memory_space=pltpu.VMEM)
    hbm = pl.BlockSpec(memory_space=pl.ANY)
    scratch = [
        ((4, 256, 128), BF16),
        ((4, 256, 128), BF16),
        ((27, 128, 128), BF16),
        ((27, 2, 3456), F32),
        ((128, 128), F32),
        ((4, 256, 128), BF16),
        ((4, 256, 128), BF16),
        ((2, 256, 128), BF16),
        ((2, 256, 128), BF16),
        ((4, 256, 128), BF16),
        ((5, 6, 320, 128), BF16),
        ((3, 6, 288, 128), BF16),
        ((2, 128, 1536), BF16),
        ((256, 1024), BF16),
        ((128, 1024), BF16),
        ((2, 32, 128, 128), F32),
        ((2, 32, 64, 128), F32),
        ((2, 32, 64, 128), BF16),
        ((2, 3, 32, 16, 128), BF16),
        ((2, 512, 128), F32),
        ((2, 4, 4, 32, 128), F32),
        ((2, 3, 4, 32, 128), F32),
        ((8, 32, 128), F32),
        ((7, 32, 128), F32),
        ((4, 2, 4, 128, 128), F32),
        ((4, 2, 4, 64, 128), F32),
        ((4, 2, 4, 64, 128), BF16),
        ((15, 4, 2, 16, 128), BF16),
        ((4, 2, 16, 128), F32),
        ((8, 2, 16, 128), F32),
        ((2, 4, 128, 128), F32),
        ((56, 3584), F32),
        ((2, 56, 896), F32),
        ((2, 56, 64), F32),
        ((4, 2, 56, 64), F32),
    ]
    shapes = (
        jax.ShapeDtypeStruct((4, 256, 128), BF16),
        jax.ShapeDtypeStruct((4, 256, 128), BF16),
        jax.ShapeDtypeStruct((2, 32, 63), F32),
        jax.ShapeDtypeStruct((128, 128), F32),
        jax.ShapeDtypeStruct((27, 2, 128), F32),
    )
    outs = pl.pallas_call(
        step_kernel,
        out_shape=shapes,
        in_specs=[hbm] * 5,
        out_specs=[hbm, hbm, vmem, vmem, vmem],
        scratch_shapes=[pltpu.VMEM(shape, dtype) for shape, dtype in scratch]
        + [
            pltpu.SemaphoreType.DMA((8,)),
            pltpu.SemaphoreType.DMA((128,)),
            pltpu.SemaphoreType.DMA((128,)),
        ],
        compiler_params=pltpu.CompilerParams(
            collective_id=0, has_side_effects=True, vmem_limit_bytes=60 * 1024 * 1024
        ),
        name="step_kernel",
    )(
        activations.reshape(4, 256, 128),
        upstream.reshape(4, 256, 128),
        kernel_weight,
        patch_inverse,
        output_inverse,
    )
    outs = pl.pallas_call(
        hand_on,
        out_shape=shapes,
        in_specs=[hbm] * 5,
        out_specs=[hbm] * 5,
        scratch_shapes=[pltpu.VMEM(shape.shape, shape.dtype) for shape in shapes]
        + [pltpu.SemaphoreType.DMA((10,))],
        compiler_params=pltpu.CompilerParams(vmem_limit_bytes=60 * 1024 * 1024),
        name="hand_on",
    )(*outs)
    activated, input_grad, patch_factor, output_factor, precond = outs
    return (
        activated.reshape(activations.shape),
        input_grad.reshape(activations.shape),
        jnp.transpose(patch_factor, (0, 2, 1)),
        output_factor,
        precond,
    )


def solution(mesh):
    return jax.shard_map(
        per_device,
        mesh=mesh,
        in_specs=(
            P("dp", "space", None, None, None),
            P("dp", "space", None, None, None),
            P(),
            P(None, "space", None),
            P(),
        ),
        out_specs=(
            P("dp", "space", None, None, None),
            P("dp", "space", None, None, None),
            P("space", None, "dp"),
            P(),
            P(None, "space", None),
        ),
        check_vma=False,
    )
```

```python
import functools

import jax
import jax.numpy as jnp
from jax import lax
from jax.experimental import pallas as pl
from jax.experimental.pallas import tpu as pltpu
from jax.sharding import PartitionSpec as P

F32 = jnp.float32
BF16 = jnp.bfloat16
TOTAL = 262144.0
NT = (((1,), (1,)), ((), ()))
HIGHEST = lax.Precision.HIGHEST


def dot(a, b):
    return jnp.dot(a, b, preferred_element_type=F32)


def tap_shift(offset):
    return (offset // 9 - 1, offset // 3 % 3 - 1, offset % 3 - 1)


def step_kernel(
    act_hbm,
    up_hbm,
    kw_hbm,
    pinv_hbm,
    oinv_hbm,
    activated_hbm,
    input_grad_hbm,
    patch_factor,
    output_factor,
    precond,
    act,
    up,
    kw,
    pinv,
    oinv,
    activated,
    input_grad,
    halo_a,
    halo_s,
    slope,
    ext_a,
    ext_s,
    left,
    left12,
    slope_t,
    begun,
    prod_l,
    got_lc,
    out_l1,
    got_l1,
    sum_l1,
    out_l2,
    got_l2,
    out_l3,
    got_l3,
    prod_w,
    got_wc,
    out_w1,
    got_w1,
    out_w3,
    got_w3,
    weights,
    inverse,
    inverse2,
    part_p,
    got_p,
    local_sem,
    send_sem,
    recv_sem,
):
    space = lax.axis_index("space")
    quarter = lax.axis_index("dp")
    core = lax.rem(space, 2)
    col = lax.rem(space // 2, 4)
    row = lax.rem(space // 8, 4)
    half = space // 32
    depth = half * 4 + quarter
    other = 1 - core

    def device(half, row, col, core, quarter):
        return {"space": ((half * 4 + row) * 4 + col) * 2 + core, "dp": quarter}

    sibling = device(half, row, col, other, quarter)
    following = {"space": lax.rem(space + 1, 64), "dp": quarter}
    preceding = {"space": lax.rem(space + 63, 64), "dp": quarter}
    far = {"space": lax.rem(space + 2 * core + 63, 64), "dp": quarter}

    def along_x(t):
        at = lax.rem(col + t, 4)
        return at, device(half, row, at, core, quarter)

    def along_y(t):
        at = lax.rem(row + t, 4)
        return at, device(half, at, col, core, quarter)

    def in_plane(t):
        at_y = lax.rem(row + t // 4, 4)
        at_x = lax.rem(col + t % 4, 4)
        return at_y, at_x, device(half, at_y, at_x, core, quarter)

    def along_z(t):
        at = lax.rem(depth + t, 8)
        return at, device(at // 4, row, col, core, lax.rem(at, 4))

    def along_dp(t, which):
        return device(half, row, col, which, lax.rem(quarter + t, 4))

    def sixteen(at):
        return pl.ds(pl.multiple_of(at * 16, 16), 16)

    count = [0, 0]
    sent = []
    moved_out = []

    def send(src, dst, to):
        n = count[0]
        count[0] += 1
        copy = pltpu.make_async_remote_copy(
            src_ref=src,
            dst_ref=dst,
            send_sem=send_sem.at[n],
            recv_sem=recv_sem.at[n],
            device_id=to,
            device_id_type=pl.DeviceIdType.MESH,
        )
        copy.start()
        sent.append(copy)
        return copy

    def move(src, dst):
        n = count[1]
        count[1] += 1
        copy = pltpu.make_async_copy(src, dst, local_sem.at[n])
        copy.start()
        return copy

    partners = [sibling, far]
    partners += [in_plane(t)[2] for t in range(1, 16)]
    partners += [along_z(t)[1] for t in range(1, 8)]
    partners += [along_dp(t, other) for t in range(1, 4)]
    barrier = pltpu.get_barrier_semaphore()
    for partner in partners:
        pl.semaphore_signal(
            barrier, inc=1, device_id=partner, device_id_type=pl.DeviceIdType.MESH
        )

    act_in = move(act_hbm, act)
    kw_in = move(kw_hbm, kw)
    up_in = move(up_hbm, up)
    pinv_in = move(pinv_hbm, pinv)
    oinv_in = move(oinv_hbm, oinv)

    r = lax.broadcasted_iota(jnp.int32, (128, 128), 0)
    c = lax.broadcasted_iota(jnp.int32, (128, 128), 1)

    def picked(first, second):
        chan = (
            (r & 1)
            + 2 * ((r >> 6) & 1)
            + first * ((r >> 4) & 3)
            + second * ((r >> 2) & 3)
            + 64 * ((r >> 1) & 1)
        )
        return jnp.where(c == chan, 1.0, 0.0).astype(BF16)

    orders = (picked(4, 16), picked(16, 4))
    unit = jnp.where(c == r, 1.0, 0.0).astype(BF16)

    def turned(order, plane):
        return lax.dot_general(order, plane, NT, preferred_element_type=F32).astype(BF16)

    def place_a(plane, at):
        wide = plane.astype(F32).reshape(16, 16, 128)
        for dx in range(-2, 3):
            moved = plane
            if dx:
                moved = pltpu.roll(wide, (-dx) % 16, 1).reshape(256, 128).astype(BF16)
            ext_a[dx + 2, at, 32:288, :] = moved
            ext_a[dx + 2, at, 0:32, :] = moved[224:256]
            ext_a[dx + 2, at, 288:320, :] = moved[0:32]

    def turn_a(plane, at):
        for part in range(2):
            left[part, :, at * 256 : (at + 1) * 256] = turned(orders[part], plane)

    def place_s(plane, at):
        wide = plane.astype(F32).reshape(16, 16, 128)
        for dx in range(-1, 2):
            moved = plane
            if dx:
                moved = pltpu.roll(wide, (-dx) % 16, 1).reshape(256, 128).astype(BF16)
            ext_s[dx + 1, at, 16:272, :] = moved
            ext_s[dx + 1, at, 0:16, :] = moved[240:256]
            ext_s[dx + 1, at, 272:288, :] = moved[0:16]

    def rows_a(first, dy, dx, planes=4):
        return ext_a[
            dx + 2, first : first + planes, (2 + dy) * 16 : (2 + dy) * 16 + 256, :
        ].reshape(planes * 256, 128)

    def ends_a(dz, dy, dx):
        return jnp.concatenate([rows_a(1 + dz, dy, dx, 1), rows_a(4 + dz, dy, dx, 1)], axis=0)

    prod_l[1, 31] = jnp.zeros((128, 128), F32)
    prod_w[3, 1, 2] = jnp.zeros((128, 128), F32)
    inverse[:, 3456:3584] = jnp.zeros((64, 128), F32)
    inverse[48:64, :] = jnp.zeros((16, 3584), F32)

    act_in.wait()
    for z in range(4):
        place_a(act[z], z + 1)
        turn_a(act[z], z + 1)
    for k in range(13):
        m = k + 62
        part, slot = (0, 25 + k) if k < 7 else (1, 18 + k)
        prod_l[part, slot] = dot(
            left[part, :, 256:1280], rows_a(1, m // 5 % 5 - 2, m % 5 - 2)
        )

    kw_in.wait()
    up_in.wait()

    def taps_sum(z, depths):
        taps = []
        for dz in depths:
            for o in range(9):
                dy, dx = o // 3 - 1, o % 3 - 1
                first = (2 + dy) * 16
                taps.append(ext_a[dx + 2, z + 1 + dz, first : first + 256, :])
        matrix = kw[9 * depths[0] + 9 : 9 * depths[-1] + 18].reshape(len(taps) * 128, 128)
        return dot(jnp.concatenate(taps, axis=1), matrix)

    def forward(z, pre):
        logistic = jax.nn.sigmoid(pre)
        activated[z] = (pre * logistic).astype(BF16)
        sloped = (up[z].astype(F32) * logistic * (1.0 + pre * (1.0 - logistic))).astype(BF16)
        slope[z] = sloped
        slope_t[:, z * 256 : (z + 1) * 256] = turned(unit, sloped)

    forward(1, taps_sum(1, (-1, 0, 1)))
    forward(2, taps_sum(2, (-1, 0, 1)))
    begun[0] = taps_sum(0, (0, 1))
    begun[1] = taps_sum(3, (-1, 0))

    pl.semaphore_wait(barrier, len(partners))
    before = send(act.at[3], halo_a.at[0], following)
    after = send(act.at[0], halo_a.at[1], preceding)

    theirs = pl.ds(pl.multiple_of(other * 64, 64), 64)
    mine = pl.ds(pl.multiple_of(core * 64, 64), 64)
    firsts = (col, row)
    seconds = (row, col)
    first_axis = (along_x, along_y)
    second_axis = (along_y, along_x)

    def swap_l(first, last):
        return send(
            prod_l.at[:, first:last, theirs, :], got_lc.at[:, first:last], sibling
        )

    def spread_l(first, last):
        copies = []
        for part in range(2):
            out_l1[part, first:last] = (
                prod_l[part, first:last, mine, :] + got_lc[part, first:last]
            ).astype(BF16)
            for t in range(1, 4):
                at, to = first_axis[part](t)
                copies.append(
                    send(
                        out_l1.at[part, first:last, sixteen(at), :],
                        got_l1.at[part, t - 1, first:last],
                        to,
                    )
                )
        return copies

    early_c = swap_l(25, 32)

    def blocks(d):
        for b in range(7):
            if 7 * d + b < 27:
                yield b, tap_shift(7 * d + b)

    inner_t = slope_t[:, 256:768]
    for d in range(4):
        for b, (dz, dy, dx) in blocks(d):
            prod_w[d, b // 4, b % 4] = dot(inner_t, rows_a(2 + dz, dy, dx, 2))
    inner_own = dot(inner_t, slope[1:3].reshape(512, 128))

    early_c.wait_recv()
    l1 = spread_l(25, 32)

    pinv_in.wait()
    for o in range(27):
        inverse[2 * o : 2 * o + 2, 0:3456] = pinv[o]
    inverse2[core] = inverse[:, pl.ds(pl.multiple_of(quarter * 896, 128), 896)]
    rows_in = send(inverse2.at[core], inverse2.at[core], sibling)

    before.wait_recv()
    place_a(halo_a[0], 0)
    after.wait_recv()
    place_a(halo_a[1], 5)
    forward(3, begun[1] + taps_sum(3, (1,)))
    forward(0, begun[0] + taps_sum(0, (-1,)))
    before_s = send(slope.at[3], halo_s.at[0], following)
    after_s = send(slope.at[0], halo_s.at[1], preceding)
    activated_out = move(activated, activated_hbm)

    outer_t = jnp.concatenate([slope_t[:, 0:256], slope_t[:, 768:1024]], axis=1)
    own = inner_own + dot(outer_t, jnp.concatenate([slope[0], slope[3]], axis=0))
    wc = []
    for d in range(4):
        prod_w[d, 1, 3] = own
        for b, (dz, dy, dx) in blocks(d):
            prod_w[d, b // 4, b % 4] += dot(outer_t, ends_a(dz, dy, dx))
        wc.append(send(prod_w.at[d, :, :, theirs, :], got_wc.at[d], sibling))

    turn_a(halo_a[0], 0)
    left12[0:128, :] = left[0, :, 256:1280]
    left12[128:256, :] = left[1, :, 0:1024]
    pairs = [(dy, dx) for dy in range(-2, 3) for dx in range(-2, 3)]

    def lag_block(first, last):
        for s in range(first, last):
            both = dot(left12[...], rows_a(2, *pairs[s]))
            prod_l[0, s] = both[0:128]
            prod_l[1, s] = both[128:256]
        return swap_l(first, last)

    w1 = []

    def spread_w(first, last):
        for copy in wc[first:last]:
            copy.wait_recv()
        out_w1[first:last] = (prod_w[first:last, :, :, mine, :] + got_wc[first:last]).astype(BF16)
        for t in range(1, 16):
            at_y, at_x, to = in_plane(t)
            w1.append(
                send(
                    out_w1.at[first:last, :, at_y, sixteen(at_x), :],
                    got_w1.at[t - 1, first:last],
                    to,
                )
            )

    spread_w(0, 2)
    lc = [lag_block(0, 6)]
    spread_w(2, 4)
    lc.append(lag_block(6, 13))
    lc.append(lag_block(13, 25))
    lc[0].wait_recv()
    lc[1].wait_recv()
    l1 += spread_l(0, 13)
    lc[2].wait_recv()
    l1 += spread_l(13, 25)

    for z in range(4):
        place_s(slope[z], z + 1)
    before_s.wait_recv()
    after_s.wait_recv()
    place_s(halo_s[0], 0)
    place_s(halo_s[1], 5)

    kernel_cols = jnp.concatenate([kw[o] for o in range(27)], axis=1)

    def back(z):
        taps = []
        for o in range(27):
            dz, dy, dx = tap_shift(o)
            taps.append(ext_s[1 - dx, z + 1 - dz, (1 - dy) * 16 : (1 - dy) * 16 + 256, :])
        grad = lax.dot_general(
            jnp.concatenate(taps, axis=1), kernel_cols, NT, preferred_element_type=F32
        )
        input_grad[z] = grad.astype(BF16)

    back(0)

    for copy in w1:
        copy.wait_recv()
    tall = sixteen(core * 4 + col)
    total_w = prod_w[:, :, row, tall, :] + got_wc[:, :, row, sixteen(col), :]
    for t in range(15):
        total_w = total_w + got_w1[t].astype(F32)
    out_w3[...] = total_w
    got_w3[depth] = out_w3[quarter]
    w3 = []
    for t in range(1, 8):
        at, to = along_z(t)
        w3.append(send(out_w3.at[lax.rem(at, 4)], got_w3.at[depth], to))

    back(1)

    for copy in l1:
        copy.wait_recv()
    l2 = []
    for part in range(2):
        kept = sixteen(firsts[part])
        high = sixteen(core * 4 + firsts[part])
        total = prod_l[part, :, high, :] + got_lc[part, :, kept, :]
        for t in range(3):
            total = total + got_l1[part, t].astype(F32)
        sum_l1[part] = total.reshape(512, 128)
        for b in range(4):
            for n in range(4):
                for g in range(4):
                    out_l2[part, b, n, 8 * g : 8 * g + 8, :] = sum_l1[
                        part, pl.ds(4 * b + n + 128 * g, 8, stride=16), :
                    ]
        for t in range(1, 4):
            at, to = second_axis[part](t)
            l2.append(send(out_l2.at[part, at], got_l2.at[part, t - 1], to))

    back(2)

    for copy in w3:
        copy.wait_recv()
    reduced = got_w3[0]
    for z in range(1, 8):
        reduced = reduced + got_w3[z]
    weights[:, row, tall, :] = reduced
    g1 = []
    for t in range(1, 16):
        piece = weights.at[:, row, tall, :]
        g1.append(send(piece, piece, in_plane(t)[2]))

    back(3)
    input_grad_out = move(input_grad, input_grad_hbm)

    for copy in l2:
        copy.wait_recv()
    group = c[0:32] // 32
    totals = []
    for part in range(2):
        total = out_l2[part, seconds[part]]
        for t in range(3):
            total = total + got_l2[part, t]
        totals.append(total)
    for h in range(2):
        groups = [totals[part][2 * h + i] for part in range(2) for i in range(2)]
        for q in range(4):
            packed = jnp.zeros((32, 128), F32)
            for j in range(4):
                shift = (32 * (j - q)) % 128
                piece = pltpu.roll(groups[j], shift, 1) if shift else groups[j]
                packed = jnp.where(group == j, piece, packed)
            out_l3[4 * h + q] = packed
    l3 = []
    for t in range(1, 8):
        at, to = along_z(t)
        l3.append(send(out_l3.at[at], got_l3.at[t - 1], to))

    for copy in g1:
        copy.wait_recv()
    own_in = send(weights.at[1, 3, mine, :], weights.at[1, 3, mine, :], sibling)
    rows_in.wait_recv()
    gathered = jnp.concatenate([weights[b // 4, b % 4, mine, :] for b in range(7)], axis=1)
    blank = jnp.zeros((64, 896), F32)
    packed_p = jnp.zeros((64, 128), F32)
    for n in range(2):
        packed_p += lax.dot_general(
            inverse2[:, 32 * n : 32 * n + 32, :].reshape(64, 896),
            jnp.concatenate([gathered, blank] if n == 0 else [blank, gathered], axis=0),
            NT,
            preferred_element_type=F32,
            precision=HIGHEST,
        )
    part_p[...] = packed_p.reshape(2, 32, 128)
    got_p[quarter, core] = part_p[core]
    pp = [send(part_p.at[other], got_p.at[quarter, core], sibling)]
    for t in (3, 1, 2):
        for which in (core, other):
            pp.append(send(part_p.at[which], got_p.at[quarter, core], along_dp(t, which)))
    own_in.wait_recv()
    output_factor[...] = weights[1, 3] * (1.0 / TOTAL)

    for copy in l3:
        copy.wait_recv()
    final = out_l3[depth]
    for t in range(7):
        final = final + got_l3[t]
    final = final * (1.0 / TOTAL)
    flipped = jnp.concatenate([final, jnp.zeros((96, 128), F32)], axis=0).T
    lane = c[0:32]
    for i in range(2):
        one = flipped[32 * i : 32 * i + 32]
        two = flipped[64 + 32 * i : 96 + 32 * i]
        piece = jnp.where(lane < 7, pltpu.roll(one, 103, 1), pltpu.roll(two, 110, 1))
        piece = jnp.where(lane < 13, piece, pltpu.roll(one, 13, 1))
        piece = jnp.where(lane < 38, piece, pltpu.roll(two, 38, 1))
        patch_factor[i] = piece[:, 0:63]

    oinv_in.wait()
    for copy in pp:
        copy.wait_recv()
    products = [jnp.zeros((32, 128), F32), jnp.zeros((32, 128), F32)]
    empty = jnp.zeros((64, 128), F32)
    for which in range(2):
        piece = got_p[0, which] + got_p[1, which] + got_p[2, which] + got_p[3, which]
        factor = oinv[64 * which : 64 * which + 64, :]
        for n in range(2):
            products[n] += jnp.dot(
                piece,
                jnp.concatenate([factor, empty] if n == 0 else [empty, factor], axis=0),
                preferred_element_type=F32,
                precision=HIGHEST,
            )
    product = jnp.concatenate(products, axis=0) * (1.0 / TOTAL)
    for o in range(27):
        precond[o] = product[2 * o : 2 * o + 2]

    activated_out.wait()
    input_grad_out.wait()
    for copy in sent:
        copy.wait_send()


def hand_on(*refs):
    sources, results, stops, sems = refs[:5], refs[5:10], refs[10:15], refs[15]
    arrivals = []
    for n in range(5):
        copy = pltpu.make_async_copy(sources[n], stops[n], sems.at[n])
        copy.start()
        arrivals.append(copy)
    departures = []
    for n in range(5):
        arrivals[n].wait()
        copy = pltpu.make_async_copy(stops[n], results[n], sems.at[5 + n])
        copy.start()
        departures.append(copy)
    for copy in departures:
        copy.wait()


def per_device(activations, upstream, kernel_weight, patch_inverse, output_inverse):
    vmem = pl.BlockSpec(memory_space=pltpu.VMEM)
    hbm = pl.BlockSpec(memory_space=pl.ANY)
    scratch = [
        ((4, 256, 128), BF16),
        ((4, 256, 128), BF16),
        ((27, 128, 128), BF16),
        ((27, 2, 3456), F32),
        ((128, 128), F32),
        ((4, 256, 128), BF16),
        ((4, 256, 128), BF16),
        ((2, 256, 128), BF16),
        ((2, 256, 128), BF16),
        ((4, 256, 128), BF16),
        ((5, 6, 320, 128), BF16),
        ((3, 6, 288, 128), BF16),
        ((2, 128, 1536), BF16),
        ((256, 1024), BF16),
        ((128, 1024), BF16),
        ((2, 256, 128), F32),
        ((2, 32, 128, 128), F32),
        ((2, 32, 64, 128), F32),
        ((2, 32, 64, 128), BF16),
        ((2, 3, 32, 16, 128), BF16),
        ((2, 512, 128), F32),
        ((2, 4, 4, 32, 128), F32),
        ((2, 3, 4, 32, 128), F32),
        ((8, 32, 128), F32),
        ((7, 32, 128), F32),
        ((4, 2, 4, 128, 128), F32),
        ((4, 2, 4, 64, 128), F32),
        ((4, 2, 4, 64, 128), BF16),
        ((15, 4, 2, 16, 128), BF16),
        ((4, 2, 16, 128), F32),
        ((8, 2, 16, 128), F32),
        ((2, 4, 128, 128), F32),
        ((64, 3584), F32),
        ((2, 64, 896), F32),
        ((2, 32, 128), F32),
        ((4, 2, 32, 128), F32),
    ]
    shapes = (
        jax.ShapeDtypeStruct((4, 256, 128), BF16),
        jax.ShapeDtypeStruct((4, 256, 128), BF16),
        jax.ShapeDtypeStruct((2, 32, 63), F32),
        jax.ShapeDtypeStruct((128, 128), F32),
        jax.ShapeDtypeStruct((27, 2, 128), F32),
    )
    outs = pl.pallas_call(
        step_kernel,
        out_shape=shapes,
        in_specs=[hbm] * 5,
        out_specs=[hbm, hbm, vmem, vmem, vmem],
        scratch_shapes=[pltpu.VMEM(shape, dtype) for shape, dtype in scratch]
        + [
            pltpu.SemaphoreType.DMA((8,)),
            pltpu.SemaphoreType.DMA((128,)),
            pltpu.SemaphoreType.DMA((128,)),
        ],
        compiler_params=pltpu.CompilerParams(
            collective_id=0, has_side_effects=True, vmem_limit_bytes=60 * 1024 * 1024
        ),
        name="step_kernel",
    )(
        activations.reshape(4, 256, 128),
        upstream.reshape(4, 256, 128),
        kernel_weight,
        patch_inverse,
        output_inverse,
    )
    outs = pl.pallas_call(
        hand_on,
        out_shape=shapes,
        in_specs=[hbm] * 5,
        out_specs=[hbm] * 5,
        scratch_shapes=[pltpu.VMEM(shape.shape, shape.dtype) for shape in shapes]
        + [pltpu.SemaphoreType.DMA((10,))],
        compiler_params=pltpu.CompilerParams(vmem_limit_bytes=60 * 1024 * 1024),
        name="hand_on",
    )(*outs)
    activated, input_grad, patch_factor, output_factor, precond = outs
    return (
        activated.reshape(activations.shape),
        input_grad.reshape(activations.shape),
        jnp.transpose(patch_factor, (0, 2, 1)),
        output_factor,
        precond,
    )


def solution(mesh):
    return jax.shard_map(
        per_device,
        mesh=mesh,
        in_specs=(
            P("dp", "space", None, None, None),
            P("dp", "space", None, None, None),
            P(),
            P(None, "space", None),
            P(),
        ),
        out_specs=(
            P("dp", "space", None, None, None),
            P("dp", "space", None, None, None),
            P("space", None, "dp"),
            P(),
            P(None, "space", None),
        ),
        check_vma=False,
    )
```

```python
import functools

import jax
import jax.numpy as jnp
from jax import lax
from jax.experimental import pallas as pl
from jax.experimental.pallas import tpu as pltpu
from jax.sharding import PartitionSpec as P

F32 = jnp.float32
BF16 = jnp.bfloat16
TOTAL = 262144.0
PLANE = (10, 6, 9, 11, 14, 5, 7, 13, 15, 2, 8, 1, 3, 4, 12)
RING = (4, 3, 5, 2, 6, 1, 7)
NT = (((1,), (1,)), ((), ()))
HIGHEST = lax.Precision.HIGHEST


def dot(a, b):
    return jnp.dot(a, b, preferred_element_type=F32)


def tap_shift(offset):
    return (offset // 9 - 1, offset // 3 % 3 - 1, offset % 3 - 1)


def step_kernel(
    act_hbm,
    up_hbm,
    kw_hbm,
    pinv_hbm,
    oinv_hbm,
    activated_hbm,
    input_grad_hbm,
    patch_factor,
    output_factor,
    precond,
    act,
    up,
    kw,
    pinv,
    oinv,
    activated,
    input_grad,
    halo_a,
    halo_s,
    slope,
    ext_a,
    ext_s,
    left,
    left12,
    slope_t,
    begun,
    prod_l,
    got_lc,
    out_l1,
    got_l1,
    sum_l1,
    out_l2,
    got_l2,
    out_l3,
    got_l3,
    prod_w,
    got_wc,
    out_w1,
    got_w1,
    out_w3,
    got_w3,
    weights,
    inverse,
    inverse2,
    part_p,
    got_p,
    local_sem,
    send_sem,
    recv_sem,
):
    space = lax.axis_index("space")
    quarter = lax.axis_index("dp")
    core = lax.rem(space, 2)
    col = lax.rem(space // 2, 4)
    row = lax.rem(space // 8, 4)
    half = space // 32
    depth = half * 4 + quarter
    other = 1 - core

    def device(half, row, col, core, quarter):
        return {"space": ((half * 4 + row) * 4 + col) * 2 + core, "dp": quarter}

    sibling = device(half, row, col, other, quarter)
    following = {"space": lax.rem(space + 1, 64), "dp": quarter}
    preceding = {"space": lax.rem(space + 63, 64), "dp": quarter}
    far = {"space": lax.rem(space + 2 * core + 63, 64), "dp": quarter}

    def along_x(t):
        at = lax.rem(col + t, 4)
        return at, device(half, row, at, core, quarter)

    def along_y(t):
        at = lax.rem(row + t, 4)
        return at, device(half, at, col, core, quarter)

    def in_plane(t):
        at_y = lax.rem(row + t // 4, 4)
        at_x = lax.rem(col + t % 4, 4)
        return at_y, at_x, device(half, at_y, at_x, core, quarter)

    def along_z(t):
        at = lax.rem(depth + t, 8)
        return at, device(at // 4, row, col, core, lax.rem(at, 4))

    def along_dp(t, which):
        return device(half, row, col, which, lax.rem(quarter + t, 4))

    def sixteen(at):
        return pl.ds(pl.multiple_of(at * 16, 16), 16)

    count = [0, 0]
    sent = []
    moved_out = []

    def send(src, dst, to):
        n = count[0]
        count[0] += 1
        copy = pltpu.make_async_remote_copy(
            src_ref=src,
            dst_ref=dst,
            send_sem=send_sem.at[n],
            recv_sem=recv_sem.at[n],
            device_id=to,
            device_id_type=pl.DeviceIdType.MESH,
        )
        copy.start()
        sent.append(copy)
        return copy

    def move(src, dst):
        n = count[1]
        count[1] += 1
        copy = pltpu.make_async_copy(src, dst, local_sem.at[n])
        copy.start()
        return copy

    partners = [far]
    partners += [along_z(t)[1] for t in RING]
    partners += [in_plane(t)[2] for t in PLANE]
    partners += [along_dp(t, other) for t in (3, 1, 2)]
    partners += [sibling]
    barrier = pltpu.get_barrier_semaphore()
    for partner in partners:
        pl.semaphore_signal(
            barrier, inc=1, device_id=partner, device_id_type=pl.DeviceIdType.MESH
        )

    act_in = move(act_hbm, act)
    kw_in = move(kw_hbm, kw)
    up_in = move(up_hbm, up)
    pinv_in = move(pinv_hbm, pinv)
    oinv_in = move(oinv_hbm, oinv)

    r = lax.broadcasted_iota(jnp.int32, (128, 128), 0)
    c = lax.broadcasted_iota(jnp.int32, (128, 128), 1)

    def picked(first, second):
        chan = (
            (r & 1)
            + 2 * ((r >> 6) & 1)
            + first * ((r >> 4) & 3)
            + second * ((r >> 2) & 3)
            + 64 * ((r >> 1) & 1)
        )
        return jnp.where(c == chan, 1.0, 0.0).astype(BF16)

    orders = (picked(4, 16), picked(16, 4))
    unit = jnp.where(c == r, 1.0, 0.0).astype(BF16)

    def turned(order, plane):
        return lax.dot_general(order, plane, NT, preferred_element_type=F32).astype(BF16)

    def place_a(plane, at):
        wide = plane.astype(F32).reshape(16, 16, 128)
        for dx in range(-2, 3):
            moved = plane
            if dx:
                moved = pltpu.roll(wide, (-dx) % 16, 1).reshape(256, 128).astype(BF16)
            ext_a[dx + 2, at, 32:288, :] = moved
            ext_a[dx + 2, at, 0:32, :] = moved[224:256]
            ext_a[dx + 2, at, 288:320, :] = moved[0:32]

    def turn_a(plane, at):
        for part in range(2):
            left[part, :, at * 256 : (at + 1) * 256] = turned(orders[part], plane)

    def place_s(plane, at):
        wide = plane.astype(F32).reshape(16, 16, 128)
        for dx in range(-1, 2):
            moved = plane
            if dx:
                moved = pltpu.roll(wide, (-dx) % 16, 1).reshape(256, 128).astype(BF16)
            ext_s[dx + 1, at, 16:272, :] = moved
            ext_s[dx + 1, at, 0:16, :] = moved[240:256]
            ext_s[dx + 1, at, 272:288, :] = moved[0:16]

    def rows_a(first, dy, dx, planes=4):
        return ext_a[
            dx + 2, first : first + planes, (2 + dy) * 16 : (2 + dy) * 16 + 256, :
        ].reshape(planes * 256, 128)

    def ends_a(dz, dy, dx):
        return jnp.concatenate([rows_a(1 + dz, dy, dx, 1), rows_a(4 + dz, dy, dx, 1)], axis=0)

    prod_l[1, 31] = jnp.zeros((128, 128), F32)
    prod_w[3, 1, 2] = jnp.zeros((128, 128), F32)
    inverse[:, 3456:3584] = jnp.zeros((64, 128), F32)
    inverse[48:64, :] = jnp.zeros((16, 3584), F32)

    act_in.wait()
    for z in range(4):
        place_a(act[z], z + 1)
        turn_a(act[z], z + 1)
    for k in range(13):
        m = k + 62
        part, slot = (0, 25 + k) if k < 7 else (1, 18 + k)
        prod_l[part, slot] = dot(
            left[part, :, 256:1280], rows_a(1, m // 5 % 5 - 2, m % 5 - 2)
        )

    pl.semaphore_wait(barrier, len(partners))
    before = send(act.at[3], halo_a.at[0], following)
    after = send(act.at[0], halo_a.at[1], preceding)

    def taps_sum(z, depths):
        taps = []
        for dz in depths:
            for o in range(9):
                dy, dx = o // 3 - 1, o % 3 - 1
                first = (2 + dy) * 16
                taps.append(ext_a[dx + 2, z + 1 + dz, first : first + 256, :])
        matrix = kw[9 * depths[0] + 9 : 9 * depths[-1] + 18].reshape(len(taps) * 128, 128)
        return dot(jnp.concatenate(taps, axis=1), matrix)

    def forward(z, pre):
        logistic = jax.nn.sigmoid(pre)
        activated[z] = (pre * logistic).astype(BF16)
        sloped = (up[z].astype(F32) * logistic * (1.0 + pre * (1.0 - logistic))).astype(BF16)
        slope[z] = sloped
        slope_t[:, z * 256 : (z + 1) * 256] = turned(unit, sloped)

    theirs = pl.ds(pl.multiple_of(other * 64, 64), 64)
    mine = pl.ds(pl.multiple_of(core * 64, 64), 64)
    firsts = (col, row)
    seconds = (row, col)
    first_axis = (along_x, along_y)
    second_axis = (along_y, along_x)

    def swap_l(first, last):
        return send(
            prod_l.at[:, first:last, theirs, :], got_lc.at[:, first:last], sibling
        )

    def spread_l(first, last):
        copies = []
        for part in range(2):
            out_l1[part, first:last] = (
                prod_l[part, first:last, mine, :] + got_lc[part, first:last]
            ).astype(BF16)
            for t in (2, 1, 3):
                at, to = first_axis[part](t)
                copies.append(
                    send(
                        out_l1.at[part, first:last, sixteen(at), :],
                        got_l1.at[part, t - 1, first:last],
                        to,
                    )
                )
        return copies

    early_c = swap_l(25, 32)
    kw_in.wait()
    up_in.wait()
    forward(1, taps_sum(1, (-1, 0, 1)))
    forward(2, taps_sum(2, (-1, 0, 1)))
    begun[0] = taps_sum(0, (0, 1))
    begun[1] = taps_sum(3, (-1, 0))

    def blocks(d):
        for b in range(7):
            if 7 * d + b < 27:
                yield b, tap_shift(7 * d + b)

    inner_t = slope_t[:, 256:768]
    for d in range(4):
        for b, (dz, dy, dx) in blocks(d):
            prod_w[d, b // 4, b % 4] = dot(inner_t, rows_a(2 + dz, dy, dx, 2))
    inner_own = dot(inner_t, slope[1:3].reshape(512, 128))

    early_c.wait_recv()
    l1 = spread_l(25, 32)

    pinv_in.wait()
    for o in range(27):
        inverse[2 * o : 2 * o + 2, 0:3456] = pinv[o]
    inverse2[core] = inverse[:, pl.ds(pl.multiple_of(quarter * 896, 128), 896)]
    rows_in = send(inverse2.at[core], inverse2.at[core], sibling)

    before.wait_recv()
    place_a(halo_a[0], 0)
    after.wait_recv()
    place_a(halo_a[1], 5)
    forward(3, begun[1] + taps_sum(3, (1,)))
    forward(0, begun[0] + taps_sum(0, (-1,)))
    before_s = send(slope.at[3], halo_s.at[0], following)
    after_s = send(slope.at[0], halo_s.at[1], preceding)
    activated_out = move(activated, activated_hbm)

    outer_t = jnp.concatenate([slope_t[:, 0:256], slope_t[:, 768:1024]], axis=1)
    own = inner_own + dot(outer_t, jnp.concatenate([slope[0], slope[3]], axis=0))
    wc = []
    for d in range(4):
        prod_w[d, 1, 3] = own
        for b, (dz, dy, dx) in blocks(d):
            prod_w[d, b // 4, b % 4] += dot(outer_t, ends_a(dz, dy, dx))
        wc.append(send(prod_w.at[d, :, :, theirs, :], got_wc.at[d], sibling))

    turn_a(halo_a[0], 0)
    left12[0:128, :] = left[0, :, 256:1280]
    left12[128:256, :] = left[1, :, 0:1024]
    pairs = [(dy, dx) for dy in range(-2, 3) for dx in range(-2, 3)]

    def lag_block(first, last):
        for s in range(first, last):
            both = dot(left12[...], rows_a(2, *pairs[s]))
            prod_l[0, s] = both[0:128]
            prod_l[1, s] = both[128:256]
        return swap_l(first, last)

    w1 = []

    def spread_w(first, last):
        for copy in wc[first:last]:
            copy.wait_recv()
        out_w1[first:last] = (prod_w[first:last, :, :, mine, :] + got_wc[first:last]).astype(BF16)
        for t in PLANE:
            at_y, at_x, to = in_plane(t)
            w1.append(
                send(
                    out_w1.at[first:last, :, at_y, sixteen(at_x), :],
                    got_w1.at[t - 1, first:last],
                    to,
                )
            )

    spread_w(0, 2)
    lc = [lag_block(0, 6)]
    spread_w(2, 4)
    lc.append(lag_block(6, 13))
    lc.append(lag_block(13, 25))
    lc[0].wait_recv()
    lc[1].wait_recv()
    l1 += spread_l(0, 13)
    lc[2].wait_recv()
    l1 += spread_l(13, 25)

    for z in range(4):
        place_s(slope[z], z + 1)
    before_s.wait_recv()
    after_s.wait_recv()
    place_s(halo_s[0], 0)
    place_s(halo_s[1], 5)

    kernel_cols = jnp.concatenate([kw[o] for o in range(27)], axis=1)

    def back(z):
        taps = []
        for o in range(27):
            dz, dy, dx = tap_shift(o)
            taps.append(ext_s[1 - dx, z + 1 - dz, (1 - dy) * 16 : (1 - dy) * 16 + 256, :])
        grad = lax.dot_general(
            jnp.concatenate(taps, axis=1), kernel_cols, NT, preferred_element_type=F32
        )
        input_grad[z] = grad.astype(BF16)

    back(0)

    for copy in w1:
        copy.wait_recv()
    tall = sixteen(core * 4 + col)
    total_w = prod_w[:, :, row, tall, :] + got_wc[:, :, row, sixteen(col), :]
    for t in range(15):
        total_w = total_w + got_w1[t].astype(F32)
    out_w3[...] = total_w
    got_w3[depth] = out_w3[quarter]
    w3 = []
    for t in RING:
        at, to = along_z(t)
        w3.append(send(out_w3.at[lax.rem(at, 4)], got_w3.at[depth], to))

    back(1)

    for copy in l1:
        copy.wait_recv()
    l2 = []
    for part in range(2):
        kept = sixteen(firsts[part])
        high = sixteen(core * 4 + firsts[part])
        total = prod_l[part, :, high, :] + got_lc[part, :, kept, :]
        for t in range(3):
            total = total + got_l1[part, t].astype(F32)
        sum_l1[part] = total.reshape(512, 128)
        for b in range(4):
            for n in range(4):
                groups = [
                    sum_l1[part, pl.ds(4 * b + n + 128 * g, 8, stride=16), :] for g in range(4)
                ]
                out_l2[part, b, n] = jnp.concatenate(groups, axis=0).astype(BF16)
        for t in (2, 1, 3):
            at, to = second_axis[part](t)
            l2.append(send(out_l2.at[part, at], got_l2.at[part, t - 1], to))

    back(2)

    for copy in w3:
        copy.wait_recv()
    reduced = got_w3[0]
    for z in range(1, 8):
        reduced = reduced + got_w3[z]
    weights[:, row, tall, :] = reduced
    g1 = []
    for t in PLANE:
        piece = weights.at[:, row, tall, :]
        g1.append(send(piece, piece, in_plane(t)[2]))

    back(3)
    input_grad_out = move(input_grad, input_grad_hbm)

    for copy in l2:
        copy.wait_recv()
    group = c[0:32] // 32
    totals = []
    for part in range(2):
        total = out_l2[part, seconds[part]].astype(F32)
        for t in range(3):
            total = total + got_l2[part, t].astype(F32)
        totals.append(total)
    for h in range(2):
        groups = [totals[part][2 * h + i] for part in range(2) for i in range(2)]
        for q in range(4):
            packed = jnp.zeros((32, 128), F32)
            for j in range(4):
                shift = (32 * (j - q)) % 128
                piece = pltpu.roll(groups[j], shift, 1) if shift else groups[j]
                packed = jnp.where(group == j, piece, packed)
            out_l3[4 * h + q] = packed
    l3 = []
    for t in RING:
        at, to = along_z(t)
        l3.append(send(out_l3.at[at], got_l3.at[t - 1], to))

    for copy in g1:
        copy.wait_recv()
    own_in = send(weights.at[1, 3, mine, :], weights.at[1, 3, mine, :], sibling)
    rows_in.wait_recv()
    gathered = jnp.concatenate([weights[b // 4, b % 4, mine, :] for b in range(7)], axis=1)
    blank = jnp.zeros((64, 896), F32)
    packed_p = jnp.zeros((64, 128), F32)
    for n in range(2):
        packed_p += lax.dot_general(
            inverse2[:, 32 * n : 32 * n + 32, :].reshape(64, 896),
            jnp.concatenate([gathered, blank] if n == 0 else [blank, gathered], axis=0),
            NT,
            preferred_element_type=F32,
            precision=HIGHEST,
        )
    part_p[...] = packed_p.reshape(2, 32, 128)
    got_p[quarter, core] = part_p[core]
    pp = [send(part_p.at[other], got_p.at[quarter, core], sibling)]
    for t in (3, 1, 2):
        for which in (core, other):
            pp.append(send(part_p.at[which], got_p.at[quarter, core], along_dp(t, which)))
    own_in.wait_recv()
    output_factor[...] = weights[1, 3] * (1.0 / TOTAL)

    for copy in l3:
        copy.wait_recv()
    final = out_l3[depth]
    for t in range(7):
        final = final + got_l3[t]
    final = final * (1.0 / TOTAL)
    flipped = jnp.concatenate([final, jnp.zeros((96, 128), F32)], axis=0).T
    lane = c[0:32]
    for i in range(2):
        one = flipped[32 * i : 32 * i + 32]
        two = flipped[64 + 32 * i : 96 + 32 * i]
        piece = jnp.where(lane < 7, pltpu.roll(one, 103, 1), pltpu.roll(two, 110, 1))
        piece = jnp.where(lane < 13, piece, pltpu.roll(one, 13, 1))
        piece = jnp.where(lane < 38, piece, pltpu.roll(two, 38, 1))
        patch_factor[i] = piece[:, 0:63]

    oinv_in.wait()
    for copy in pp:
        copy.wait_recv()
    products = [jnp.zeros((32, 128), F32), jnp.zeros((32, 128), F32)]
    empty = jnp.zeros((64, 128), F32)
    for which in range(2):
        piece = got_p[0, which] + got_p[1, which] + got_p[2, which] + got_p[3, which]
        factor = oinv[64 * which : 64 * which + 64, :]
        for n in range(2):
            products[n] += jnp.dot(
                piece,
                jnp.concatenate([factor, empty] if n == 0 else [empty, factor], axis=0),
                preferred_element_type=F32,
                precision=HIGHEST,
            )
    product = jnp.concatenate(products, axis=0) * (1.0 / TOTAL)
    for o in range(27):
        precond[o] = product[2 * o : 2 * o + 2]

    activated_out.wait()
    input_grad_out.wait()
    for copy in sent:
        copy.wait_send()


def hand_on(*refs):
    sources, results, stops, sems = refs[:5], refs[5:10], refs[10:15], refs[15]
    arrivals = []
    for n in range(5):
        copy = pltpu.make_async_copy(sources[n], stops[n], sems.at[n])
        copy.start()
        arrivals.append(copy)
    departures = []
    for n in range(5):
        arrivals[n].wait()
        copy = pltpu.make_async_copy(stops[n], results[n], sems.at[5 + n])
        copy.start()
        departures.append(copy)
    for copy in departures:
        copy.wait()


def per_device(activations, upstream, kernel_weight, patch_inverse, output_inverse):
    vmem = pl.BlockSpec(memory_space=pltpu.VMEM)
    hbm = pl.BlockSpec(memory_space=pl.ANY)
    scratch = [
        ((4, 256, 128), BF16),
        ((4, 256, 128), BF16),
        ((27, 128, 128), BF16),
        ((27, 2, 3456), F32),
        ((128, 128), F32),
        ((4, 256, 128), BF16),
        ((4, 256, 128), BF16),
        ((2, 256, 128), BF16),
        ((2, 256, 128), BF16),
        ((4, 256, 128), BF16),
        ((5, 6, 320, 128), BF16),
        ((3, 6, 288, 128), BF16),
        ((2, 128, 1536), BF16),
        ((256, 1024), BF16),
        ((128, 1024), BF16),
        ((2, 256, 128), F32),
        ((2, 32, 128, 128), F32),
        ((2, 32, 64, 128), F32),
        ((2, 32, 64, 128), BF16),
        ((2, 3, 32, 16, 128), BF16),
        ((2, 512, 128), F32),
        ((2, 4, 4, 32, 128), BF16),
        ((2, 3, 4, 32, 128), BF16),
        ((8, 32, 128), F32),
        ((7, 32, 128), F32),
        ((4, 2, 4, 128, 128), F32),
        ((4, 2, 4, 64, 128), F32),
        ((4, 2, 4, 64, 128), BF16),
        ((15, 4, 2, 16, 128), BF16),
        ((4, 2, 16, 128), F32),
        ((8, 2, 16, 128), F32),
        ((2, 4, 128, 128), F32),
        ((64, 3584), F32),
        ((2, 64, 896), F32),
        ((2, 32, 128), F32),
        ((4, 2, 32, 128), F32),
    ]
    shapes = (
        jax.ShapeDtypeStruct((4, 256, 128), BF16),
        jax.ShapeDtypeStruct((4, 256, 128), BF16),
        jax.ShapeDtypeStruct((2, 32, 63), F32),
        jax.ShapeDtypeStruct((128, 128), F32),
        jax.ShapeDtypeStruct((27, 2, 128), F32),
    )
    outs = pl.pallas_call(
        step_kernel,
        out_shape=shapes,
        in_specs=[hbm] * 5,
        out_specs=[hbm, hbm, vmem, vmem, vmem],
        scratch_shapes=[pltpu.VMEM(shape, dtype) for shape, dtype in scratch]
        + [
            pltpu.SemaphoreType.DMA((8,)),
            pltpu.SemaphoreType.DMA((128,)),
            pltpu.SemaphoreType.DMA((128,)),
        ],
        compiler_params=pltpu.CompilerParams(
            collective_id=0, has_side_effects=True, vmem_limit_bytes=60 * 1024 * 1024
        ),
        name="step_kernel",
    )(
        activations.reshape(4, 256, 128),
        upstream.reshape(4, 256, 128),
        kernel_weight,
        patch_inverse,
        output_inverse,
    )
    outs = pl.pallas_call(
        hand_on,
        out_shape=shapes,
        in_specs=[hbm] * 5,
        out_specs=[hbm] * 5,
        scratch_shapes=[pltpu.VMEM(shape.shape, shape.dtype) for shape in shapes]
        + [pltpu.SemaphoreType.DMA((10,))],
        compiler_params=pltpu.CompilerParams(vmem_limit_bytes=60 * 1024 * 1024),
        name="hand_on",
    )(*outs)
    activated, input_grad, patch_factor, output_factor, precond = outs
    return (
        activated.reshape(activations.shape),
        input_grad.reshape(activations.shape),
        jnp.transpose(patch_factor, (0, 2, 1)),
        output_factor,
        precond,
    )


def solution(mesh):
    return jax.shard_map(
        per_device,
        mesh=mesh,
        in_specs=(
            P("dp", "space", None, None, None),
            P("dp", "space", None, None, None),
            P(),
            P(None, "space", None),
            P(),
        ),
        out_specs=(
            P("dp", "space", None, None, None),
            P("dp", "space", None, None, None),
            P("space", None, "dp"),
            P(),
            P(None, "space", None),
        ),
        check_vma=False,
    )
```

```python
import functools

import jax
import jax.numpy as jnp
from jax import lax
from jax.experimental import pallas as pl
from jax.experimental.pallas import tpu as pltpu
from jax.sharding import PartitionSpec as P

F32 = jnp.float32
BF16 = jnp.bfloat16
TOTAL = 262144.0
PLANE = (10, 6, 9, 11, 14, 5, 7, 13, 15, 2, 8, 1, 3, 4, 12)
RING = (4, 3, 5, 2, 6, 1, 7)
NT = (((1,), (1,)), ((), ()))
HIGHEST = lax.Precision.HIGHEST


def dot(a, b):
    return jnp.dot(a, b, preferred_element_type=F32)


def tap_shift(offset):
    return (offset // 9 - 1, offset // 3 % 3 - 1, offset % 3 - 1)


def step_kernel(
    act_hbm,
    up_hbm,
    kw_hbm,
    pinv_hbm,
    oinv_hbm,
    activated_hbm,
    input_grad_hbm,
    patch_factor,
    output_factor,
    precond,
    act,
    up,
    kw,
    pinv,
    oinv,
    activated,
    input_grad,
    halo_a,
    halo_s,
    slope,
    ext_a,
    ext_s,
    left,
    left12,
    slope_t,
    begun,
    prod_l,
    got_lc,
    out_l1,
    got_l1,
    sum_l1,
    out_l2,
    got_l2,
    out_l3,
    got_l3,
    prod_w,
    got_wc,
    out_w1,
    got_w1,
    out_w3,
    got_w3,
    weights,
    inverse,
    inverse2,
    part_p,
    got_p,
    local_sem,
    send_sem,
    recv_sem,
):
    space = lax.axis_index("space")
    quarter = lax.axis_index("dp")
    core = lax.rem(space, 2)
    col = lax.rem(space // 2, 4)
    row = lax.rem(space // 8, 4)
    half = space // 32
    depth = half * 4 + quarter
    other = 1 - core

    def device(half, row, col, core, quarter):
        return {"space": ((half * 4 + row) * 4 + col) * 2 + core, "dp": quarter}

    sibling = device(half, row, col, other, quarter)
    following = {"space": lax.rem(space + 1, 64), "dp": quarter}
    preceding = {"space": lax.rem(space + 63, 64), "dp": quarter}
    far = {"space": lax.rem(space + 2 * core + 63, 64), "dp": quarter}

    def along_x(t):
        at = lax.rem(col + t, 4)
        return at, device(half, row, at, core, quarter)

    def along_y(t):
        at = lax.rem(row + t, 4)
        return at, device(half, at, col, core, quarter)

    def in_plane(t):
        at_y = lax.rem(row + t // 4, 4)
        at_x = lax.rem(col + t % 4, 4)
        return at_y, at_x, device(half, at_y, at_x, core, quarter)

    def along_z(t):
        at = lax.rem(depth + t, 8)
        return at, device(at // 4, row, col, core, lax.rem(at, 4))

    def along_dp(t, which):
        return device(half, row, col, which, lax.rem(quarter + t, 4))

    def sixteen(at):
        return pl.ds(pl.multiple_of(at * 16, 16), 16)

    count = [0, 0]
    sent = []

    def send(src, dst, to):
        n = count[0]
        count[0] += 1
        copy = pltpu.make_async_remote_copy(
            src_ref=src,
            dst_ref=dst,
            send_sem=send_sem.at[n],
            recv_sem=recv_sem.at[n],
            device_id=to,
            device_id_type=pl.DeviceIdType.MESH,
        )
        copy.start()
        sent.append(copy)
        return copy

    settled = [0]

    def settle(upto):
        for copy in sent[settled[0] : upto]:
            copy.wait_send()
        settled[0] = upto

    def move(src, dst):
        n = count[1]
        count[1] += 1
        copy = pltpu.make_async_copy(src, dst, local_sem.at[n])
        copy.start()
        return copy

    partners = [far]
    partners += [along_z(t)[1] for t in RING]
    partners += [in_plane(t)[2] for t in PLANE]
    partners += [along_dp(t, other) for t in (3, 1, 2)]
    partners += [sibling]
    barrier = pltpu.get_barrier_semaphore()
    for partner in partners:
        pl.semaphore_signal(
            barrier, inc=1, device_id=partner, device_id_type=pl.DeviceIdType.MESH
        )

    act_in = move(act_hbm, act)
    kw_in = move(kw_hbm, kw)
    up_in = move(up_hbm, up)
    pinv_in = move(pinv_hbm, pinv)
    oinv_in = move(oinv_hbm, oinv)

    r = lax.broadcasted_iota(jnp.int32, (128, 128), 0)
    c = lax.broadcasted_iota(jnp.int32, (128, 128), 1)

    def picked(first, second):
        chan = (
            (r & 1)
            + 2 * ((r >> 6) & 1)
            + first * ((r >> 4) & 3)
            + second * ((r >> 2) & 3)
            + 64 * ((r >> 1) & 1)
        )
        return jnp.where(c == chan, 1.0, 0.0).astype(BF16)

    orders = (picked(4, 16), picked(16, 4))
    unit = jnp.where(c == r, 1.0, 0.0).astype(BF16)

    def turned(order, plane):
        return lax.dot_general(order, plane, NT, preferred_element_type=F32).astype(BF16)

    def place_a(plane, at, shifts):
        wide = plane.astype(F32).reshape(16, 16, 128)
        for dx in shifts:
            moved = plane
            if dx:
                moved = pltpu.roll(wide, (-dx) % 16, 1).reshape(256, 128).astype(BF16)
            ext_a[dx + 2, at, 32:288, :] = moved
            ext_a[dx + 2, at, 0:32, :] = moved[224:256]
            ext_a[dx + 2, at, 288:320, :] = moved[0:32]

    def turn_a(plane, at):
        for part in range(2):
            left[part, :, at * 256 : (at + 1) * 256] = turned(orders[part], plane)

    def place_s(plane, at):
        wide = plane.astype(F32).reshape(16, 16, 128)
        for dx in range(-1, 2):
            moved = plane
            if dx:
                moved = pltpu.roll(wide, (-dx) % 16, 1).reshape(256, 128).astype(BF16)
            ext_s[dx + 1, at, 16:272, :] = moved
            ext_s[dx + 1, at, 0:16, :] = moved[240:256]
            ext_s[dx + 1, at, 272:288, :] = moved[0:16]

    def rows_a(first, dy, dx, planes=4):
        return ext_a[
            dx + 2, first : first + planes, (2 + dy) * 16 : (2 + dy) * 16 + 256, :
        ].reshape(planes * 256, 128)

    def ends_a(dz, dy, dx):
        return jnp.concatenate([rows_a(1 + dz, dy, dx, 1), rows_a(4 + dz, dy, dx, 1)], axis=0)

    prod_l[1, 31] = jnp.zeros((128, 128), F32)
    prod_w[3, 1, 2] = jnp.zeros((128, 128), F32)
    inverse[:, 3456:3584] = jnp.zeros((64, 128), F32)
    inverse[48:64, :] = jnp.zeros((16, 3584), F32)

    act_in.wait()
    for z in range(4):
        place_a(act[z], z + 1, (-2, -1, 0, 1, 2))
        turn_a(act[z], z + 1)
    for k in range(13):
        m = k + 62
        part, slot = (0, 25 + k) if k < 7 else (1, 18 + k)
        prod_l[part, slot] = dot(
            left[part, :, 256:1280], rows_a(1, m // 5 % 5 - 2, m % 5 - 2)
        )

    pl.semaphore_wait(barrier, len(partners))
    before = send(act.at[3], halo_a.at[0], following)
    after = send(act.at[0], halo_a.at[1], preceding)

    def taps_sum(z, depths):
        taps = []
        for dz in depths:
            for o in range(9):
                dy, dx = o // 3 - 1, o % 3 - 1
                first = (2 + dy) * 16
                taps.append(ext_a[dx + 2, z + 1 + dz, first : first + 256, :])
        matrix = kw[9 * depths[0] + 9 : 9 * depths[-1] + 18].reshape(len(taps) * 128, 128)
        return dot(jnp.concatenate(taps, axis=1), matrix)

    def forward(z, pre):
        logistic = jax.nn.sigmoid(pre)
        activated[z] = (pre * logistic).astype(BF16)
        sloped = (up[z].astype(F32) * logistic * (1.0 + pre * (1.0 - logistic))).astype(BF16)
        slope[z] = sloped
        slope_t[:, z * 256 : (z + 1) * 256] = turned(unit, sloped)

    theirs = pl.ds(pl.multiple_of(other * 64, 64), 64)
    mine = pl.ds(pl.multiple_of(core * 64, 64), 64)
    firsts = (col, row)
    seconds = (row, col)
    first_axis = (along_x, along_y)
    second_axis = (along_y, along_x)

    def swap_l(first, last):
        return send(
            prod_l.at[:, first:last, theirs, :], got_lc.at[:, first:last], sibling
        )

    def spread_l(first, last):
        copies = []
        for part in range(2):
            out_l1[part, first:last] = (
                prod_l[part, first:last, mine, :] + got_lc[part, first:last]
            ).astype(BF16)
            for t in (2, 1, 3):
                at, to = first_axis[part](t)
                copies.append(
                    send(
                        out_l1.at[part, first:last, sixteen(at), :],
                        got_l1.at[part, t - 1, first:last],
                        to,
                    )
                )
        return copies

    early_c = swap_l(25, 32)
    kw_in.wait()
    up_in.wait()
    forward(1, taps_sum(1, (-1, 0, 1)))
    forward(2, taps_sum(2, (-1, 0, 1)))
    begun[0] = taps_sum(0, (0, 1))
    begun[1] = taps_sum(3, (-1, 0))

    def blocks(d):
        for b in range(7):
            if 7 * d + b < 27:
                yield b, tap_shift(7 * d + b)

    inner_t = slope_t[:, 256:768]
    for d in range(4):
        for b, (dz, dy, dx) in blocks(d):
            prod_w[d, b // 4, b % 4] = dot(inner_t, rows_a(2 + dz, dy, dx, 2))
    inner_own = dot(inner_t, slope[1:3].reshape(512, 128))

    early_c.wait_recv()
    l1 = spread_l(25, 32)

    pinv_in.wait()
    for o in range(27):
        inverse[2 * o : 2 * o + 2, 0:3456] = pinv[o]
    inverse2[core] = inverse[:, pl.ds(pl.multiple_of(quarter * 896, 128), 896)]
    rows_in = send(inverse2.at[core], inverse2.at[core], sibling)

    before.wait_recv()
    place_a(halo_a[0], 0, (-1, 0, 1))
    after.wait_recv()
    place_a(halo_a[1], 5, (-1, 0, 1))
    forward(3, begun[1] + taps_sum(3, (1,)))
    forward(0, begun[0] + taps_sum(0, (-1,)))
    before_s = send(slope.at[3], halo_s.at[0], following)
    after_s = send(slope.at[0], halo_s.at[1], preceding)
    activated_out = move(activated, activated_hbm)

    outer_t = jnp.concatenate([slope_t[:, 0:256], slope_t[:, 768:1024]], axis=1)
    own = inner_own + dot(outer_t, jnp.concatenate([slope[0], slope[3]], axis=0))
    wc = []
    for d in range(4):
        prod_w[d, 1, 3] = own
        for b, (dz, dy, dx) in blocks(d):
            prod_w[d, b // 4, b % 4] += dot(outer_t, ends_a(dz, dy, dx))
        wc.append(send(prod_w.at[d, :, :, theirs, :], got_wc.at[d], sibling))

    turn_a(halo_a[0], 0)
    place_a(halo_a[1], 5, (-2, 2))
    left12[0:128, :] = left[0, :, 256:1280]
    left12[128:256, :] = left[1, :, 0:1024]
    pairs = [(dy, dx) for dy in range(-2, 3) for dx in range(-2, 3)]

    def lag_block(first, last):
        for s in range(first, last):
            both = dot(left12[...], rows_a(2, *pairs[s]))
            prod_l[0, s] = both[0:128]
            prod_l[1, s] = both[128:256]
        return swap_l(first, last)

    w1 = []

    def spread_w(first, last):
        for copy in wc[first:last]:
            copy.wait_recv()
        out_w1[first:last] = (prod_w[first:last, :, :, mine, :] + got_wc[first:last]).astype(BF16)
        for t in PLANE:
            at_y, at_x, to = in_plane(t)
            w1.append(
                send(
                    out_w1.at[first:last, :, at_y, sixteen(at_x), :],
                    got_w1.at[t - 1, first:last],
                    to,
                )
            )

    spread_w(0, 2)
    lc = [lag_block(0, 6)]
    spread_w(2, 4)
    lc.append(lag_block(6, 13))
    lc.append(lag_block(13, 25))
    spread_from = len(sent)
    lc[0].wait_recv()
    lc[1].wait_recv()
    l1 += spread_l(0, 13)
    lc[2].wait_recv()
    l1 += spread_l(13, 25)

    for z in range(4):
        place_s(slope[z], z + 1)
    before_s.wait_recv()
    after_s.wait_recv()
    place_s(halo_s[0], 0)
    place_s(halo_s[1], 5)

    kernel_cols = jnp.concatenate([kw[o] for o in range(27)], axis=1)

    def back(z):
        taps = []
        for o in range(27):
            dz, dy, dx = tap_shift(o)
            taps.append(ext_s[1 - dx, z + 1 - dz, (1 - dy) * 16 : (1 - dy) * 16 + 256, :])
        grad = lax.dot_general(
            jnp.concatenate(taps, axis=1), kernel_cols, NT, preferred_element_type=F32
        )
        input_grad[z] = grad.astype(BF16)

    back(0)

    settle(spread_from)
    tall = sixteen(core * 4 + col)
    for n in range(2):
        for copy in w1[15 * n : 15 * n + 15]:
            copy.wait_recv()
        two = slice(2 * n, 2 * n + 2)
        total_w = prod_w[two, :, row, tall, :] + got_wc[two, :, row, sixteen(col), :]
        for t in range(15):
            total_w = total_w + got_w1[t, two].astype(F32)
        out_w3[two] = total_w
    got_w3[depth] = out_w3[quarter]
    z_from = len(sent)
    w3 = []
    for t in RING:
        at, to = along_z(t)
        w3.append(send(out_w3.at[lax.rem(at, 4)], got_w3.at[depth], to))

    back(1)

    for copy in l1:
        copy.wait_recv()
    l2 = []
    for part in range(2):
        kept = sixteen(firsts[part])
        high = sixteen(core * 4 + firsts[part])
        total = prod_l[part, :, high, :] + got_lc[part, :, kept, :]
        for t in range(3):
            total = total + got_l1[part, t].astype(F32)
        sum_l1[part] = total.reshape(512, 128)
        for b in range(4):
            for n in range(4):
                groups = [
                    sum_l1[part, pl.ds(4 * b + n + 128 * g, 8, stride=16), :] for g in range(4)
                ]
                out_l2[part, b, n] = jnp.concatenate(groups, axis=0).astype(BF16)
        for t in (2, 1, 3):
            at, to = second_axis[part](t)
            l2.append(send(out_l2.at[part, at], got_l2.at[part, t - 1], to))

    back(2)

    settle(z_from)
    for copy in w3:
        copy.wait_recv()
    reduced = got_w3[0]
    for z in range(1, 8):
        reduced = reduced + got_w3[z]
    weights[:, row, tall, :] = reduced
    gather_from = len(sent)
    g1 = []
    for t in PLANE:
        piece = weights.at[:, row, tall, :]
        g1.append(send(piece, piece, in_plane(t)[2]))

    back(3)
    input_grad_out = move(input_grad, input_grad_hbm)

    for copy in l2:
        copy.wait_recv()
    group = c[0:32] // 32
    totals = []
    for part in range(2):
        total = out_l2[part, seconds[part]].astype(F32)
        for t in range(3):
            total = total + got_l2[part, t].astype(F32)
        totals.append(total)
    for h in range(2):
        groups = [totals[part][2 * h + i] for part in range(2) for i in range(2)]
        for q in range(4):
            packed = jnp.zeros((32, 128), F32)
            for j in range(4):
                shift = (32 * (j - q)) % 128
                piece = pltpu.roll(groups[j], shift, 1) if shift else groups[j]
                packed = jnp.where(group == j, piece, packed)
            out_l3[4 * h + q] = packed
    l3 = []
    for t in RING:
        at, to = along_z(t)
        l3.append(send(out_l3.at[at], got_l3.at[t - 1], to))

    settle(gather_from)
    for copy in g1:
        copy.wait_recv()
    own_in = send(weights.at[1, 3, mine, :], weights.at[1, 3, mine, :], sibling)
    rows_in.wait_recv()
    gathered = jnp.concatenate([weights[b // 4, b % 4, mine, :] for b in range(7)], axis=1)
    blank = jnp.zeros((64, 896), F32)
    packed_p = jnp.zeros((64, 128), F32)
    for n in range(2):
        packed_p += lax.dot_general(
            inverse2[:, 32 * n : 32 * n + 32, :].reshape(64, 896),
            jnp.concatenate([gathered, blank] if n == 0 else [blank, gathered], axis=0),
            NT,
            preferred_element_type=F32,
            precision=HIGHEST,
        )
    part_p[...] = packed_p.reshape(2, 32, 128)
    got_p[quarter, core] = part_p[core]
    last_from = len(sent)
    pp = [send(part_p.at[other], got_p.at[quarter, core], sibling)]
    for t in (3, 1, 2):
        for which in (core, other):
            pp.append(send(part_p.at[which], got_p.at[quarter, core], along_dp(t, which)))
    own_in.wait_recv()
    output_factor[...] = weights[1, 3] * (1.0 / TOTAL)

    for copy in l3:
        copy.wait_recv()
    final = out_l3[depth]
    for t in range(7):
        final = final + got_l3[t]
    final = final * (1.0 / TOTAL)
    flipped = jnp.concatenate([final, jnp.zeros((96, 128), F32)], axis=0).T
    lane = c[0:32]
    for i in range(2):
        one = flipped[32 * i : 32 * i + 32]
        two = flipped[64 + 32 * i : 96 + 32 * i]
        piece = jnp.where(lane < 7, pltpu.roll(one, 103, 1), pltpu.roll(two, 110, 1))
        piece = jnp.where(lane < 13, piece, pltpu.roll(one, 13, 1))
        piece = jnp.where(lane < 38, piece, pltpu.roll(two, 38, 1))
        patch_factor[i] = piece[:, 0:63]

    oinv_in.wait()
    settle(last_from)
    for copy in pp:
        copy.wait_recv()
    products = [jnp.zeros((32, 128), F32), jnp.zeros((32, 128), F32)]
    empty = jnp.zeros((64, 128), F32)
    for which in range(2):
        piece = got_p[0, which] + got_p[1, which] + got_p[2, which] + got_p[3, which]
        factor = oinv[64 * which : 64 * which + 64, :]
        for n in range(2):
            products[n] += jnp.dot(
                piece,
                jnp.concatenate([factor, empty] if n == 0 else [empty, factor], axis=0),
                preferred_element_type=F32,
                precision=HIGHEST,
            )
    product = jnp.concatenate(products, axis=0) * (1.0 / TOTAL)
    for o in range(27):
        precond[o] = product[2 * o : 2 * o + 2]

    activated_out.wait()
    input_grad_out.wait()
    settle(len(sent))


def hand_on(*refs):
    sources, results, stops, sems = refs[:5], refs[5:10], refs[10:15], refs[15]
    arrivals = []
    for n in range(5):
        copy = pltpu.make_async_copy(sources[n], stops[n], sems.at[n])
        copy.start()
        arrivals.append(copy)
    departures = []
    for n in range(5):
        arrivals[n].wait()
        copy = pltpu.make_async_copy(stops[n], results[n], sems.at[5 + n])
        copy.start()
        departures.append(copy)
    for copy in departures:
        copy.wait()


def per_device(activations, upstream, kernel_weight, patch_inverse, output_inverse):
    vmem = pl.BlockSpec(memory_space=pltpu.VMEM)
    hbm = pl.BlockSpec(memory_space=pl.ANY)
    scratch = [
        ((4, 256, 128), BF16),
        ((4, 256, 128), BF16),
        ((27, 128, 128), BF16),
        ((27, 2, 3456), F32),
        ((128, 128), F32),
        ((4, 256, 128), BF16),
        ((4, 256, 128), BF16),
        ((2, 256, 128), BF16),
        ((2, 256, 128), BF16),
        ((4, 256, 128), BF16),
        ((5, 6, 320, 128), BF16),
        ((3, 6, 288, 128), BF16),
        ((2, 128, 1536), BF16),
        ((256, 1024), BF16),
        ((128, 1024), BF16),
        ((2, 256, 128), F32),
        ((2, 32, 128, 128), F32),
        ((2, 32, 64, 128), F32),
        ((2, 32, 64, 128), BF16),
        ((2, 3, 32, 16, 128), BF16),
        ((2, 512, 128), F32),
        ((2, 4, 4, 32, 128), BF16),
        ((2, 3, 4, 32, 128), BF16),
        ((8, 32, 128), F32),
        ((7, 32, 128), F32),
        ((4, 2, 4, 128, 128), F32),
        ((4, 2, 4, 64, 128), F32),
        ((4, 2, 4, 64, 128), BF16),
        ((15, 4, 2, 16, 128), BF16),
        ((4, 2, 16, 128), F32),
        ((8, 2, 16, 128), F32),
        ((2, 4, 128, 128), F32),
        ((64, 3584), F32),
        ((2, 64, 896), F32),
        ((2, 32, 128), F32),
        ((4, 2, 32, 128), F32),
    ]
    shapes = (
        jax.ShapeDtypeStruct((4, 256, 128), BF16),
        jax.ShapeDtypeStruct((4, 256, 128), BF16),
        jax.ShapeDtypeStruct((2, 32, 63), F32),
        jax.ShapeDtypeStruct((128, 128), F32),
        jax.ShapeDtypeStruct((27, 2, 128), F32),
    )
    outs = pl.pallas_call(
        step_kernel,
        out_shape=shapes,
        in_specs=[hbm] * 5,
        out_specs=[hbm, hbm, vmem, vmem, vmem],
        scratch_shapes=[pltpu.VMEM(shape, dtype) for shape, dtype in scratch]
        + [
            pltpu.SemaphoreType.DMA((8,)),
            pltpu.SemaphoreType.DMA((128,)),
            pltpu.SemaphoreType.DMA((128,)),
        ],
        compiler_params=pltpu.CompilerParams(
            collective_id=0, has_side_effects=True, vmem_limit_bytes=60 * 1024 * 1024
        ),
        name="step_kernel",
    )(
        activations.reshape(4, 256, 128),
        upstream.reshape(4, 256, 128),
        kernel_weight,
        patch_inverse,
        output_inverse,
    )
    outs = pl.pallas_call(
        hand_on,
        out_shape=shapes,
        in_specs=[hbm] * 5,
        out_specs=[hbm] * 5,
        scratch_shapes=[pltpu.VMEM(shape.shape, shape.dtype) for shape in shapes]
        + [pltpu.SemaphoreType.DMA((10,))],
        compiler_params=pltpu.CompilerParams(vmem_limit_bytes=60 * 1024 * 1024),
        name="hand_on",
    )(*outs)
    activated, input_grad, patch_factor, output_factor, precond = outs
    return (
        activated.reshape(activations.shape),
        input_grad.reshape(activations.shape),
        jnp.transpose(patch_factor, (0, 2, 1)),
        output_factor,
        precond,
    )


def solution(mesh):
    return jax.shard_map(
        per_device,
        mesh=mesh,
        in_specs=(
            P("dp", "space", None, None, None),
            P("dp", "space", None, None, None),
            P(),
            P(None, "space", None),
            P(),
        ),
        out_specs=(
            P("dp", "space", None, None, None),
            P("dp", "space", None, None, None),
            P("space", None, "dp"),
            P(),
            P(None, "space", None),
        ),
        check_vma=False,
    )
```

```python
import functools

import jax
import jax.numpy as jnp
from jax import lax
from jax.experimental import pallas as pl
from jax.experimental.pallas import tpu as pltpu
from jax.sharding import PartitionSpec as P

F32 = jnp.float32
BF16 = jnp.bfloat16
TOTAL = 262144.0
PLANE = (10, 6, 9, 11, 14, 5, 7, 13, 15, 2, 8, 1, 3, 4, 12)
RING = (4, 3, 5, 2, 6, 1, 7)
NT = (((1,), (1,)), ((), ()))
HIGHEST = lax.Precision.HIGHEST


def dot(a, b):
    return jnp.dot(a, b, preferred_element_type=F32)


def tap_shift(offset):
    return (offset // 9 - 1, offset // 3 % 3 - 1, offset % 3 - 1)


def step_kernel(
    act_hbm,
    up_hbm,
    kw_hbm,
    pinv_hbm,
    oinv_hbm,
    activated_hbm,
    input_grad_hbm,
    patch_factor,
    output_factor,
    precond,
    act,
    up,
    kw,
    pinv,
    oinv,
    activated,
    input_grad,
    halo_a,
    halo_s,
    slope,
    ext_a,
    ext_s,
    left,
    left12,
    slope_t,
    begun,
    prod_l,
    got_lc,
    out_l1,
    got_l1,
    sum_l1,
    out_l2,
    got_l2,
    out_l3,
    got_l3,
    prod_w,
    got_wc,
    out_w1,
    got_w1,
    out_w3,
    got_w3,
    weights,
    inverse,
    inverse2,
    parts2,
    part_p,
    got_p,
    local_sem,
    send_sem,
    recv_sem,
):
    space = lax.axis_index("space")
    quarter = lax.axis_index("dp")
    core = lax.rem(space, 2)
    col = lax.rem(space // 2, 4)
    row = lax.rem(space // 8, 4)
    half = space // 32
    depth = half * 4 + quarter
    other = 1 - core

    def device(half, row, col, core, quarter):
        return {"space": ((half * 4 + row) * 4 + col) * 2 + core, "dp": quarter}

    sibling = device(half, row, col, other, quarter)
    following = {"space": lax.rem(space + 1, 64), "dp": quarter}
    preceding = {"space": lax.rem(space + 63, 64), "dp": quarter}
    far = {"space": lax.rem(space + 2 * core + 63, 64), "dp": quarter}

    def along_x(t):
        at = lax.rem(col + t, 4)
        return at, device(half, row, at, core, quarter)

    def along_y(t):
        at = lax.rem(row + t, 4)
        return at, device(half, at, col, core, quarter)

    def in_plane(t):
        at_y = lax.rem(row + t // 4, 4)
        at_x = lax.rem(col + t % 4, 4)
        return at_y, at_x, device(half, at_y, at_x, core, quarter)

    def along_z(t):
        at = lax.rem(depth + t, 8)
        return at, device(at // 4, row, col, core, lax.rem(at, 4))

    def along_dp(t, which):
        return device(half, row, col, which, lax.rem(quarter + t, 4))

    def sixteen(at):
        return pl.ds(pl.multiple_of(at * 16, 16), 16)

    count = [0, 0]
    sent = []

    def send(src, dst, to):
        n = count[0]
        count[0] += 1
        copy = pltpu.make_async_remote_copy(
            src_ref=src,
            dst_ref=dst,
            send_sem=send_sem.at[n],
            recv_sem=recv_sem.at[n],
            device_id=to,
            device_id_type=pl.DeviceIdType.MESH,
        )
        copy.start()
        sent.append(copy)
        return copy

    settled = [0]

    def settle(upto):
        for copy in sent[settled[0] : upto]:
            copy.wait_send()
        settled[0] = upto

    def move(src, dst):
        n = count[1]
        count[1] += 1
        copy = pltpu.make_async_copy(src, dst, local_sem.at[n])
        copy.start()
        return copy

    partners = [far]
    partners += [along_z(t)[1] for t in RING]
    partners += [in_plane(t)[2] for t in PLANE]
    partners += [along_dp(t, other) for t in (3, 1, 2)]
    partners += [sibling]
    barrier = pltpu.get_barrier_semaphore()
    for partner in partners:
        pl.semaphore_signal(
            barrier, inc=1, device_id=partner, device_id_type=pl.DeviceIdType.MESH
        )

    act_in = move(act_hbm, act)
    kw_in = move(kw_hbm, kw)
    up_in = move(up_hbm, up)
    pinv_in = move(pinv_hbm, pinv)
    oinv_in = move(oinv_hbm, oinv)

    r = lax.broadcasted_iota(jnp.int32, (128, 128), 0)
    c = lax.broadcasted_iota(jnp.int32, (128, 128), 1)

    def picked(first, second):
        chan = (
            (r & 1)
            + 2 * ((r >> 6) & 1)
            + first * ((r >> 4) & 3)
            + second * ((r >> 2) & 3)
            + 64 * ((r >> 1) & 1)
        )
        return jnp.where(c == chan, 1.0, 0.0).astype(BF16)

    orders = (picked(4, 16), picked(16, 4))
    unit = jnp.where(c == r, 1.0, 0.0).astype(BF16)

    def turned(order, plane):
        return lax.dot_general(order, plane, NT, preferred_element_type=F32).astype(BF16)

    def place_a(plane, at, shifts):
        wide = plane.astype(F32).reshape(16, 16, 128)
        for dx in shifts:
            moved = plane
            if dx:
                moved = pltpu.roll(wide, (-dx) % 16, 1).reshape(256, 128).astype(BF16)
            ext_a[dx + 2, at, 32:288, :] = moved
            ext_a[dx + 2, at, 0:32, :] = moved[224:256]
            ext_a[dx + 2, at, 288:320, :] = moved[0:32]

    def turn_a(plane, at):
        for part in range(2):
            left[part, :, at * 256 : (at + 1) * 256] = turned(orders[part], plane)

    def place_s(plane, at):
        wide = plane.astype(F32).reshape(16, 16, 128)
        for dx in range(-1, 2):
            moved = plane
            if dx:
                moved = pltpu.roll(wide, (-dx) % 16, 1).reshape(256, 128).astype(BF16)
            ext_s[dx + 1, at, 16:272, :] = moved
            ext_s[dx + 1, at, 0:16, :] = moved[240:256]
            ext_s[dx + 1, at, 272:288, :] = moved[0:16]

    def rows_a(first, dy, dx, planes=4):
        return ext_a[
            dx + 2, first : first + planes, (2 + dy) * 16 : (2 + dy) * 16 + 256, :
        ].reshape(planes * 256, 128)

    def ends_a(dz, dy, dx):
        return jnp.concatenate([rows_a(1 + dz, dy, dx, 1), rows_a(4 + dz, dy, dx, 1)], axis=0)

    prod_l[1, 31] = jnp.zeros((128, 128), F32)
    prod_w[3, 1, 2] = jnp.zeros((128, 128), F32)
    inverse[:, 3456:3584] = jnp.zeros((64, 128), F32)
    inverse[48:64, :] = jnp.zeros((16, 3584), F32)

    act_in.wait()
    for z in range(4):
        place_a(act[z], z + 1, (-2, -1, 0, 1, 2))
        turn_a(act[z], z + 1)
    for k in range(13):
        m = k + 62
        part, slot = (0, 25 + k) if k < 7 else (1, 18 + k)
        prod_l[part, slot] = dot(
            left[part, :, 256:1280], rows_a(1, m // 5 % 5 - 2, m % 5 - 2)
        )

    pl.semaphore_wait(barrier, len(partners))
    before = send(act.at[3], halo_a.at[0], following)
    after = send(act.at[0], halo_a.at[1], preceding)

    def taps_sum(z, depths):
        taps = []
        for dz in depths:
            for o in range(9):
                dy, dx = o // 3 - 1, o % 3 - 1
                first = (2 + dy) * 16
                taps.append(ext_a[dx + 2, z + 1 + dz, first : first + 256, :])
        matrix = kw[9 * depths[0] + 9 : 9 * depths[-1] + 18].reshape(len(taps) * 128, 128)
        return dot(jnp.concatenate(taps, axis=1), matrix)

    def forward(z, pre):
        logistic = jax.nn.sigmoid(pre)
        activated[z] = (pre * logistic).astype(BF16)
        sloped = (up[z].astype(F32) * logistic * (1.0 + pre * (1.0 - logistic))).astype(BF16)
        slope[z] = sloped
        slope_t[:, z * 256 : (z + 1) * 256] = turned(unit, sloped)

    theirs = pl.ds(pl.multiple_of(other * 64, 64), 64)
    mine = pl.ds(pl.multiple_of(core * 64, 64), 64)
    firsts = (col, row)
    seconds = (row, col)
    first_axis = (along_x, along_y)
    second_axis = (along_y, along_x)

    def swap_l(first, last):
        return send(
            prod_l.at[:, first:last, theirs, :], got_lc.at[:, first:last], sibling
        )

    def spread_l(first, last):
        copies = []
        for part in range(2):
            out_l1[part, first:last] = (
                prod_l[part, first:last, mine, :] + got_lc[part, first:last]
            ).astype(BF16)
            for t in (2, 1, 3):
                at, to = first_axis[part](t)
                copies.append(
                    send(
                        out_l1.at[part, first:last, sixteen(at), :],
                        got_l1.at[part, t - 1, first:last],
                        to,
                    )
                )
        return copies

    early_c = swap_l(25, 32)
    kw_in.wait()
    up_in.wait()
    forward(1, taps_sum(1, (-1, 0, 1)))
    forward(2, taps_sum(2, (-1, 0, 1)))
    begun[0] = taps_sum(0, (0, 1))
    begun[1] = taps_sum(3, (-1, 0))

    def blocks(d):
        for b in range(7):
            if 7 * d + b < 27:
                yield b, tap_shift(7 * d + b)

    inner_t = slope_t[:, 256:768]
    for d in range(4):
        for b, (dz, dy, dx) in blocks(d):
            prod_w[d, b // 4, b % 4] = dot(inner_t, rows_a(2 + dz, dy, dx, 2))
    inner_own = dot(inner_t, slope[1:3].reshape(512, 128))

    early_c.wait_recv()
    l1 = spread_l(25, 32)

    pinv_in.wait()
    for o in range(27):
        inverse[2 * o : 2 * o + 2, 0:3456] = pinv[o]
    inverse2[core] = inverse[:, pl.ds(pl.multiple_of(quarter * 896, 128), 896)]
    rows_in = send(inverse2.at[core], inverse2.at[core], sibling)

    before.wait_recv()
    place_a(halo_a[0], 0, (-1, 0, 1))
    after.wait_recv()
    place_a(halo_a[1], 5, (-1, 0, 1))
    forward(3, begun[1] + taps_sum(3, (1,)))
    forward(0, begun[0] + taps_sum(0, (-1,)))
    before_s = send(slope.at[3], halo_s.at[0], following)
    after_s = send(slope.at[0], halo_s.at[1], preceding)
    activated_out = move(activated, activated_hbm)

    outer_t = jnp.concatenate([slope_t[:, 0:256], slope_t[:, 768:1024]], axis=1)
    own = inner_own + dot(outer_t, jnp.concatenate([slope[0], slope[3]], axis=0))
    wc = []
    for d in range(4):
        prod_w[d, 1, 3] = own
        ends = jnp.concatenate([ends_a(*shift) for _, shift in blocks(d)], axis=1)
        wide = dot(outer_t, ends)
        for b, _ in blocks(d):
            prod_w[d, b // 4, b % 4] += wide[:, 128 * b : 128 * b + 128]
        wc.append(send(prod_w.at[d, :, :, theirs, :], got_wc.at[d], sibling))

    turn_a(halo_a[0], 0)
    place_a(halo_a[1], 5, (-2, 2))
    left12[0:128, :] = left[0, :, 256:1280]
    left12[128:256, :] = left[1, :, 0:1024]
    pairs = [(dy, dx) for dy in range(-2, 3) for dx in range(-2, 3)]

    def lag_block(first, last):
        for s in range(first, last):
            both = dot(left12[...], rows_a(2, *pairs[s]))
            prod_l[0, s] = both[0:128]
            prod_l[1, s] = both[128:256]
        return swap_l(first, last)

    w1 = []

    def spread_w(first, last):
        for copy in wc[first:last]:
            copy.wait_recv()
        out_w1[first:last] = (prod_w[first:last, :, :, mine, :] + got_wc[first:last]).astype(BF16)
        for t in PLANE:
            at_y, at_x, to = in_plane(t)
            w1.append(
                send(
                    out_w1.at[first:last, :, at_y, sixteen(at_x), :],
                    got_w1.at[t - 1, first:last],
                    to,
                )
            )

    spread_w(0, 2)
    lc = [lag_block(0, 6)]
    spread_w(2, 4)
    lc.append(lag_block(6, 13))
    lc.append(lag_block(13, 25))
    spread_from = len(sent)
    lc[0].wait_recv()
    lc[1].wait_recv()
    l1 += spread_l(0, 13)
    lc[2].wait_recv()
    l1 += spread_l(13, 25)

    for z in range(4):
        place_s(slope[z], z + 1)
    before_s.wait_recv()
    after_s.wait_recv()
    place_s(halo_s[0], 0)
    place_s(halo_s[1], 5)

    kernel_cols = jnp.concatenate([kw[o] for o in range(27)], axis=1)

    def back(z):
        taps = []
        for o in range(27):
            dz, dy, dx = tap_shift(o)
            taps.append(ext_s[1 - dx, z + 1 - dz, (1 - dy) * 16 : (1 - dy) * 16 + 256, :])
        grad = lax.dot_general(
            jnp.concatenate(taps, axis=1), kernel_cols, NT, preferred_element_type=F32
        )
        input_grad[z] = grad.astype(BF16)

    back(0)

    rows_in.wait_recv()
    both_rows = inverse2[...].reshape(128, 896)
    rows_high = both_rows.astype(BF16)
    parts2[0:128, :] = rows_high
    parts2[128:256, :] = (both_rows - rows_high.astype(F32)).astype(BF16)
    settle(spread_from)
    tall = sixteen(core * 4 + col)
    for n in range(2):
        for copy in w1[15 * n : 15 * n + 15]:
            copy.wait_recv()
        two = slice(2 * n, 2 * n + 2)
        total_w = prod_w[two, :, row, tall, :] + got_wc[two, :, row, sixteen(col), :]
        for t in range(15):
            total_w = total_w + got_w1[t, two].astype(F32)
        out_w3[two] = total_w
    got_w3[depth] = out_w3[quarter]
    z_from = len(sent)
    w3 = []
    for t in RING:
        at, to = along_z(t)
        w3.append(send(out_w3.at[lax.rem(at, 4)], got_w3.at[depth], to))

    back(1)

    for copy in l1:
        copy.wait_recv()
    l2 = []
    for part in range(2):
        kept = sixteen(firsts[part])
        high = sixteen(core * 4 + firsts[part])
        total = prod_l[part, :, high, :] + got_lc[part, :, kept, :]
        for t in range(3):
            total = total + got_l1[part, t].astype(F32)
        sum_l1[part] = total.reshape(512, 128)
        for b in range(4):
            for n in range(4):
                groups = [
                    sum_l1[part, pl.ds(4 * b + n + 128 * g, 8, stride=16), :] for g in range(4)
                ]
                out_l2[part, b, n] = jnp.concatenate(groups, axis=0).astype(BF16)
        for t in (2, 1, 3):
            at, to = second_axis[part](t)
            l2.append(send(out_l2.at[part, at], got_l2.at[part, t - 1], to))

    back(2)

    settle(z_from)
    for copy in w3:
        copy.wait_recv()
    reduced = got_w3[0]
    for z in range(1, 8):
        reduced = reduced + got_w3[z]
    weights[:, row, tall, :] = reduced
    gather_from = len(sent)
    g1 = []
    for t in PLANE:
        piece = weights.at[:, row, tall, :]
        g1.append(send(piece, piece, in_plane(t)[2]))

    back(3)
    input_grad_out = move(input_grad, input_grad_hbm)

    for copy in l2:
        copy.wait_recv()
    group = c[0:32] // 32
    totals = []
    for part in range(2):
        total = out_l2[part, seconds[part]].astype(F32)
        for t in range(3):
            total = total + got_l2[part, t].astype(F32)
        totals.append(total)
    for h in range(2):
        groups = [totals[part][2 * h + i] for part in range(2) for i in range(2)]
        for q in range(4):
            packed = jnp.zeros((32, 128), F32)
            for j in range(4):
                shift = (32 * (j - q)) % 128
                piece = pltpu.roll(groups[j], shift, 1) if shift else groups[j]
                packed = jnp.where(group == j, piece, packed)
            out_l3[4 * h + q] = packed
    l3 = []
    for t in RING:
        at, to = along_z(t)
        l3.append(send(out_l3.at[at], got_l3.at[t - 1], to))

    settle(gather_from)
    for copy in g1:
        copy.wait_recv()
    own_in = send(weights.at[1, 3, mine, :], weights.at[1, 3, mine, :], sibling)
    gathered = jnp.concatenate([weights[b // 4, b % 4, mine, :] for b in range(7)], axis=1)
    twice = jnp.concatenate([gathered, gathered], axis=0)
    twice_high = twice.astype(BF16)
    twice_low = (twice - twice_high.astype(F32)).astype(BF16)
    by_high = lax.dot_general(parts2[...], twice_high, NT, preferred_element_type=F32)
    by_low = lax.dot_general(parts2[0:128, :], twice_low, NT, preferred_element_type=F32)
    all_p = by_high[0:128] + (by_high[128:256] + by_low)
    left_half = c[0:32] < 64
    for which in range(2):
        base = 64 * which
        part_p[which] = jnp.where(
            left_half, all_p[base : base + 32], all_p[base + 32 : base + 64]
        )
    got_p[quarter, core] = part_p[core]
    last_from = len(sent)
    pp = [send(part_p.at[other], got_p.at[quarter, core], sibling)]
    for t in (3, 1, 2):
        for which in (core, other):
            pp.append(send(part_p.at[which], got_p.at[quarter, core], along_dp(t, which)))
    own_in.wait_recv()
    output_factor[...] = weights[1, 3] * (1.0 / TOTAL)

    for copy in l3:
        copy.wait_recv()
    final = out_l3[depth]
    for t in range(7):
        final = final + got_l3[t]
    final = final * (1.0 / TOTAL)
    flipped = jnp.concatenate([final, jnp.zeros((96, 128), F32)], axis=0).T
    lane = c[0:32]
    for i in range(2):
        one = flipped[32 * i : 32 * i + 32]
        two = flipped[64 + 32 * i : 96 + 32 * i]
        piece = jnp.where(lane < 7, pltpu.roll(one, 103, 1), pltpu.roll(two, 110, 1))
        piece = jnp.where(lane < 13, piece, pltpu.roll(one, 13, 1))
        piece = jnp.where(lane < 38, piece, pltpu.roll(two, 38, 1))
        patch_factor[i] = piece[:, 0:63]

    oinv_in.wait()
    settle(last_from)
    for copy in pp:
        copy.wait_recv()
    zero, one = (got_p[0, n] + got_p[1, n] + got_p[2, n] + got_p[3, n] for n in range(2))
    product = jnp.concatenate(
        [
            jnp.where(left_half, zero, pltpu.roll(one, 64, 1)),
            jnp.where(left_half, pltpu.roll(zero, 64, 1), one),
        ],
        axis=0,
    )
    product = jnp.dot(
        product, oinv[...], preferred_element_type=F32, precision=HIGHEST
    ) * (1.0 / TOTAL)
    for o in range(27):
        precond[o] = product[2 * o : 2 * o + 2]

    activated_out.wait()
    input_grad_out.wait()
    settle(len(sent))


def hand_on(*refs):
    sources, results, stops, sems = refs[:5], refs[5:10], refs[10:15], refs[15]
    arrivals = []
    for n in range(5):
        copy = pltpu.make_async_copy(sources[n], stops[n], sems.at[n])
        copy.start()
        arrivals.append(copy)
    departures = []
    for n in range(5):
        arrivals[n].wait()
        copy = pltpu.make_async_copy(stops[n], results[n], sems.at[5 + n])
        copy.start()
        departures.append(copy)
    for copy in departures:
        copy.wait()


def per_device(activations, upstream, kernel_weight, patch_inverse, output_inverse):
    vmem = pl.BlockSpec(memory_space=pltpu.VMEM)
    hbm = pl.BlockSpec(memory_space=pl.ANY)
    scratch = [
        ((4, 256, 128), BF16),
        ((4, 256, 128), BF16),
        ((27, 128, 128), BF16),
        ((27, 2, 3456), F32),
        ((128, 128), F32),
        ((4, 256, 128), BF16),
        ((4, 256, 128), BF16),
        ((2, 256, 128), BF16),
        ((2, 256, 128), BF16),
        ((4, 256, 128), BF16),
        ((5, 6, 320, 128), BF16),
        ((3, 6, 288, 128), BF16),
        ((2, 128, 1536), BF16),
        ((256, 1024), BF16),
        ((128, 1024), BF16),
        ((2, 256, 128), F32),
        ((2, 32, 128, 128), F32),
        ((2, 32, 64, 128), F32),
        ((2, 32, 64, 128), BF16),
        ((2, 3, 32, 16, 128), BF16),
        ((2, 512, 128), F32),
        ((2, 4, 4, 32, 128), BF16),
        ((2, 3, 4, 32, 128), BF16),
        ((8, 32, 128), F32),
        ((7, 32, 128), F32),
        ((4, 2, 4, 128, 128), F32),
        ((4, 2, 4, 64, 128), F32),
        ((4, 2, 4, 64, 128), BF16),
        ((15, 4, 2, 16, 128), BF16),
        ((4, 2, 16, 128), F32),
        ((8, 2, 16, 128), F32),
        ((2, 4, 128, 128), F32),
        ((64, 3584), F32),
        ((2, 64, 896), F32),
        ((256, 896), BF16),
        ((2, 32, 128), F32),
        ((4, 2, 32, 128), F32),
    ]
    shapes = (
        jax.ShapeDtypeStruct((4, 256, 128), BF16),
        jax.ShapeDtypeStruct((4, 256, 128), BF16),
        jax.ShapeDtypeStruct((2, 32, 63), F32),
        jax.ShapeDtypeStruct((128, 128), F32),
        jax.ShapeDtypeStruct((27, 2, 128), F32),
    )
    outs = pl.pallas_call(
        step_kernel,
        out_shape=shapes,
        in_specs=[hbm] * 5,
        out_specs=[hbm, hbm, vmem, vmem, vmem],
        scratch_shapes=[pltpu.VMEM(shape, dtype) for shape, dtype in scratch]
        + [
            pltpu.SemaphoreType.DMA((8,)),
            pltpu.SemaphoreType.DMA((128,)),
            pltpu.SemaphoreType.DMA((128,)),
        ],
        compiler_params=pltpu.CompilerParams(
            collective_id=0, has_side_effects=True, vmem_limit_bytes=60 * 1024 * 1024
        ),
        name="step_kernel",
    )(
        activations.reshape(4, 256, 128),
        upstream.reshape(4, 256, 128),
        kernel_weight,
        patch_inverse,
        output_inverse,
    )
    outs = pl.pallas_call(
        hand_on,
        out_shape=shapes,
        in_specs=[hbm] * 5,
        out_specs=[hbm] * 5,
        scratch_shapes=[pltpu.VMEM(shape.shape, shape.dtype) for shape in shapes]
        + [pltpu.SemaphoreType.DMA((10,))],
        compiler_params=pltpu.CompilerParams(vmem_limit_bytes=60 * 1024 * 1024),
        name="hand_on",
    )(*outs)
    activated, input_grad, patch_factor, output_factor, precond = outs
    return (
        activated.reshape(activations.shape),
        input_grad.reshape(activations.shape),
        jnp.transpose(patch_factor, (0, 2, 1)),
        output_factor,
        precond,
    )


def solution(mesh):
    return jax.shard_map(
        per_device,
        mesh=mesh,
        in_specs=(
            P("dp", "space", None, None, None),
            P("dp", "space", None, None, None),
            P(),
            P(None, "space", None),
            P(),
        ),
        out_specs=(
            P("dp", "space", None, None, None),
            P("dp", "space", None, None, None),
            P("space", None, "dp"),
            P(),
            P(None, "space", None),
        ),
        check_vma=False,
    )
```

```python
import functools

import jax
import jax.numpy as jnp
from jax import lax
from jax.experimental import pallas as pl
from jax.experimental.pallas import tpu as pltpu
from jax.sharding import PartitionSpec as P

F32 = jnp.float32
BF16 = jnp.bfloat16
TOTAL = 262144.0
PLANE = (10, 6, 9, 11, 14, 5, 7, 13, 15, 2, 8, 1, 3, 4, 12)
RING = (4, 3, 5, 2, 6, 1, 7)
NT = (((1,), (1,)), ((), ()))
HIGHEST = lax.Precision.HIGHEST


def dot(a, b):
    return jnp.dot(a, b, preferred_element_type=F32)


def tap_shift(offset):
    return (offset // 9 - 1, offset // 3 % 3 - 1, offset % 3 - 1)


def step_kernel(
    act_hbm,
    up_hbm,
    kw_hbm,
    pinv_hbm,
    oinv_hbm,
    activated_hbm,
    input_grad_hbm,
    patch_factor,
    output_factor,
    precond,
    act,
    up,
    kw,
    pinv,
    oinv,
    activated,
    input_grad,
    halo_a,
    halo_s,
    slope,
    ext_a,
    ext_s,
    left,
    left12,
    slope_t,
    begun,
    prod_l,
    got_lc,
    out_l1,
    got_l1,
    sum_l1,
    out_l2,
    got_l2,
    out_l3,
    got_l3,
    prod_w,
    got_wc,
    out_w1,
    got_w1,
    out_w3,
    got_w3,
    weights,
    inverse,
    inverse2,
    parts2,
    part_p,
    got_p,
    local_sem,
    send_sem,
    recv_sem,
):
    space = lax.axis_index("space")
    quarter = lax.axis_index("dp")
    core = lax.rem(space, 2)
    col = lax.rem(space // 2, 4)
    row = lax.rem(space // 8, 4)
    half = space // 32
    depth = half * 4 + quarter
    other = 1 - core

    def device(half, row, col, core, quarter):
        return {"space": ((half * 4 + row) * 4 + col) * 2 + core, "dp": quarter}

    sibling = device(half, row, col, other, quarter)
    following = {"space": lax.rem(space + 1, 64), "dp": quarter}
    preceding = {"space": lax.rem(space + 63, 64), "dp": quarter}
    far = {"space": lax.rem(space + 2 * core + 63, 64), "dp": quarter}

    def along_x(t):
        at = lax.rem(col + t, 4)
        return at, device(half, row, at, core, quarter)

    def along_y(t):
        at = lax.rem(row + t, 4)
        return at, device(half, at, col, core, quarter)

    def in_plane(t):
        at_y = lax.rem(row + t // 4, 4)
        at_x = lax.rem(col + t % 4, 4)
        return at_y, at_x, device(half, at_y, at_x, core, quarter)

    def along_z(t):
        at = lax.rem(depth + t, 8)
        return at, device(at // 4, row, col, core, lax.rem(at, 4))

    def along_dp(t, which):
        return device(half, row, col, which, lax.rem(quarter + t, 4))

    def sixteen(at):
        return pl.ds(pl.multiple_of(at * 16, 16), 16)

    count = [0, 0]
    sent = []

    def send(src, dst, to):
        n = count[0]
        count[0] += 1
        copy = pltpu.make_async_remote_copy(
            src_ref=src,
            dst_ref=dst,
            send_sem=send_sem.at[n],
            recv_sem=recv_sem.at[n],
            device_id=to,
            device_id_type=pl.DeviceIdType.MESH,
        )
        copy.start()
        sent.append(copy)
        return copy

    settled = [0]

    def settle(upto):
        for copy in sent[settled[0] : upto]:
            copy.wait_send()
        settled[0] = upto

    def move(src, dst):
        n = count[1]
        count[1] += 1
        copy = pltpu.make_async_copy(src, dst, local_sem.at[n])
        copy.start()
        return copy

    partners = [far]
    partners += [along_z(t)[1] for t in RING]
    partners += [in_plane(t)[2] for t in PLANE]
    partners += [along_dp(t, other) for t in (3, 1, 2)]
    partners += [sibling]
    barrier = pltpu.get_barrier_semaphore()
    for partner in partners:
        pl.semaphore_signal(
            barrier, inc=1, device_id=partner, device_id_type=pl.DeviceIdType.MESH
        )

    act_in = move(act_hbm, act)
    kw_in = move(kw_hbm, kw)
    up_in = move(up_hbm, up)
    pinv_in = move(pinv_hbm, pinv)
    oinv_in = move(oinv_hbm, oinv)

    r = lax.broadcasted_iota(jnp.int32, (128, 128), 0)
    c = lax.broadcasted_iota(jnp.int32, (128, 128), 1)

    def picked(first, second):
        chan = (
            (r & 1)
            + 2 * ((r >> 6) & 1)
            + first * ((r >> 4) & 3)
            + second * ((r >> 2) & 3)
            + 64 * ((r >> 1) & 1)
        )
        return jnp.where(c == chan, 1.0, 0.0).astype(BF16)

    orders = (picked(4, 16), picked(16, 4))
    unit = jnp.where(c == r, 1.0, 0.0).astype(BF16)

    def turned(order, plane):
        return lax.dot_general(order, plane, NT, preferred_element_type=F32).astype(BF16)

    def place_a(plane, at, shifts):
        wide = plane.astype(F32).reshape(16, 16, 128)
        for dx in shifts:
            moved = plane
            if dx:
                moved = pltpu.roll(wide, (-dx) % 16, 1).reshape(256, 128).astype(BF16)
            ext_a[dx + 2, at, 32:288, :] = moved
            ext_a[dx + 2, at, 0:32, :] = moved[224:256]
            ext_a[dx + 2, at, 288:320, :] = moved[0:32]

    def turn_a(plane, at):
        for part in range(2):
            left[part, :, at * 256 : (at + 1) * 256] = turned(orders[part], plane)

    def place_s(plane, at):
        wide = plane.astype(F32).reshape(16, 16, 128)
        for dx in range(-1, 2):
            moved = plane
            if dx:
                moved = pltpu.roll(wide, (-dx) % 16, 1).reshape(256, 128).astype(BF16)
            ext_s[dx + 1, at, 16:272, :] = moved
            ext_s[dx + 1, at, 0:16, :] = moved[240:256]
            ext_s[dx + 1, at, 272:288, :] = moved[0:16]

    def rows_a(first, dy, dx, planes=4):
        return ext_a[
            dx + 2, first : first + planes, (2 + dy) * 16 : (2 + dy) * 16 + 256, :
        ].reshape(planes * 256, 128)

    def ends_a(dz, dy, dx):
        return jnp.concatenate([rows_a(1 + dz, dy, dx, 1), rows_a(4 + dz, dy, dx, 1)], axis=0)

    prod_l[1, 31] = jnp.zeros((128, 128), F32)
    prod_w[3, 1, 2] = jnp.zeros((128, 128), F32)
    inverse[:, 3456:3584] = jnp.zeros((64, 128), F32)
    inverse[48:64, :] = jnp.zeros((16, 3584), F32)

    act_in.wait()
    for z in range(4):
        place_a(act[z], z + 1, (-2, -1, 0, 1, 2))
        turn_a(act[z], z + 1)
    for k in range(13):
        m = k + 62
        part, slot = (0, 25 + k) if k < 7 else (1, 18 + k)
        prod_l[part, slot] = dot(
            left[part, :, 256:1280], rows_a(1, m // 5 % 5 - 2, m % 5 - 2)
        )

    pl.semaphore_wait(barrier, len(partners))
    before = send(act.at[3], halo_a.at[0], following)
    after = send(act.at[0], halo_a.at[1], preceding)

    def taps_sum(z, depths):
        taps = []
        for dz in depths:
            for o in range(9):
                dy, dx = o // 3 - 1, o % 3 - 1
                first = (2 + dy) * 16
                taps.append(ext_a[dx + 2, z + 1 + dz, first : first + 256, :])
        matrix = kw[9 * depths[0] + 9 : 9 * depths[-1] + 18].reshape(len(taps) * 128, 128)
        return dot(jnp.concatenate(taps, axis=1), matrix)

    def forward(z, pre):
        logistic = jax.nn.sigmoid(pre)
        activated[z] = (pre * logistic).astype(BF16)
        sloped = (up[z].astype(F32) * logistic * (1.0 + pre * (1.0 - logistic))).astype(BF16)
        slope[z] = sloped
        slope_t[:, z * 256 : (z + 1) * 256] = turned(unit, sloped)

    theirs = pl.ds(pl.multiple_of(other * 64, 64), 64)
    mine = pl.ds(pl.multiple_of(core * 64, 64), 64)
    firsts = (col, row)
    seconds = (row, col)
    first_axis = (along_x, along_y)
    second_axis = (along_y, along_x)

    def swap_l(first, last):
        return send(
            prod_l.at[:, first:last, theirs, :], got_lc.at[:, first:last], sibling
        )

    def spread_l(first, last):
        copies = []
        for part in range(2):
            out_l1[part, first:last] = (
                prod_l[part, first:last, mine, :] + got_lc[part, first:last]
            ).astype(BF16)
            for t in (2, 1, 3):
                at, to = first_axis[part](t)
                copies.append(
                    send(
                        out_l1.at[part, first:last, sixteen(at), :],
                        got_l1.at[part, t - 1, first:last],
                        to,
                    )
                )
        return copies

    early_c = swap_l(25, 32)
    kw_in.wait()
    up_in.wait()
    forward(1, taps_sum(1, (-1, 0, 1)))
    forward(2, taps_sum(2, (-1, 0, 1)))
    begun[0] = taps_sum(0, (0, 1))
    begun[1] = taps_sum(3, (-1, 0))

    def blocks(d):
        for b in range(7):
            if 7 * d + b < 27:
                yield b, tap_shift(7 * d + b)

    inner_t = slope_t[:, 256:768]
    for d in range(4):
        for b, (dz, dy, dx) in blocks(d):
            prod_w[d, b // 4, b % 4] = dot(inner_t, rows_a(2 + dz, dy, dx, 2))
    inner_own = dot(inner_t, slope[1:3].reshape(512, 128))

    early_c.wait_recv()
    l1 = spread_l(25, 32)

    pinv_in.wait()
    for o in range(27):
        inverse[2 * o : 2 * o + 2, 0:3456] = pinv[o]
    inverse2[core] = inverse[:, pl.ds(pl.multiple_of(quarter * 896, 128), 896)]
    rows_in = send(inverse2.at[core], inverse2.at[core], sibling)

    before.wait_recv()
    place_a(halo_a[0], 0, (-1, 0, 1))
    after.wait_recv()
    place_a(halo_a[1], 5, (-1, 0, 1))
    forward(3, begun[1] + taps_sum(3, (1,)))
    forward(0, begun[0] + taps_sum(0, (-1,)))
    before_s = send(slope.at[3], halo_s.at[0], following)
    after_s = send(slope.at[0], halo_s.at[1], preceding)
    activated_out = move(activated, activated_hbm)

    outer_t = jnp.concatenate([slope_t[:, 0:256], slope_t[:, 768:1024]], axis=1)
    own = inner_own + dot(outer_t, jnp.concatenate([slope[0], slope[3]], axis=0))
    wc = []
    for d in range(4):
        prod_w[d, 1, 3] = own
        ends = jnp.concatenate([ends_a(*shift) for _, shift in blocks(d)], axis=1)
        wide = dot(outer_t, ends)
        for b, _ in blocks(d):
            prod_w[d, b // 4, b % 4] += wide[:, 128 * b : 128 * b + 128]
        wc.append(send(prod_w.at[d, :, :, theirs, :], got_wc.at[d], sibling))

    pairs = [(dy, dx) for dy in range(-2, 3) for dx in range(-2, 3)]

    def lag_block(first, last):
        for s in range(first, last):
            both = dot(left12[...], rows_a(2, *pairs[s]))
            prod_l[0, s] = both[0:128]
            prod_l[1, s] = both[128:256]
        return swap_l(first, last)

    w1 = []

    def spread_w(first, last):
        for copy in wc[first:last]:
            copy.wait_recv()
        out_w1[first:last] = (prod_w[first:last, :, :, mine, :] + got_wc[first:last]).astype(BF16)
        for t in PLANE:
            at_y, at_x, to = in_plane(t)
            w1.append(
                send(
                    out_w1.at[first:last, :, at_y, sixteen(at_x), :],
                    got_w1.at[t - 1, first:last],
                    to,
                )
            )

    spread_w(0, 2)
    turn_a(halo_a[0], 0)
    place_a(halo_a[1], 5, (-2, 2))
    left12[0:128, :] = left[0, :, 256:1280]
    left12[128:256, :] = left[1, :, 0:1024]
    spread_w(2, 4)
    lc = [lag_block(0, 6), lag_block(6, 13)]
    lc.append(lag_block(13, 25))
    spread_from = len(sent)
    lc[0].wait_recv()
    lc[1].wait_recv()
    l1 += spread_l(0, 13)
    lc[2].wait_recv()
    l1 += spread_l(13, 25)

    for z in range(4):
        place_s(slope[z], z + 1)
    before_s.wait_recv()
    after_s.wait_recv()
    place_s(halo_s[0], 0)
    place_s(halo_s[1], 5)

    kernel_cols = jnp.concatenate([kw[o] for o in range(27)], axis=1)

    def back(z):
        taps = []
        for o in range(27):
            dz, dy, dx = tap_shift(o)
            taps.append(ext_s[1 - dx, z + 1 - dz, (1 - dy) * 16 : (1 - dy) * 16 + 256, :])
        grad = lax.dot_general(
            jnp.concatenate(taps, axis=1), kernel_cols, NT, preferred_element_type=F32
        )
        input_grad[z] = grad.astype(BF16)

    back(0)

    rows_in.wait_recv()
    both_rows = inverse2[...].reshape(128, 896)
    rows_high = both_rows.astype(BF16)
    parts2[0:128, :] = rows_high
    parts2[128:256, :] = (both_rows - rows_high.astype(F32)).astype(BF16)
    settle(spread_from)
    tall = sixteen(core * 4 + col)
    for n in range(2):
        for copy in w1[15 * n : 15 * n + 15]:
            copy.wait_recv()
        two = slice(2 * n, 2 * n + 2)
        total_w = prod_w[two, :, row, tall, :] + got_wc[two, :, row, sixteen(col), :]
        for t in range(15):
            total_w = total_w + got_w1[t, two].astype(F32)
        out_w3[two] = total_w
    got_w3[depth] = out_w3[quarter]
    z_from = len(sent)
    w3 = []
    for t in RING:
        at, to = along_z(t)
        w3.append(send(out_w3.at[lax.rem(at, 4)], got_w3.at[depth], to))

    back(1)

    for copy in l1:
        copy.wait_recv()
    l2 = []
    for part in range(2):
        kept = sixteen(firsts[part])
        high = sixteen(core * 4 + firsts[part])
        total = prod_l[part, :, high, :] + got_lc[part, :, kept, :]
        for t in range(3):
            total = total + got_l1[part, t].astype(F32)
        sum_l1[part] = total.reshape(512, 128)
        for b in range(4):
            for n in range(4):
                groups = [
                    sum_l1[part, pl.ds(4 * b + n + 128 * g, 8, stride=16), :] for g in range(4)
                ]
                out_l2[part, b, n] = jnp.concatenate(groups, axis=0).astype(BF16)
        for t in (2, 1, 3):
            at, to = second_axis[part](t)
            l2.append(send(out_l2.at[part, at], got_l2.at[part, t - 1], to))

    back(2)

    settle(z_from)
    for copy in w3:
        copy.wait_recv()
    reduced = got_w3[0]
    for z in range(1, 8):
        reduced = reduced + got_w3[z]
    weights[:, row, tall, :] = reduced
    gather_from = len(sent)
    g1 = []
    for t in PLANE:
        piece = weights.at[:, row, tall, :]
        g1.append(send(piece, piece, in_plane(t)[2]))

    back(3)
    input_grad_out = move(input_grad, input_grad_hbm)

    for copy in l2:
        copy.wait_recv()
    group = c[0:32] // 32
    totals = []
    for part in range(2):
        total = out_l2[part, seconds[part]].astype(F32)
        for t in range(3):
            total = total + got_l2[part, t].astype(F32)
        totals.append(total)
    for h in range(2):
        groups = [totals[part][2 * h + i] for part in range(2) for i in range(2)]
        for q in range(4):
            packed = jnp.zeros((32, 128), F32)
            for j in range(4):
                shift = (32 * (j - q)) % 128
                piece = pltpu.roll(groups[j], shift, 1) if shift else groups[j]
                packed = jnp.where(group == j, piece, packed)
            out_l3[4 * h + q] = packed
    l3 = []
    for t in RING:
        at, to = along_z(t)
        l3.append(send(out_l3.at[at], got_l3.at[t - 1], to))

    settle(gather_from)
    for copy in g1:
        copy.wait_recv()
    own_in = send(weights.at[1, 3, mine, :], weights.at[1, 3, mine, :], sibling)
    gathered = jnp.concatenate([weights[b // 4, b % 4, mine, :] for b in range(7)], axis=1)
    twice = jnp.concatenate([gathered, gathered], axis=0)
    twice_high = twice.astype(BF16)
    twice_low = (twice - twice_high.astype(F32)).astype(BF16)
    by_high = lax.dot_general(parts2[...], twice_high, NT, preferred_element_type=F32)
    by_low = lax.dot_general(parts2[0:128, :], twice_low, NT, preferred_element_type=F32)
    all_p = by_high[0:128] + (by_high[128:256] + by_low)
    left_half = c[0:32] < 64
    for which in range(2):
        base = 64 * which
        part_p[which] = jnp.where(
            left_half, all_p[base : base + 32], all_p[base + 32 : base + 64]
        )
    got_p[quarter, core] = part_p[core]
    last_from = len(sent)
    pp = [send(part_p.at[other], got_p.at[quarter, core], sibling)]
    for t in (3, 1, 2):
        for which in (core, other):
            pp.append(send(part_p.at[which], got_p.at[quarter, core], along_dp(t, which)))
    own_in.wait_recv()
    output_factor[...] = weights[1, 3] * (1.0 / TOTAL)

    for copy in l3:
        copy.wait_recv()
    final = out_l3[depth]
    for t in range(7):
        final = final + got_l3[t]
    final = final * (1.0 / TOTAL)
    flipped = jnp.concatenate([final, jnp.zeros((96, 128), F32)], axis=0).T
    lane = c[0:32]
    for i in range(2):
        one = flipped[32 * i : 32 * i + 32]
        two = flipped[64 + 32 * i : 96 + 32 * i]
        piece = jnp.where(lane < 7, pltpu.roll(one, 103, 1), pltpu.roll(two, 110, 1))
        piece = jnp.where(lane < 13, piece, pltpu.roll(one, 13, 1))
        piece = jnp.where(lane < 38, piece, pltpu.roll(two, 38, 1))
        patch_factor[i] = piece[:, 0:63]

    oinv_in.wait()
    settle(last_from)
    for copy in pp:
        copy.wait_recv()
    zero, one = (got_p[0, n] + got_p[1, n] + got_p[2, n] + got_p[3, n] for n in range(2))
    product = jnp.concatenate(
        [
            jnp.where(left_half, zero, pltpu.roll(one, 64, 1)),
            jnp.where(left_half, pltpu.roll(zero, 64, 1), one),
        ],
        axis=0,
    )
    product = jnp.dot(
        product, oinv[...], preferred_element_type=F32, precision=HIGHEST
    ) * (1.0 / TOTAL)
    for o in range(27):
        precond[o] = product[2 * o : 2 * o + 2]

    activated_out.wait()
    input_grad_out.wait()
    settle(len(sent))


def hand_on(*refs):
    sources, results, stops, sems = refs[:5], refs[5:10], refs[10:15], refs[15]
    arrivals = []
    for n in range(5):
        copy = pltpu.make_async_copy(sources[n], stops[n], sems.at[n])
        copy.start()
        arrivals.append(copy)
    departures = []
    for n in range(5):
        arrivals[n].wait()
        copy = pltpu.make_async_copy(stops[n], results[n], sems.at[5 + n])
        copy.start()
        departures.append(copy)
    for copy in departures:
        copy.wait()


def per_device(activations, upstream, kernel_weight, patch_inverse, output_inverse):
    vmem = pl.BlockSpec(memory_space=pltpu.VMEM)
    hbm = pl.BlockSpec(memory_space=pl.ANY)
    scratch = [
        ((4, 256, 128), BF16),
        ((4, 256, 128), BF16),
        ((27, 128, 128), BF16),
        ((27, 2, 3456), F32),
        ((128, 128), F32),
        ((4, 256, 128), BF16),
        ((4, 256, 128), BF16),
        ((2, 256, 128), BF16),
        ((2, 256, 128), BF16),
        ((4, 256, 128), BF16),
        ((5, 6, 320, 128), BF16),
        ((3, 6, 288, 128), BF16),
        ((2, 128, 1536), BF16),
        ((256, 1024), BF16),
        ((128, 1024), BF16),
        ((2, 256, 128), F32),
        ((2, 32, 128, 128), F32),
        ((2, 32, 64, 128), F32),
        ((2, 32, 64, 128), BF16),
        ((2, 3, 32, 16, 128), BF16),
        ((2, 512, 128), F32),
        ((2, 4, 4, 32, 128), BF16),
        ((2, 3, 4, 32, 128), BF16),
        ((8, 32, 128), F32),
        ((7, 32, 128), F32),
        ((4, 2, 4, 128, 128), F32),
        ((4, 2, 4, 64, 128), F32),
        ((4, 2, 4, 64, 128), BF16),
        ((15, 4, 2, 16, 128), BF16),
        ((4, 2, 16, 128), F32),
        ((8, 2, 16, 128), F32),
        ((2, 4, 128, 128), F32),
        ((64, 3584), F32),
        ((2, 64, 896), F32),
        ((256, 896), BF16),
        ((2, 32, 128), F32),
        ((4, 2, 32, 128), F32),
    ]
    shapes = (
        jax.ShapeDtypeStruct((4, 256, 128), BF16),
        jax.ShapeDtypeStruct((4, 256, 128), BF16),
        jax.ShapeDtypeStruct((2, 32, 63), F32),
        jax.ShapeDtypeStruct((128, 128), F32),
        jax.ShapeDtypeStruct((27, 2, 128), F32),
    )
    outs = pl.pallas_call(
        step_kernel,
        out_shape=shapes,
        in_specs=[hbm] * 5,
        out_specs=[hbm, hbm, vmem, vmem, vmem],
        scratch_shapes=[pltpu.VMEM(shape, dtype) for shape, dtype in scratch]
        + [
            pltpu.SemaphoreType.DMA((8,)),
            pltpu.SemaphoreType.DMA((128,)),
            pltpu.SemaphoreType.DMA((128,)),
        ],
        compiler_params=pltpu.CompilerParams(
            collective_id=0, has_side_effects=True, vmem_limit_bytes=60 * 1024 * 1024
        ),
        name="step_kernel",
    )(
        activations.reshape(4, 256, 128),
        upstream.reshape(4, 256, 128),
        kernel_weight,
        patch_inverse,
        output_inverse,
    )
    outs = pl.pallas_call(
        hand_on,
        out_shape=shapes,
        in_specs=[hbm] * 5,
        out_specs=[hbm] * 5,
        scratch_shapes=[pltpu.VMEM(shape.shape, shape.dtype) for shape in shapes]
        + [pltpu.SemaphoreType.DMA((10,))],
        compiler_params=pltpu.CompilerParams(vmem_limit_bytes=60 * 1024 * 1024),
        name="hand_on",
    )(*outs)
    activated, input_grad, patch_factor, output_factor, precond = outs
    return (
        activated.reshape(activations.shape),
        input_grad.reshape(activations.shape),
        jnp.transpose(patch_factor, (0, 2, 1)),
        output_factor,
        precond,
    )


def solution(mesh):
    return jax.shard_map(
        per_device,
        mesh=mesh,
        in_specs=(
            P("dp", "space", None, None, None),
            P("dp", "space", None, None, None),
            P(),
            P(None, "space", None),
            P(),
        ),
        out_specs=(
            P("dp", "space", None, None, None),
            P("dp", "space", None, None, None),
            P("space", None, "dp"),
            P(),
            P(None, "space", None),
        ),
        check_vma=False,
    )
```

```python
import functools

import jax
import jax.numpy as jnp
from jax import lax
from jax.experimental import pallas as pl
from jax.experimental.pallas import tpu as pltpu
from jax.sharding import PartitionSpec as P

F32 = jnp.float32
BF16 = jnp.bfloat16
TOTAL = 262144.0
PLANE = (10, 6, 9, 11, 14, 5, 7, 13, 15, 2, 8, 1, 3, 4, 12)
RING = (4, 3, 5, 2, 6, 1, 7)
NT = (((1,), (1,)), ((), ()))
HIGHEST = lax.Precision.HIGHEST


def dot(a, b):
    return jnp.dot(a, b, preferred_element_type=F32)


def tap_shift(offset):
    return (offset // 9 - 1, offset // 3 % 3 - 1, offset % 3 - 1)


def step_kernel(
    act_hbm,
    up_hbm,
    kw_hbm,
    pinv_hbm,
    oinv_hbm,
    activated_hbm,
    input_grad_hbm,
    patch_factor,
    output_factor,
    precond,
    act,
    up,
    kw,
    pinv,
    oinv,
    activated,
    input_grad,
    halo_a,
    halo_s,
    slope,
    ext_a,
    ext_s,
    left,
    left12,
    slope_t,
    begun,
    prod_l,
    got_lc,
    out_l1,
    got_l1,
    sum_l1,
    out_l2,
    got_l2,
    out_l3,
    got_l3,
    prod_w,
    got_wc,
    out_w1,
    got_w1,
    out_w3,
    got_w3,
    weights,
    inverse,
    inverse2,
    parts2,
    part_p,
    got_p,
    local_sem,
    send_sem,
    recv_sem,
):
    space = lax.axis_index("space")
    quarter = lax.axis_index("dp")
    core = lax.rem(space, 2)
    col = lax.rem(space // 2, 4)
    row = lax.rem(space // 8, 4)
    half = space // 32
    depth = half * 4 + quarter
    other = 1 - core

    def device(half, row, col, core, quarter):
        return {"space": ((half * 4 + row) * 4 + col) * 2 + core, "dp": quarter}

    sibling = device(half, row, col, other, quarter)
    following = {"space": lax.rem(space + 1, 64), "dp": quarter}
    preceding = {"space": lax.rem(space + 63, 64), "dp": quarter}
    far = {"space": lax.rem(space + 2 * core + 63, 64), "dp": quarter}

    def along_x(t):
        at = lax.rem(col + t, 4)
        return at, device(half, row, at, core, quarter)

    def along_y(t):
        at = lax.rem(row + t, 4)
        return at, device(half, at, col, core, quarter)

    def in_plane(t):
        at_y = lax.rem(row + t // 4, 4)
        at_x = lax.rem(col + t % 4, 4)
        return at_y, at_x, device(half, at_y, at_x, core, quarter)

    def along_z(t):
        at = lax.rem(depth + t, 8)
        return at, device(at // 4, row, col, core, lax.rem(at, 4))

    def along_dp(t, which):
        return device(half, row, col, which, lax.rem(quarter + t, 4))

    def sixteen(at):
        return pl.ds(pl.multiple_of(at * 16, 16), 16)

    count = [0, 0]
    sent = []

    def send(src, dst, to):
        n = count[0]
        count[0] += 1
        copy = pltpu.make_async_remote_copy(
            src_ref=src,
            dst_ref=dst,
            send_sem=send_sem.at[n],
            recv_sem=recv_sem.at[n],
            device_id=to,
            device_id_type=pl.DeviceIdType.MESH,
        )
        copy.start()
        sent.append(copy)
        return copy

    settled = [0]

    def settle(upto):
        for copy in sent[settled[0] : upto]:
            copy.wait_send()
        settled[0] = upto

    def move(src, dst):
        n = count[1]
        count[1] += 1
        copy = pltpu.make_async_copy(src, dst, local_sem.at[n])
        copy.start()
        return copy

    partners = [far]
    partners += [along_z(t)[1] for t in RING]
    partners += [in_plane(t)[2] for t in PLANE]
    partners += [along_dp(t, other) for t in (3, 1, 2)]
    partners += [sibling]
    barrier = pltpu.get_barrier_semaphore()
    for partner in partners:
        pl.semaphore_signal(
            barrier, inc=1, device_id=partner, device_id_type=pl.DeviceIdType.MESH
        )

    act_in = move(act_hbm, act)
    kw_in = move(kw_hbm, kw)
    up_in = move(up_hbm, up)
    pinv_in = move(pinv_hbm, pinv)
    oinv_in = move(oinv_hbm, oinv)

    r = lax.broadcasted_iota(jnp.int32, (128, 128), 0)
    c = lax.broadcasted_iota(jnp.int32, (128, 128), 1)

    def picked(first, second):
        chan = (
            (r & 1)
            + 2 * ((r >> 6) & 1)
            + first * ((r >> 4) & 3)
            + second * ((r >> 2) & 3)
            + 64 * ((r >> 1) & 1)
        )
        return jnp.where(c == chan, 1.0, 0.0).astype(BF16)

    orders = (picked(4, 16), picked(16, 4))
    unit = jnp.where(c == r, 1.0, 0.0).astype(BF16)

    def turned(order, plane):
        return lax.dot_general(order, plane, NT, preferred_element_type=F32).astype(BF16)

    def place_a(plane, at, shifts):
        wide = plane.astype(F32).reshape(16, 16, 128)
        for dx in shifts:
            moved = plane
            if dx:
                moved = pltpu.roll(wide, (-dx) % 16, 1).reshape(256, 128).astype(BF16)
            ext_a[dx + 2, at, 32:288, :] = moved
            ext_a[dx + 2, at, 0:32, :] = moved[224:256]
            ext_a[dx + 2, at, 288:320, :] = moved[0:32]

    def turn_a(plane, at):
        for part in range(2):
            left[part, :, at * 256 : (at + 1) * 256] = turned(orders[part], plane)

    def place_s(plane, at):
        wide = plane.astype(F32).reshape(16, 16, 128)
        for dx in range(-1, 2):
            moved = plane
            if dx:
                moved = pltpu.roll(wide, (-dx) % 16, 1).reshape(256, 128).astype(BF16)
            ext_s[dx + 1, at, 16:272, :] = moved
            ext_s[dx + 1, at, 0:16, :] = moved[240:256]
            ext_s[dx + 1, at, 272:288, :] = moved[0:16]

    def rows_a(first, dy, dx, planes=4):
        return ext_a[
            dx + 2, first : first + planes, (2 + dy) * 16 : (2 + dy) * 16 + 256, :
        ].reshape(planes * 256, 128)

    def ends_a(dz, dy, dx):
        return jnp.concatenate([rows_a(1 + dz, dy, dx, 1), rows_a(4 + dz, dy, dx, 1)], axis=0)

    prod_l[1, 31] = jnp.zeros((128, 128), F32)
    prod_w[3, 1, 2] = jnp.zeros((128, 128), F32)
    inverse[:, 3456:3584] = jnp.zeros((64, 128), F32)
    inverse[48:64, :] = jnp.zeros((16, 3584), F32)

    act_in.wait()
    for z in range(4):
        place_a(act[z], z + 1, (-2, -1, 0, 1, 2))
        turn_a(act[z], z + 1)
    for k in range(13):
        m = k + 62
        part, slot = (0, 25 + k) if k < 7 else (1, 18 + k)
        prod_l[part, slot] = dot(
            left[part, :, 256:1280], rows_a(1, m // 5 % 5 - 2, m % 5 - 2)
        )

    pl.semaphore_wait(barrier, len(partners))
    before = send(act.at[3], halo_a.at[0], following)
    after = send(act.at[0], halo_a.at[1], preceding)

    def taps_sum(z, depths):
        taps = []
        for dz in depths:
            for o in range(9):
                dy, dx = o // 3 - 1, o % 3 - 1
                first = (2 + dy) * 16
                taps.append(ext_a[dx + 2, z + 1 + dz, first : first + 256, :])
        matrix = kw[9 * depths[0] + 9 : 9 * depths[-1] + 18].reshape(len(taps) * 128, 128)
        return dot(jnp.concatenate(taps, axis=1), matrix)

    def forward(z, pre):
        logistic = jax.nn.sigmoid(pre)
        activated[z] = (pre * logistic).astype(BF16)
        sloped = (up[z].astype(F32) * logistic * (1.0 + pre * (1.0 - logistic))).astype(BF16)
        slope[z] = sloped
        slope_t[:, z * 256 : (z + 1) * 256] = turned(unit, sloped)

    theirs = pl.ds(pl.multiple_of(other * 64, 64), 64)
    mine = pl.ds(pl.multiple_of(core * 64, 64), 64)
    firsts = (col, row)
    seconds = (row, col)
    first_axis = (along_x, along_y)
    second_axis = (along_y, along_x)

    def swap_l(first, last):
        return send(
            prod_l.at[:, first:last, theirs, :], got_lc.at[:, first:last], sibling
        )

    def spread_l(first, last):
        copies = []
        for part in range(2):
            out_l1[part, first:last] = (
                prod_l[part, first:last, mine, :] + got_lc[part, first:last]
            ).astype(BF16)
            for t in (2, 1, 3):
                at, to = first_axis[part](t)
                copies.append(
                    send(
                        out_l1.at[part, first:last, sixteen(at), :],
                        got_l1.at[part, t - 1, first:last],
                        to,
                    )
                )
        return copies

    early_c = swap_l(25, 32)
    kw_in.wait()
    up_in.wait()
    forward(1, taps_sum(1, (-1, 0, 1)))
    forward(2, taps_sum(2, (-1, 0, 1)))
    begun[0] = taps_sum(0, (0, 1))
    begun[1] = taps_sum(3, (-1, 0))

    def blocks(d):
        for b in range(7):
            if 7 * d + b < 27:
                yield b, tap_shift(7 * d + b)

    inner_t = slope_t[:, 256:768]
    for d in range(4):
        for b, (dz, dy, dx) in blocks(d):
            prod_w[d, b // 4, b % 4] = dot(inner_t, rows_a(2 + dz, dy, dx, 2))
    inner_own = dot(inner_t, slope[1:3].reshape(512, 128))

    early_c.wait_recv()
    l1 = spread_l(25, 32)

    pinv_in.wait()
    for o in range(27):
        inverse[2 * o : 2 * o + 2, 0:3456] = pinv[o]
    inverse2[core] = inverse[:, pl.ds(pl.multiple_of(quarter * 896, 128), 896)]
    rows_in = send(inverse2.at[core], inverse2.at[core], sibling)

    before.wait_recv()
    place_a(halo_a[0], 0, (-1, 0, 1))
    after.wait_recv()
    place_a(halo_a[1], 5, (-1, 0, 1))
    forward(3, begun[1] + taps_sum(3, (1,)))
    forward(0, begun[0] + taps_sum(0, (-1,)))
    before_s = send(slope.at[3], halo_s.at[0], following)
    after_s = send(slope.at[0], halo_s.at[1], preceding)
    activated_out = move(activated, activated_hbm)

    outer_t = jnp.concatenate([slope_t[:, 0:256], slope_t[:, 768:1024]], axis=1)
    own = inner_own + dot(outer_t, jnp.concatenate([slope[0], slope[3]], axis=0))
    wc = []
    for d in range(4):
        prod_w[d, 1, 3] = own
        ends = jnp.concatenate([ends_a(*shift) for _, shift in blocks(d)], axis=1)
        wide = dot(outer_t, ends)
        for b, _ in blocks(d):
            prod_w[d, b // 4, b % 4] += wide[:, 128 * b : 128 * b + 128]
        wc.append(send(prod_w.at[d, :, :, theirs, :], got_wc.at[d], sibling))

    turn_a(halo_a[0], 0)
    place_a(halo_a[1], 5, (-2, 2))
    left12[0:128, :] = left[0, :, 256:1280]
    left12[128:256, :] = left[1, :, 0:1024]
    pairs = [(dy, dx) for dy in range(-2, 3) for dx in range(-2, 3)]

    def lag_block(first, last):
        for s in range(first, last):
            both = dot(left12[...], rows_a(2, *pairs[s]))
            prod_l[0, s] = both[0:128]
            prod_l[1, s] = both[128:256]
        return swap_l(first, last)

    w1 = []

    def spread_w(first, last):
        for copy in wc[first:last]:
            copy.wait_recv()
        out_w1[first:last] = (prod_w[first:last, :, :, mine, :] + got_wc[first:last]).astype(BF16)
        for t in PLANE:
            at_y, at_x, to = in_plane(t)
            w1.append(
                send(
                    out_w1.at[first:last, :, at_y, sixteen(at_x), :],
                    got_w1.at[t - 1, first:last],
                    to,
                )
            )

    spread_w(0, 2)
    lc = [lag_block(0, 6)]
    spread_w(2, 4)
    lc.append(lag_block(6, 13))
    lc.append(lag_block(13, 25))
    spread_from = len(sent)
    lc[0].wait_recv()
    lc[1].wait_recv()
    l1 += spread_l(0, 13)
    lc[2].wait_recv()
    l1 += spread_l(13, 25)

    for z in range(4):
        place_s(slope[z], z + 1)
    before_s.wait_recv()
    after_s.wait_recv()
    place_s(halo_s[0], 0)
    place_s(halo_s[1], 5)

    kernel_cols = jnp.concatenate([kw[o] for o in range(27)], axis=1)

    def back(z):
        taps = []
        for o in range(27):
            dz, dy, dx = tap_shift(o)
            taps.append(ext_s[1 - dx, z + 1 - dz, (1 - dy) * 16 : (1 - dy) * 16 + 256, :])
        grad = lax.dot_general(
            jnp.concatenate(taps, axis=1), kernel_cols, NT, preferred_element_type=F32
        )
        input_grad[z] = grad.astype(BF16)

    back(0)

    rows_in.wait_recv()
    both_rows = inverse2[...].reshape(128, 896)
    rows_high = both_rows.astype(BF16)
    parts2[0:128, :] = rows_high
    parts2[128:256, :] = (both_rows - rows_high.astype(F32)).astype(BF16)
    settle(spread_from)
    tall = sixteen(core * 4 + col)
    for n in range(2):
        for copy in w1[15 * n : 15 * n + 15]:
            copy.wait_recv()
        two = slice(2 * n, 2 * n + 2)
        total_w = prod_w[two, :, row, tall, :] + got_wc[two, :, row, sixteen(col), :]
        for t in range(15):
            total_w = total_w + got_w1[t, two].astype(F32)
        out_w3[two] = total_w
    got_w3[depth] = out_w3[quarter]
    z_from = len(sent)
    w3 = []
    for t in RING:
        at, to = along_z(t)
        w3.append(send(out_w3.at[lax.rem(at, 4)], got_w3.at[depth], to))

    for copy in l1:
        copy.wait_recv()
    l2 = []
    for part in range(2):
        kept = sixteen(firsts[part])
        high = sixteen(core * 4 + firsts[part])
        total = prod_l[part, :, high, :] + got_lc[part, :, kept, :]
        for t in range(3):
            total = total + got_l1[part, t].astype(F32)
        sum_l1[part] = total.reshape(512, 128)
        for b in range(4):
            for n in range(4):
                groups = [
                    sum_l1[part, pl.ds(4 * b + n + 128 * g, 8, stride=16), :] for g in range(4)
                ]
                out_l2[part, b, n] = jnp.concatenate(groups, axis=0).astype(BF16)
        for t in (2, 1, 3):
            at, to = second_axis[part](t)
            l2.append(send(out_l2.at[part, at], got_l2.at[part, t - 1], to))

    back(1)
    back(2)

    settle(z_from)
    for copy in w3:
        copy.wait_recv()
    reduced = got_w3[0]
    for z in range(1, 8):
        reduced = reduced + got_w3[z]
    weights[:, row, tall, :] = reduced
    gather_from = len(sent)
    g1 = []
    for t in PLANE:
        piece = weights.at[:, row, tall, :]
        g1.append(send(piece, piece, in_plane(t)[2]))

    for copy in l2:
        copy.wait_recv()
    group = c[0:32] // 32
    totals = []
    for part in range(2):
        total = out_l2[part, seconds[part]].astype(F32)
        for t in range(3):
            total = total + got_l2[part, t].astype(F32)
        totals.append(total)
    for h in range(2):
        groups = [totals[part][2 * h + i] for part in range(2) for i in range(2)]
        for q in range(4):
            packed = jnp.zeros((32, 128), F32)
            for j in range(4):
                shift = (32 * (j - q)) % 128
                piece = pltpu.roll(groups[j], shift, 1) if shift else groups[j]
                packed = jnp.where(group == j, piece, packed)
            out_l3[4 * h + q] = packed
    l3 = []
    for t in RING:
        at, to = along_z(t)
        l3.append(send(out_l3.at[at], got_l3.at[t - 1], to))

    back(3)
    input_grad_out = move(input_grad, input_grad_hbm)

    settle(gather_from)
    for copy in g1:
        copy.wait_recv()
    own_in = send(weights.at[1, 3, mine, :], weights.at[1, 3, mine, :], sibling)
    gathered = jnp.concatenate([weights[b // 4, b % 4, mine, :] for b in range(7)], axis=1)
    twice = jnp.concatenate([gathered, gathered], axis=0)
    twice_high = twice.astype(BF16)
    twice_low = (twice - twice_high.astype(F32)).astype(BF16)
    by_high = lax.dot_general(parts2[...], twice_high, NT, preferred_element_type=F32)
    by_low = lax.dot_general(parts2[0:128, :], twice_low, NT, preferred_element_type=F32)
    all_p = by_high[0:128] + (by_high[128:256] + by_low)
    left_half = c[0:32] < 64
    for which in range(2):
        base = 64 * which
        part_p[which] = jnp.where(
            left_half, all_p[base : base + 32], all_p[base + 32 : base + 64]
        )
    got_p[quarter, core] = part_p[core]
    last_from = len(sent)
    pp = [send(part_p.at[other], got_p.at[quarter, core], sibling)]
    for t in (3, 1, 2):
        for which in (core, other):
            pp.append(send(part_p.at[which], got_p.at[quarter, core], along_dp(t, which)))
    own_in.wait_recv()
    output_factor[...] = weights[1, 3] * (1.0 / TOTAL)

    for copy in l3:
        copy.wait_recv()
    final = out_l3[depth]
    for t in range(7):
        final = final + got_l3[t]
    final = final * (1.0 / TOTAL)
    flipped = jnp.concatenate([final, jnp.zeros((96, 128), F32)], axis=0).T
    lane = c[0:32]
    for i in range(2):
        one = flipped[32 * i : 32 * i + 32]
        two = flipped[64 + 32 * i : 96 + 32 * i]
        piece = jnp.where(lane < 7, pltpu.roll(one, 103, 1), pltpu.roll(two, 110, 1))
        piece = jnp.where(lane < 13, piece, pltpu.roll(one, 13, 1))
        piece = jnp.where(lane < 38, piece, pltpu.roll(two, 38, 1))
        patch_factor[i] = piece[:, 0:63]

    oinv_in.wait()
    settle(last_from)
    for copy in pp:
        copy.wait_recv()
    zero, one = (got_p[0, n] + got_p[1, n] + got_p[2, n] + got_p[3, n] for n in range(2))
    product = jnp.concatenate(
        [
            jnp.where(left_half, zero, pltpu.roll(one, 64, 1)),
            jnp.where(left_half, pltpu.roll(zero, 64, 1), one),
        ],
        axis=0,
    )
    product = jnp.dot(
        product, oinv[...], preferred_element_type=F32, precision=HIGHEST
    ) * (1.0 / TOTAL)
    for o in range(27):
        precond[o] = product[2 * o : 2 * o + 2]

    activated_out.wait()
    input_grad_out.wait()
    settle(len(sent))


def hand_on(*refs):
    sources, results, stops, sems = refs[:5], refs[5:10], refs[10:15], refs[15]
    arrivals = []
    for n in range(5):
        copy = pltpu.make_async_copy(sources[n], stops[n], sems.at[n])
        copy.start()
        arrivals.append(copy)
    departures = []
    for n in range(5):
        arrivals[n].wait()
        copy = pltpu.make_async_copy(stops[n], results[n], sems.at[5 + n])
        copy.start()
        departures.append(copy)
    for copy in departures:
        copy.wait()


def per_device(activations, upstream, kernel_weight, patch_inverse, output_inverse):
    vmem = pl.BlockSpec(memory_space=pltpu.VMEM)
    hbm = pl.BlockSpec(memory_space=pl.ANY)
    scratch = [
        ((4, 256, 128), BF16),
        ((4, 256, 128), BF16),
        ((27, 128, 128), BF16),
        ((27, 2, 3456), F32),
        ((128, 128), F32),
        ((4, 256, 128), BF16),
        ((4, 256, 128), BF16),
        ((2, 256, 128), BF16),
        ((2, 256, 128), BF16),
        ((4, 256, 128), BF16),
        ((5, 6, 320, 128), BF16),
        ((3, 6, 288, 128), BF16),
        ((2, 128, 1536), BF16),
        ((256, 1024), BF16),
        ((128, 1024), BF16),
        ((2, 256, 128), F32),
        ((2, 32, 128, 128), F32),
        ((2, 32, 64, 128), F32),
        ((2, 32, 64, 128), BF16),
        ((2, 3, 32, 16, 128), BF16),
        ((2, 512, 128), F32),
        ((2, 4, 4, 32, 128), BF16),
        ((2, 3, 4, 32, 128), BF16),
        ((8, 32, 128), F32),
        ((7, 32, 128), F32),
        ((4, 2, 4, 128, 128), F32),
        ((4, 2, 4, 64, 128), F32),
        ((4, 2, 4, 64, 128), BF16),
        ((15, 4, 2, 16, 128), BF16),
        ((4, 2, 16, 128), F32),
        ((8, 2, 16, 128), F32),
        ((2, 4, 128, 128), F32),
        ((64, 3584), F32),
        ((2, 64, 896), F32),
        ((256, 896), BF16),
        ((2, 32, 128), F32),
        ((4, 2, 32, 128), F32),
    ]
    shapes = (
        jax.ShapeDtypeStruct((4, 256, 128), BF16),
        jax.ShapeDtypeStruct((4, 256, 128), BF16),
        jax.ShapeDtypeStruct((2, 32, 63), F32),
        jax.ShapeDtypeStruct((128, 128), F32),
        jax.ShapeDtypeStruct((27, 2, 128), F32),
    )
    outs = pl.pallas_call(
        step_kernel,
        out_shape=shapes,
        in_specs=[hbm] * 5,
        out_specs=[hbm, hbm, vmem, vmem, vmem],
        scratch_shapes=[pltpu.VMEM(shape, dtype) for shape, dtype in scratch]
        + [
            pltpu.SemaphoreType.DMA((8,)),
            pltpu.SemaphoreType.DMA((128,)),
            pltpu.SemaphoreType.DMA((128,)),
        ],
        compiler_params=pltpu.CompilerParams(
            collective_id=0, has_side_effects=True, vmem_limit_bytes=60 * 1024 * 1024
        ),
        name="step_kernel",
    )(
        activations.reshape(4, 256, 128),
        upstream.reshape(4, 256, 128),
        kernel_weight,
        patch_inverse,
        output_inverse,
    )
    outs = pl.pallas_call(
        hand_on,
        out_shape=shapes,
        in_specs=[hbm] * 5,
        out_specs=[hbm] * 5,
        scratch_shapes=[pltpu.VMEM(shape.shape, shape.dtype) for shape in shapes]
        + [pltpu.SemaphoreType.DMA((10,))],
        compiler_params=pltpu.CompilerParams(vmem_limit_bytes=60 * 1024 * 1024),
        name="hand_on",
    )(*outs)
    activated, input_grad, patch_factor, output_factor, precond = outs
    return (
        activated.reshape(activations.shape),
        input_grad.reshape(activations.shape),
        jnp.transpose(patch_factor, (0, 2, 1)),
        output_factor,
        precond,
    )


def solution(mesh):
    return jax.shard_map(
        per_device,
        mesh=mesh,
        in_specs=(
            P("dp", "space", None, None, None),
            P("dp", "space", None, None, None),
            P(),
            P(None, "space", None),
            P(),
        ),
        out_specs=(
            P("dp", "space", None, None, None),
            P("dp", "space", None, None, None),
            P("space", None, "dp"),
            P(),
            P(None, "space", None),
        ),
        check_vma=False,
    )
```

```python
import functools

import jax
import jax.numpy as jnp
from jax import lax
from jax.experimental import pallas as pl
from jax.experimental.pallas import tpu as pltpu
from jax.sharding import PartitionSpec as P

F32 = jnp.float32
BF16 = jnp.bfloat16
TOTAL = 262144.0
PLANE = (10, 6, 9, 11, 14, 5, 7, 13, 15, 2, 8, 1, 3, 4, 12)
RING = (4, 3, 5, 2, 6, 1, 7)
NT = (((1,), (1,)), ((), ()))
HIGHEST = lax.Precision.HIGHEST


def dot(a, b):
    return jnp.dot(a, b, preferred_element_type=F32)


def tap_shift(offset):
    return (offset // 9 - 1, offset // 3 % 3 - 1, offset % 3 - 1)


def step_kernel(
    act_hbm,
    up_hbm,
    kw_hbm,
    pinv_hbm,
    oinv_hbm,
    activated_hbm,
    input_grad_hbm,
    patch_factor,
    output_factor,
    precond,
    act,
    up,
    kw,
    pinv,
    oinv,
    activated,
    input_grad,
    halo_a,
    halo_s,
    slope,
    ext_a,
    ext_s,
    left,
    left12,
    slope_t,
    begun,
    prod_l,
    got_lc,
    out_l1,
    got_l1,
    sum_l1,
    out_l2,
    got_l2,
    out_l3,
    got_l3,
    prod_w,
    got_wc,
    out_w1,
    got_w1,
    out_w3,
    got_w3,
    weights,
    inverse,
    inverse2,
    parts2,
    part_p,
    got_p,
    local_sem,
    send_sem,
    recv_sem,
):
    space = lax.axis_index("space")
    quarter = lax.axis_index("dp")
    core = lax.rem(space, 2)
    col = lax.rem(space // 2, 4)
    row = lax.rem(space // 8, 4)
    half = space // 32
    depth = half * 4 + quarter
    other = 1 - core

    def device(half, row, col, core, quarter):
        return {"space": ((half * 4 + row) * 4 + col) * 2 + core, "dp": quarter}

    sibling = device(half, row, col, other, quarter)
    following = {"space": lax.rem(space + 1, 64), "dp": quarter}
    preceding = {"space": lax.rem(space + 63, 64), "dp": quarter}
    far = {"space": lax.rem(space + 2 * core + 63, 64), "dp": quarter}

    def along_x(t):
        at = lax.rem(col + t, 4)
        return at, device(half, row, at, core, quarter)

    def along_y(t):
        at = lax.rem(row + t, 4)
        return at, device(half, at, col, core, quarter)

    def in_plane(t):
        at_y = lax.rem(row + t // 4, 4)
        at_x = lax.rem(col + t % 4, 4)
        return at_y, at_x, device(half, at_y, at_x, core, quarter)

    def along_z(t):
        at = lax.rem(depth + t, 8)
        return at, device(at // 4, row, col, core, lax.rem(at, 4))

    def along_dp(t, which):
        return device(half, row, col, which, lax.rem(quarter + t, 4))

    def sixteen(at):
        return pl.ds(pl.multiple_of(at * 16, 16), 16)

    count = [0, 0]
    sent = []

    def send(src, dst, to):
        n = count[0]
        count[0] += 1
        copy = pltpu.make_async_remote_copy(
            src_ref=src,
            dst_ref=dst,
            send_sem=send_sem.at[n],
            recv_sem=recv_sem.at[n],
            device_id=to,
            device_id_type=pl.DeviceIdType.MESH,
        )
        copy.start()
        sent.append(copy)
        return copy

    settled = [0]

    def settle(upto):
        for copy in sent[settled[0] : upto]:
            copy.wait_send()
        settled[0] = upto

    def move(src, dst):
        n = count[1]
        count[1] += 1
        copy = pltpu.make_async_copy(src, dst, local_sem.at[n])
        copy.start()
        return copy

    partners = [far]
    partners += [along_z(t)[1] for t in RING]
    partners += [in_plane(t)[2] for t in PLANE]
    partners += [along_dp(t, other) for t in (3, 1, 2)]
    partners += [sibling]
    barrier = pltpu.get_barrier_semaphore()
    for partner in partners:
        pl.semaphore_signal(
            barrier, inc=1, device_id=partner, device_id_type=pl.DeviceIdType.MESH
        )

    act_in = move(act_hbm, act)
    kw_in = move(kw_hbm, kw)
    up_in = move(up_hbm, up)
    pinv_in = move(pinv_hbm, pinv)
    oinv_in = move(oinv_hbm, oinv)

    r = lax.broadcasted_iota(jnp.int32, (128, 128), 0)
    c = lax.broadcasted_iota(jnp.int32, (128, 128), 1)

    def picked(first, second):
        chan = (
            (r & 1)
            + 2 * ((r >> 6) & 1)
            + first * ((r >> 4) & 3)
            + second * ((r >> 2) & 3)
            + 64 * ((r >> 1) & 1)
        )
        return jnp.where(c == chan, 1.0, 0.0).astype(BF16)

    orders = (picked(4, 16), picked(16, 4))
    unit = jnp.where(c == r, 1.0, 0.0).astype(BF16)

    def turned(order, plane):
        return lax.dot_general(order, plane, NT, preferred_element_type=F32).astype(BF16)

    def place_a(plane, at, shifts):
        wide = plane.astype(F32).reshape(16, 16, 128)
        for dx in shifts:
            moved = plane
            if dx:
                moved = pltpu.roll(wide, (-dx) % 16, 1).reshape(256, 128).astype(BF16)
            ext_a[dx + 2, at, 32:288, :] = moved
            ext_a[dx + 2, at, 0:32, :] = moved[224:256]
            ext_a[dx + 2, at, 288:320, :] = moved[0:32]

    def turn_a(plane, at):
        for part in range(2):
            left[part, :, at * 256 : (at + 1) * 256] = turned(orders[part], plane)

    def place_s(plane, at):
        wide = plane.astype(F32).reshape(16, 16, 128)
        for dx in range(-1, 2):
            moved = plane
            if dx:
                moved = pltpu.roll(wide, (-dx) % 16, 1).reshape(256, 128).astype(BF16)
            ext_s[dx + 1, at, 16:272, :] = moved
            ext_s[dx + 1, at, 0:16, :] = moved[240:256]
            ext_s[dx + 1, at, 272:288, :] = moved[0:16]

    def rows_a(first, dy, dx, planes=4):
        return ext_a[
            dx + 2, first : first + planes, (2 + dy) * 16 : (2 + dy) * 16 + 256, :
        ].reshape(planes * 256, 128)

    def ends_a(dz, dy, dx):
        return jnp.concatenate([rows_a(1 + dz, dy, dx, 1), rows_a(4 + dz, dy, dx, 1)], axis=0)

    prod_l[1, 31] = jnp.zeros((128, 128), F32)
    prod_w[3, 1, 2] = jnp.zeros((128, 128), F32)
    inverse[:, 3456:3584] = jnp.zeros((64, 128), F32)
    inverse[48:64, :] = jnp.zeros((16, 3584), F32)

    act_in.wait()
    for z in range(4):
        place_a(act[z], z + 1, (-2, -1, 0, 1, 2))
        turn_a(act[z], z + 1)
    pl.semaphore_wait(barrier, len(partners))
    before = send(act.at[3], halo_a.at[0], following)
    after = send(act.at[0], halo_a.at[1], preceding)

    for k in range(13):
        m = k + 62
        part, slot = (0, 25 + k) if k < 7 else (1, 18 + k)
        prod_l[part, slot] = dot(
            left[part, :, 256:1280], rows_a(1, m // 5 % 5 - 2, m % 5 - 2)
        )

    def taps_sum(z, depths):
        taps = []
        for dz in depths:
            for o in range(9):
                dy, dx = o // 3 - 1, o % 3 - 1
                first = (2 + dy) * 16
                taps.append(ext_a[dx + 2, z + 1 + dz, first : first + 256, :])
        matrix = kw[9 * depths[0] + 9 : 9 * depths[-1] + 18].reshape(len(taps) * 128, 128)
        return dot(jnp.concatenate(taps, axis=1), matrix)

    def forward(z, pre):
        logistic = jax.nn.sigmoid(pre)
        activated[z] = (pre * logistic).astype(BF16)
        sloped = (up[z].astype(F32) * logistic * (1.0 + pre * (1.0 - logistic))).astype(BF16)
        slope[z] = sloped
        slope_t[:, z * 256 : (z + 1) * 256] = turned(unit, sloped)

    theirs = pl.ds(pl.multiple_of(other * 64, 64), 64)
    mine = pl.ds(pl.multiple_of(core * 64, 64), 64)
    firsts = (col, row)
    seconds = (row, col)
    first_axis = (along_x, along_y)
    second_axis = (along_y, along_x)

    def swap_l(first, last):
        return send(
            prod_l.at[:, first:last, theirs, :], got_lc.at[:, first:last], sibling
        )

    def spread_l(first, last):
        copies = []
        for part in range(2):
            out_l1[part, first:last] = (
                prod_l[part, first:last, mine, :] + got_lc[part, first:last]
            ).astype(BF16)
            for t in (2, 1, 3):
                at, to = first_axis[part](t)
                copies.append(
                    send(
                        out_l1.at[part, first:last, sixteen(at), :],
                        got_l1.at[part, t - 1, first:last],
                        to,
                    )
                )
        return copies

    early_c = swap_l(25, 32)
    kw_in.wait()
    up_in.wait()
    forward(1, taps_sum(1, (-1, 0, 1)))
    forward(2, taps_sum(2, (-1, 0, 1)))
    begun[0] = taps_sum(0, (0, 1))
    begun[1] = taps_sum(3, (-1, 0))

    def blocks(d):
        for b in range(7):
            if 7 * d + b < 27:
                yield b, tap_shift(7 * d + b)

    inner_t = slope_t[:, 256:768]
    for d in range(4):
        for b, (dz, dy, dx) in blocks(d):
            prod_w[d, b // 4, b % 4] = dot(inner_t, rows_a(2 + dz, dy, dx, 2))
    inner_own = dot(inner_t, slope[1:3].reshape(512, 128))

    early_c.wait_recv()
    l1 = spread_l(25, 32)

    pinv_in.wait()
    for o in range(27):
        inverse[2 * o : 2 * o + 2, 0:3456] = pinv[o]
    inverse2[core] = inverse[:, pl.ds(pl.multiple_of(quarter * 896, 128), 896)]
    rows_in = send(inverse2.at[core], inverse2.at[core], sibling)

    before.wait_recv()
    place_a(halo_a[0], 0, (-1, 0, 1))
    after.wait_recv()
    place_a(halo_a[1], 5, (-1, 0, 1))
    forward(3, begun[1] + taps_sum(3, (1,)))
    forward(0, begun[0] + taps_sum(0, (-1,)))
    before_s = send(slope.at[3], halo_s.at[0], following)
    after_s = send(slope.at[0], halo_s.at[1], preceding)
    activated_out = move(activated, activated_hbm)

    outer_t = jnp.concatenate([slope_t[:, 0:256], slope_t[:, 768:1024]], axis=1)
    own = inner_own + dot(outer_t, jnp.concatenate([slope[0], slope[3]], axis=0))
    wc = []
    for d in range(4):
        prod_w[d, 1, 3] = own
        ends = jnp.concatenate([ends_a(*shift) for _, shift in blocks(d)], axis=1)
        wide = dot(outer_t, ends)
        for b, _ in blocks(d):
            prod_w[d, b // 4, b % 4] += wide[:, 128 * b : 128 * b + 128]
        wc.append(send(prod_w.at[d, :, :, theirs, :], got_wc.at[d], sibling))

    turn_a(halo_a[0], 0)
    place_a(halo_a[1], 5, (-2, 2))
    left12[0:128, :] = left[0, :, 256:1280]
    left12[128:256, :] = left[1, :, 0:1024]
    pairs = [(dy, dx) for dy in range(-2, 3) for dx in range(-2, 3)]

    def lag_block(first, last):
        for s in range(first, last):
            both = dot(left12[...], rows_a(2, *pairs[s]))
            prod_l[0, s] = both[0:128]
            prod_l[1, s] = both[128:256]
        return swap_l(first, last)

    w1 = []

    def spread_w(first, last):
        for copy in wc[first:last]:
            copy.wait_recv()
        out_w1[first:last] = (prod_w[first:last, :, :, mine, :] + got_wc[first:last]).astype(BF16)
        for t in PLANE:
            at_y, at_x, to = in_plane(t)
            w1.append(
                send(
                    out_w1.at[first:last, :, at_y, sixteen(at_x), :],
                    got_w1.at[t - 1, first:last],
                    to,
                )
            )

    spread_w(0, 2)
    lc = [lag_block(0, 6)]
    spread_w(2, 4)
    lc.append(lag_block(6, 13))
    lc.append(lag_block(13, 25))
    spread_from = len(sent)
    lc[0].wait_recv()
    lc[1].wait_recv()
    l1 += spread_l(0, 13)
    lc[2].wait_recv()
    l1 += spread_l(13, 25)

    for z in range(4):
        place_s(slope[z], z + 1)
    before_s.wait_recv()
    after_s.wait_recv()
    place_s(halo_s[0], 0)
    place_s(halo_s[1], 5)

    kernel_cols = jnp.concatenate([kw[o] for o in range(27)], axis=1)

    def back(z):
        taps = []
        for o in range(27):
            dz, dy, dx = tap_shift(o)
            taps.append(ext_s[1 - dx, z + 1 - dz, (1 - dy) * 16 : (1 - dy) * 16 + 256, :])
        grad = lax.dot_general(
            jnp.concatenate(taps, axis=1), kernel_cols, NT, preferred_element_type=F32
        )
        input_grad[z] = grad.astype(BF16)

    back(0)

    rows_in.wait_recv()
    both_rows = inverse2[...].reshape(128, 896)
    rows_high = both_rows.astype(BF16)
    parts2[0:128, :] = rows_high
    parts2[128:256, :] = (both_rows - rows_high.astype(F32)).astype(BF16)
    settle(spread_from)
    tall = sixteen(core * 4 + col)
    for n in range(2):
        for copy in w1[15 * n : 15 * n + 15]:
            copy.wait_recv()
        two = slice(2 * n, 2 * n + 2)
        total_w = prod_w[two, :, row, tall, :] + got_wc[two, :, row, sixteen(col), :]
        for t in range(15):
            total_w = total_w + got_w1[t, two].astype(F32)
        out_w3[two] = total_w
    got_w3[depth] = out_w3[quarter]
    z_from = len(sent)
    w3 = []
    for t in RING:
        at, to = along_z(t)
        w3.append(send(out_w3.at[lax.rem(at, 4)], got_w3.at[depth], to))

    for copy in l1:
        copy.wait_recv()
    l2 = []
    for part in range(2):
        kept = sixteen(firsts[part])
        high = sixteen(core * 4 + firsts[part])
        total = prod_l[part, :, high, :] + got_lc[part, :, kept, :]
        for t in range(3):
            total = total + got_l1[part, t].astype(F32)
        sum_l1[part] = total.reshape(512, 128)
        for b in range(4):
            for n in range(4):
                groups = [
                    sum_l1[part, pl.ds(4 * b + n + 128 * g, 8, stride=16), :] for g in range(4)
                ]
                out_l2[part, b, n] = jnp.concatenate(groups, axis=0).astype(BF16)
        for t in (2, 1, 3):
            at, to = second_axis[part](t)
            l2.append(send(out_l2.at[part, at], got_l2.at[part, t - 1], to))

    back(1)
    back(2)

    settle(z_from)
    for copy in w3:
        copy.wait_recv()
    reduced = got_w3[0]
    for z in range(1, 8):
        reduced = reduced + got_w3[z]
    weights[:, row, tall, :] = reduced
    gather_from = len(sent)
    g1 = []
    for t in PLANE:
        piece = weights.at[:, row, tall, :]
        g1.append(send(piece, piece, in_plane(t)[2]))

    for copy in l2:
        copy.wait_recv()
    group = c[0:32] // 32
    totals = []
    for part in range(2):
        total = out_l2[part, seconds[part]].astype(F32)
        for t in range(3):
            total = total + got_l2[part, t].astype(F32)
        totals.append(total)
    for h in range(2):
        groups = [totals[part][2 * h + i] for part in range(2) for i in range(2)]
        for q in range(4):
            packed = jnp.zeros((32, 128), F32)
            for j in range(4):
                shift = (32 * (j - q)) % 128
                piece = pltpu.roll(groups[j], shift, 1) if shift else groups[j]
                packed = jnp.where(group == j, piece, packed)
            out_l3[4 * h + q] = packed
    l3 = []
    for t in RING:
        at, to = along_z(t)
        l3.append(send(out_l3.at[at], got_l3.at[t - 1], to))

    back(3)
    input_grad_out = move(input_grad, input_grad_hbm)

    settle(gather_from)
    for copy in g1:
        copy.wait_recv()
    own_in = send(weights.at[1, 3, mine, :], weights.at[1, 3, mine, :], sibling)
    gathered = jnp.concatenate([weights[b // 4, b % 4, mine, :] for b in range(7)], axis=1)
    twice = jnp.concatenate([gathered, gathered], axis=0)
    twice_high = twice.astype(BF16)
    twice_low = (twice - twice_high.astype(F32)).astype(BF16)
    by_high = lax.dot_general(parts2[...], twice_high, NT, preferred_element_type=F32)
    by_low = lax.dot_general(parts2[0:128, :], twice_low, NT, preferred_element_type=F32)
    all_p = by_high[0:128] + (by_high[128:256] + by_low)
    left_half = c[0:32] < 64
    for which in range(2):
        base = 64 * which
        part_p[which] = jnp.where(
            left_half, all_p[base : base + 32], all_p[base + 32 : base + 64]
        )
    got_p[quarter, core] = part_p[core]
    last_from = len(sent)
    pp = [send(part_p.at[other], got_p.at[quarter, core], sibling)]
    for t in (3, 1, 2):
        for which in (core, other):
            pp.append(send(part_p.at[which], got_p.at[quarter, core], along_dp(t, which)))
    own_in.wait_recv()
    output_factor[...] = weights[1, 3] * (1.0 / TOTAL)

    for copy in l3:
        copy.wait_recv()
    final = out_l3[depth]
    for t in range(7):
        final = final + got_l3[t]
    final = final * (1.0 / TOTAL)
    flipped = jnp.concatenate([final, jnp.zeros((96, 128), F32)], axis=0).T
    lane = c[0:32]
    for i in range(2):
        one = flipped[32 * i : 32 * i + 32]
        two = flipped[64 + 32 * i : 96 + 32 * i]
        piece = jnp.where(lane < 7, pltpu.roll(one, 103, 1), pltpu.roll(two, 110, 1))
        piece = jnp.where(lane < 13, piece, pltpu.roll(one, 13, 1))
        piece = jnp.where(lane < 38, piece, pltpu.roll(two, 38, 1))
        patch_factor[i] = piece[:, 0:63]

    oinv_in.wait()
    settle(last_from)
    for copy in pp:
        copy.wait_recv()
    zero, one = (got_p[0, n] + got_p[1, n] + got_p[2, n] + got_p[3, n] for n in range(2))
    product = jnp.concatenate(
        [
            jnp.where(left_half, zero, pltpu.roll(one, 64, 1)),
            jnp.where(left_half, pltpu.roll(zero, 64, 1), one),
        ],
        axis=0,
    )
    product = jnp.dot(
        product, oinv[...], preferred_element_type=F32, precision=HIGHEST
    ) * (1.0 / TOTAL)
    for o in range(27):
        precond[o] = product[2 * o : 2 * o + 2]

    activated_out.wait()
    input_grad_out.wait()
    settle(len(sent))


def hand_on(*refs):
    sources, results, stops, sems = refs[:5], refs[5:10], refs[10:15], refs[15]
    arrivals = []
    for n in range(5):
        copy = pltpu.make_async_copy(sources[n], stops[n], sems.at[n])
        copy.start()
        arrivals.append(copy)
    departures = []
    for n in range(5):
        arrivals[n].wait()
        copy = pltpu.make_async_copy(stops[n], results[n], sems.at[5 + n])
        copy.start()
        departures.append(copy)
    for copy in departures:
        copy.wait()


def per_device(activations, upstream, kernel_weight, patch_inverse, output_inverse):
    vmem = pl.BlockSpec(memory_space=pltpu.VMEM)
    hbm = pl.BlockSpec(memory_space=pl.ANY)
    scratch = [
        ((4, 256, 128), BF16),
        ((4, 256, 128), BF16),
        ((27, 128, 128), BF16),
        ((27, 2, 3456), F32),
        ((128, 128), F32),
        ((4, 256, 128), BF16),
        ((4, 256, 128), BF16),
        ((2, 256, 128), BF16),
        ((2, 256, 128), BF16),
        ((4, 256, 128), BF16),
        ((5, 6, 320, 128), BF16),
        ((3, 6, 288, 128), BF16),
        ((2, 128, 1536), BF16),
        ((256, 1024), BF16),
        ((128, 1024), BF16),
        ((2, 256, 128), F32),
        ((2, 32, 128, 128), F32),
        ((2, 32, 64, 128), F32),
        ((2, 32, 64, 128), BF16),
        ((2, 3, 32, 16, 128), BF16),
        ((2, 512, 128), F32),
        ((2, 4, 4, 32, 128), BF16),
        ((2, 3, 4, 32, 128), BF16),
        ((8, 32, 128), F32),
        ((7, 32, 128), F32),
        ((4, 2, 4, 128, 128), F32),
        ((4, 2, 4, 64, 128), F32),
        ((4, 2, 4, 64, 128), BF16),
        ((15, 4, 2, 16, 128), BF16),
        ((4, 2, 16, 128), F32),
        ((8, 2, 16, 128), F32),
        ((2, 4, 128, 128), F32),
        ((64, 3584), F32),
        ((2, 64, 896), F32),
        ((256, 896), BF16),
        ((2, 32, 128), F32),
        ((4, 2, 32, 128), F32),
    ]
    shapes = (
        jax.ShapeDtypeStruct((4, 256, 128), BF16),
        jax.ShapeDtypeStruct((4, 256, 128), BF16),
        jax.ShapeDtypeStruct((2, 32, 63), F32),
        jax.ShapeDtypeStruct((128, 128), F32),
        jax.ShapeDtypeStruct((27, 2, 128), F32),
    )
    outs = pl.pallas_call(
        step_kernel,
        out_shape=shapes,
        in_specs=[hbm] * 5,
        out_specs=[hbm, hbm, vmem, vmem, vmem],
        scratch_shapes=[pltpu.VMEM(shape, dtype) for shape, dtype in scratch]
        + [
            pltpu.SemaphoreType.DMA((8,)),
            pltpu.SemaphoreType.DMA((128,)),
            pltpu.SemaphoreType.DMA((128,)),
        ],
        compiler_params=pltpu.CompilerParams(
            collective_id=0, has_side_effects=True, vmem_limit_bytes=60 * 1024 * 1024
        ),
        name="step_kernel",
    )(
        activations.reshape(4, 256, 128),
        upstream.reshape(4, 256, 128),
        kernel_weight,
        patch_inverse,
        output_inverse,
    )
    outs = pl.pallas_call(
        hand_on,
        out_shape=shapes,
        in_specs=[hbm] * 5,
        out_specs=[hbm] * 5,
        scratch_shapes=[pltpu.VMEM(shape.shape, shape.dtype) for shape in shapes]
        + [pltpu.SemaphoreType.DMA((10,))],
        compiler_params=pltpu.CompilerParams(vmem_limit_bytes=60 * 1024 * 1024),
        name="hand_on",
    )(*outs)
    activated, input_grad, patch_factor, output_factor, precond = outs
    return (
        activated.reshape(activations.shape),
        input_grad.reshape(activations.shape),
        jnp.transpose(patch_factor, (0, 2, 1)),
        output_factor,
        precond,
    )


def solution(mesh):
    return jax.shard_map(
        per_device,
        mesh=mesh,
        in_specs=(
            P("dp", "space", None, None, None),
            P("dp", "space", None, None, None),
            P(),
            P(None, "space", None),
            P(),
        ),
        out_specs=(
            P("dp", "space", None, None, None),
            P("dp", "space", None, None, None),
            P("space", None, "dp"),
            P(),
            P(None, "space", None),
        ),
        check_vma=False,
    )
```
